128 devices in a mesh: seq: 8 (over x, core), fsdp: 16 (over z, y).
Axes of the slice: x: 4, y: 4, z: 4, core: 2. Of those that a mesh axis runs over, the one named last changes fastest.
Arguments:
- bytes_in: bfloat16 [8, 4096, 1280], P('seq', 'fsdp'), may hold values from -12 to 12, as said below
- doc_lengths: int32 [32], replicated, may hold values from 1 to 2048, 32768 in all
- patch_offsets: int32 [8, 1024], P('seq', 'fsdp'), may hold values from 0 to 256, as said below
- patch_counts: int32 [8, 16], P('seq', 'fsdp'), may hold values from 32 to 64, as said below
- w_query: bfloat16 [1280, 1280], replicated, may hold values from -0.15625 to 0.15625
- w_key: bfloat16 [1280, 1280], replicated, may hold values from -0.15625 to 0.15625
- w_value: bfloat16 [1280, 1280], replicated, may hold values from -0.15625 to 0.15625
- w_proj: bfloat16 [1280, 4096], replicated, may hold values from -0.15625 to 0.15625
- norm_gain: float32 [4096], replicated, may hold values from 0.1 to 1.9
- gate_w: bfloat16 [4096, 7168], P('fsdp', 'seq'), may hold values from -0.09375 to 0.09375
- up_w: bfloat16 [4096, 7168], P('fsdp', 'seq'), may hold values from -0.09375 to 0.09375
- d_hidden: bfloat16 [8, 1024, 7168], P(None, 'fsdp', 'seq'), may hold values from -6 to 6
Outputs:
- hidden: bfloat16 [8, 1024, 7168], P(None, 'fsdp', 'seq')
- grad_gate: float32 [4096, 7168], P('fsdp', 'seq')
- grad_up: float32 [4096, 7168], P('fsdp', 'seq')
- d_patches: float32 [8, 1024, 4096], P('seq', 'fsdp')
The draws below stay inside these ranges and needn't reach their ends.
Inputs may be any that keep to these rules, and one draw needn't show every extreme that they name: `bytes_in`: byte states of order one. `patch_offsets`: in each device block of 64 slots, slot 0 holds 0, the first c slots hold strictly rising offsets, c being the block's entry of patch_counts, and the other slots hold 256. `patch_counts`: patches of one device block; 64 is reached by some block in every draw.
All inputs are finite; a program needn't handle non-finite values.
Results may differ from the reference program's by a relative error of at most 0.022.
Values may be sent and summed in bfloat16 or wider, within the bound.
A program may use at most 192 MiB of HBM per device.

```python
import math
import jax
import jax.numpy as jnp
import numpy as np
from jax import lax

DL = 1280
HEAD = 128
D = 4096
FF = 7168
WINDOW = 512
BYTES_DEV = 256
PATCH_DEV = 64
PATCH_ROW = 1024
BYTES = 32768
DOCS = 32
N_SEQ = 8
N_FSDP = 16


def draw_bytes_in(key, part):
    full_shape = (N_SEQ, N_FSDP * BYTES_DEV, DL)
    noise_key = jax.random.fold_in(jax.random.fold_in(key, 11), 0)
    normal_part = jax.random.normal(noise_key, full_shape, jnp.float32)
    return jnp.clip(normal_part, -6.0, 6.0).astype(jnp.bfloat16)


def patch_layout(key):
    shards = N_SEQ * N_FSDP
    count_key, busy_key, score_key = jax.random.split(jax.random.fold_in(key, 7), 3)
    counts = jax.random.randint(count_key, (shards,), PATCH_DEV // 2, PATCH_DEV + 1)
    busiest = jax.random.randint(busy_key, (), 0, shards)
    counts = jnp.where(jnp.arange(shards) == busiest, PATCH_DEV, counts).astype(jnp.int32)
    scores = jax.random.randint(score_key, (shards, BYTES_DEV - 1), 0, 1 << 16) * BYTES_DEV + jnp.arange(BYTES_DEV - 1)[None, :]
    order_rank = jnp.argsort(jnp.argsort(scores, axis=1), axis=1)
    chosen = order_rank < (counts - 1)[:, None]
    starts_at = jnp.concatenate([jnp.ones((shards, 1), bool), chosen], axis=1)
    slot_index = jnp.cumsum(starts_at.astype(jnp.int32), axis=1) - 1
    target = jnp.where(starts_at, slot_index, PATCH_DEV)
    positions = jnp.broadcast_to(jnp.arange(BYTES_DEV, dtype=jnp.int32)[None, :], (shards, BYTES_DEV))
    shard_rows = jnp.broadcast_to(jnp.arange(shards)[:, None], (shards, BYTES_DEV))
    offsets = jnp.full((shards, PATCH_DEV), BYTES_DEV, jnp.int32).at[shard_rows, target].set(positions, mode='drop')
    return (offsets.reshape(N_SEQ, N_FSDP * PATCH_DEV), counts.reshape(N_SEQ, N_FSDP))


def draw_patch_offsets(key, part):
    return patch_layout(key)[0]


def draw_patch_counts(key, part):
    return patch_layout(key)[1]


def block_levels(key, extent, cuts, least, largest):
    factor_of, own = 1.0, jax.random.fold_in(key, 6)
    for position, parts in cuts:
        steps = jnp.exp(jax.random.uniform(jax.random.fold_in(own, position), (parts,), jnp.float32, least / len(cuts), largest / len(cuts)))
        factor_of = factor_of * jnp.repeat(steps, extent[position] // parts).reshape([-1 if axis == position else 1 for axis in range(len(extent))])
    return factor_of


def length_profile(amount, total, bound, slope):
    portions = [(1 << 20) // math.isqrt(rank ** slope) + 1 for rank in range(2, amount + 1)]
    surplus, given = total - bound - (amount - 1), [1] * (amount - 1)
    while surplus > 0:
        free = [i for i in range(amount - 1) if given[i] < bound]
        mass, budget = sum([portions[i] for i in free]), surplus
        for i in free:
            addition = min(bound - given[i], max(1, budget * portions[i] // mass), surplus)
            given[i] = given[i] + addition
            surplus = surplus - addition
    return np.array([bound] + given)


def uneven(own_key, amount, total, limit, slope):
    if amount == 2:
        one = jax.random.randint(own_key, (), max(1, total - limit), min(limit, total - 1) + 1)
        return jnp.stack([one, total - one])
    tallies = jnp.asarray(length_profile(amount, total, limit, slope), jnp.int32)
    couples = (amount - 1) // 2
    donor, receiver = tallies[1:1 + 2 * couples:2], tallies[2:2 + 2 * couples:2]
    margin = jnp.minimum(donor - 1, limit - receiver)
    passed = jax.random.randint(jax.random.fold_in(own_key, 1), (couples,), 0, 1 << 20) % (margin + 1)
    tallies = tallies.at[1:1 + 2 * couples:2].set(donor - passed).at[2:2 + 2 * couples:2].set(receiver + passed)
    return tallies[jax.random.permutation(jax.random.fold_in(own_key, 2), amount)]


def noise(own_key, shape, scale, limit, pieces=(), kind=jnp.bfloat16):
    entries = scale * jax.random.normal(own_key, shape, jnp.float32)
    if pieces:
        entries = entries * block_levels(own_key, shape, pieces, -0.22, 0.18)
    return jnp.clip(entries, -limit, limit).astype(kind)


def setup_inputs(seed: int = 0) -> dict:
    streams_of = jax.random.split(jax.random.key(seed), 13)
    bytes_in = draw_bytes_in(jax.random.fold_in(streams_of[12], 71), 0)
    doc_lengths = uneven(streams_of[1], DOCS, BYTES, 4 * WINDOW, 2).astype(jnp.int32)
    patch_offsets = draw_patch_offsets(jax.random.fold_in(streams_of[12], 71), 0)
    patch_counts = draw_patch_counts(jax.random.fold_in(streams_of[12], 71), 0)
    w_query = noise(streams_of[4], (DL, DL), DL ** -0.5, 0.15625)
    w_key = noise(streams_of[5], (DL, DL), DL ** -0.5, 0.15625)
    w_value = noise(streams_of[6], (DL, DL), DL ** -0.5, 0.15625)
    w_proj = noise(streams_of[7], (DL, D), DL ** -0.5, 0.15625)
    norm_gain = jnp.clip(1.0 + 0.18 * jax.random.normal(streams_of[8], (D,), jnp.float32), 0.1, 1.9)
    gate_w = noise(streams_of[9], (D, FF), D ** -0.5, 0.09375, ((0, 16), (1, 8)))
    up_w = noise(streams_of[10], (D, FF), D ** -0.5, 0.09375, ((0, 16), (1, 8)))
    d_hidden = noise(streams_of[11], (N_SEQ, PATCH_ROW, FF), 1.0, 6.0, ((1, 16), (2, 8)))
    return {"bytes_in": bytes_in, "doc_lengths": doc_lengths, "patch_offsets": patch_offsets, "patch_counts": patch_counts, "w_query": w_query, "w_key": w_key, "w_value": w_value, "w_proj": w_proj, "norm_gain": norm_gain, "gate_w": gate_w, "up_w": up_w, "d_hidden": d_hidden}


epsilon = 1e-05
masked_score = -1e+30

def doc_index(doc_lengths, positions):
    starts = jnp.cumsum(doc_lengths) - doc_lengths
    inside = (starts[None, :] <= positions[:, None]).astype(jnp.int32)
    return (lax.optimization_barrier(jnp.sum(inside, axis=1)) - 1).astype(jnp.int32)

def window_attention(queries, key_rows, values, query_pos, key_pos, query_doc, key_doc):
    row_count = queries.shape[0]
    head_count = queries.shape[1] // HEAD
    query_heads = queries.reshape(row_count, head_count, HEAD).astype(jnp.float32)
    key_heads = key_rows.reshape(-1, head_count, HEAD).astype(jnp.float32)
    value_heads = values.reshape(-1, head_count, HEAD).astype(jnp.float32)
    scores = jnp.einsum('qhd,khd->hqk', query_heads, key_heads) / math.sqrt(HEAD)
    allowed = (key_pos[None, :] <= query_pos[:, None]) & (query_pos[:, None] - key_pos[None, :] < WINDOW)
    allowed = allowed & (key_pos[None, :] >= 0) & (key_doc[None, :] == query_doc[:, None])
    scores = jnp.where(allowed[None], scores, masked_score)
    row_max = lax.optimization_barrier(jnp.max(scores, axis=-1, keepdims=True))
    weights = jnp.exp(scores - row_max)
    weights = (weights / lax.optimization_barrier(jnp.sum(weights, axis=-1, keepdims=True))).astype(jnp.bfloat16)
    mixed = jnp.einsum('hqk,khd->qhd', weights.astype(jnp.float32), value_heads)
    return mixed.reshape(row_count, head_count * HEAD)

def pool_patches(states, offsets, count):
    length = states.shape[0]
    slot_count = offsets.shape[0]
    head_count = states.shape[1] // HEAD
    slot_ids = jnp.arange(slot_count, dtype=jnp.int32)
    present = slot_ids < count
    following = jnp.concatenate([offsets[1:], jnp.full((1,), length, jnp.int32)])
    patch_ends = jnp.where(slot_ids == count - 1, length, following)
    byte_ids = jnp.arange(length, dtype=jnp.int32)
    member = present[:, None] & (offsets[:, None] <= byte_ids[None, :]) & (byte_ids[None, :] < patch_ends[:, None])
    patch_sizes = lax.optimization_barrier(jnp.sum(member.astype(jnp.float32), axis=1, keepdims=True))
    summed = jnp.dot(member.astype(jnp.bfloat16), states, preferred_element_type=jnp.float32)
    pooled = (summed / jnp.maximum(patch_sizes, 1.0)).astype(jnp.bfloat16)
    pooled_heads = pooled.reshape(slot_count, head_count, HEAD).astype(jnp.float32)
    state_heads = states.reshape(length, head_count, HEAD).astype(jnp.float32)
    scores = jnp.einsum('jhd,bhd->hjb', pooled_heads, state_heads) / math.sqrt(HEAD)
    scores = jnp.where(member[None], scores, masked_score)
    row_max = lax.optimization_barrier(jnp.max(scores, axis=-1, keepdims=True))
    weights = jnp.exp(scores - row_max)
    weights = (weights / lax.optimization_barrier(jnp.sum(weights, axis=-1, keepdims=True))).astype(jnp.bfloat16)
    context = jnp.einsum('hjb,bhd->jhd', weights.astype(jnp.float32), state_heads)
    context = context.reshape(slot_count, head_count * HEAD)
    return jnp.where(present[:, None], context, 0.0).astype(jnp.bfloat16)

def reference(bytes_in, doc_lengths, patch_offsets, patch_counts, w_query, w_key, w_value, w_proj, norm_gain, gate_w, up_w, d_hidden):
    shards = N_SEQ * N_FSDP
    total = shards * BYTES_DEV
    states = bytes_in.reshape(total, DL)
    queries = jnp.dot(states, w_query, preferred_element_type=jnp.float32).astype(jnp.bfloat16)
    key_rows = jnp.dot(states, w_key, preferred_element_type=jnp.float32).astype(jnp.bfloat16)
    values = jnp.dot(states, w_value, preferred_element_type=jnp.float32).astype(jnp.bfloat16)
    reach = (WINDOW - 2 + BYTES_DEV) // BYTES_DEV * BYTES_DEV
    positions = jnp.arange(total, dtype=jnp.int32)
    docs = doc_index(doc_lengths, positions)
    key_padded = jnp.concatenate([jnp.zeros((reach, DL), key_rows.dtype), key_rows])
    value_padded = jnp.concatenate([jnp.zeros((reach, DL), values.dtype), values])
    pos_padded = jnp.arange(total + reach, dtype=jnp.int32) - reach
    doc_padded = jnp.concatenate([jnp.full((reach,), -1, jnp.int32), docs])

    def attend(shard):
        row_start = (shard * BYTES_DEV).astype(jnp.int32)
        return window_attention(lax.dynamic_slice_in_dim(queries, row_start, BYTES_DEV), lax.dynamic_slice_in_dim(key_padded, row_start, reach + BYTES_DEV), lax.dynamic_slice_in_dim(value_padded, row_start, reach + BYTES_DEV), lax.dynamic_slice_in_dim(positions, row_start, BYTES_DEV), lax.dynamic_slice_in_dim(pos_padded, row_start, reach + BYTES_DEV), lax.dynamic_slice_in_dim(docs, row_start, BYTES_DEV), lax.dynamic_slice_in_dim(doc_padded, row_start, reach + BYTES_DEV))
    mixed = lax.map(attend, jnp.arange(shards, dtype=jnp.int32)).reshape(total, DL)
    hidden_bytes = (states.astype(jnp.float32) + mixed).astype(jnp.bfloat16)
    contexts = lax.map(lambda item: pool_patches(item[0], item[1], item[2]), (hidden_bytes.reshape(shards, BYTES_DEV, DL), patch_offsets.reshape(shards, PATCH_DEV), patch_counts.reshape(shards)))
    features = jnp.dot(contexts.reshape(shards * PATCH_DEV, DL), w_proj, preferred_element_type=jnp.float32).astype(jnp.bfloat16)
    patch_float = features.astype(jnp.float32)
    inverse = lax.rsqrt(lax.optimization_barrier(jnp.mean(patch_float * patch_float, axis=1, keepdims=True)) + epsilon)
    normed = (patch_float * inverse * norm_gain).astype(jnp.bfloat16)
    gate_pre = jnp.dot(normed, gate_w, preferred_element_type=jnp.float32)
    up_pre = jnp.dot(normed, up_w, preferred_element_type=jnp.float32)
    sigmoid_gate = jax.nn.sigmoid(gate_pre)
    hidden = (gate_pre * sigmoid_gate * up_pre).astype(jnp.bfloat16)
    cotangent = d_hidden.reshape(shards * PATCH_DEV, FF).astype(jnp.float32)
    gate_grad = (cotangent * up_pre * sigmoid_gate * (1.0 + gate_pre * (1.0 - sigmoid_gate))).astype(jnp.bfloat16)
    up_grad = (cotangent * gate_pre * sigmoid_gate).astype(jnp.bfloat16)
    both_grads = jnp.concatenate([gate_grad, up_grad], axis=1).reshape(N_SEQ, N_FSDP, PATCH_DEV, 2 * FF)
    normed_blocks = normed.reshape(N_SEQ, N_FSDP, PATCH_DEV, D)

    def add_partial(total_grad, block_index):
        rows_normed = lax.dynamic_index_in_dim(normed_blocks, block_index, 1, keepdims=False).reshape(N_SEQ * PATCH_DEV, D)
        rows_grad = lax.dynamic_index_in_dim(both_grads, block_index, 1, keepdims=False).reshape(N_SEQ * PATCH_DEV, 2 * FF)
        partial_value = lax.dot_general(rows_normed, rows_grad, (((0,), (0,)), ((), ())), preferred_element_type=jnp.float32)
        partial_value = lax.optimization_barrier(partial_value.astype(jnp.bfloat16)).astype(jnp.float32)
        return (total_grad + partial_value, None)
    weight_total, ignored = lax.scan(add_partial, jnp.zeros((D, 2 * FF), jnp.float32), jnp.arange(N_FSDP, dtype=jnp.int32))
    slice_width = FF // N_SEQ

    def add_input(total_grad, block_index):
        column_start = (block_index * slice_width).astype(jnp.int32)
        gate_part = lax.dynamic_slice_in_dim(gate_grad, column_start, slice_width, 1)
        up_part = lax.dynamic_slice_in_dim(up_grad, column_start, slice_width, 1)
        gate_cols = lax.dynamic_slice_in_dim(gate_w, column_start, slice_width, 1)
        up_cols = lax.dynamic_slice_in_dim(up_w, column_start, slice_width, 1)
        partial_value = lax.dot_general(gate_part, gate_cols, (((1,), (1,)), ((), ())), preferred_element_type=jnp.float32)
        partial_value = partial_value + lax.dot_general(up_part, up_cols, (((1,), (1,)), ((), ())), preferred_element_type=jnp.float32)
        partial_value = lax.optimization_barrier(partial_value.astype(jnp.bfloat16)).astype(jnp.float32)
        return (total_grad + partial_value, None)
    normed_grad, unused = lax.scan(add_input, jnp.zeros((shards * PATCH_DEV, D), jnp.float32), jnp.arange(N_SEQ, dtype=jnp.int32))
    scaled = norm_gain * normed_grad
    patch_grad = inverse * scaled - patch_float * (inverse * inverse * inverse) * lax.optimization_barrier(jnp.mean(scaled * patch_float, axis=1, keepdims=True))
    return (hidden.reshape(N_SEQ, N_FSDP * PATCH_DEV, FF), weight_total[:, :FF], weight_total[:, FF:], patch_grad.reshape(N_SEQ, N_FSDP * PATCH_DEV, D))
```

```python
import math

import jax
import jax.numpy as jnp
from jax import lax
from jax.experimental import pallas as pl
from jax.experimental.pallas import tpu as pltpu
from jax.sharding import PartitionSpec as P

HEAD = 128
WINDOW = 512


epsilon = 1e-05
masked_score = -1e30


def shifted(shard, axis, by):
    devices = lax.axis_size(axis)
    pairs = [(i, i + by) for i in range(devices) if 0 <= i + by < devices]
    return lax.ppermute(shard, axis, pairs)


def laid_out(pieces, dim):
    lengths = list(pieces.shape[1:])
    lengths[dim] *= pieces.shape[0]
    return jnp.moveaxis(pieces, 0, dim).reshape(lengths)


def copy_for_each(shard, axis):
    copies = jnp.broadcast_to(shard, (lax.axis_size(axis), *shard.shape))
    return lax.all_to_all(copies, axis, split_axis=0, concat_axis=0, tiled=True)


def gather_directly(shard, axis, dim):
    return laid_out(copy_for_each(shard, axis), dim)


def in_one_piece(arrays, axis, dim, along):
    both = jnp.concatenate(arrays, axis=along)
    filled, at, finished = (lax.all_gather(both, axis, axis=dim, tiled=True), 0, [])
    for a in arrays:
        finished.append(lax.slice_in_dim(filled, at, at + a.shape[along], axis=along))
        at += a.shape[along]
    return tuple(finished)


def in_blocks(shard, dim, devices):
    lengths = shard.shape
    pieces = shard.reshape(*lengths[:dim], devices, lengths[dim] // devices, *lengths[dim + 1 :])
    return jnp.moveaxis(pieces, dim, 0)


def summed_on_arrival(shard, axis, dim):
    pieces = in_blocks(shard, dim, lax.axis_size(axis))
    arrived = lax.all_to_all(pieces, axis, split_axis=0, concat_axis=0, tiled=True)
    return arrived.astype(jnp.float32).sum(axis=0)


MESH = pl.DeviceIdType.MESH
SIDE = 4


def wrapped(value):
    return lax.rem(value + 2 * SIDE, SIDE)


def grad_rings(
    normed_ref, grads_ref, out_ref, first, arrived, second, crossed, put, got, put2, got2
):
    seq = lax.axis_index("seq")
    spot = lax.axis_index("fsdp")
    z, y = lax.div(spot, SIDE), lax.rem(spot, SIDE)
    rows = first.shape[2]
    units = out_ref.shape[2]

    barrier = pltpu.get_barrier_semaphore()
    around = (
        wrapped(z + 1) * SIDE + y,
        wrapped(z - 1) * SIDE + y,
        z * SIDE + wrapped(y + 1),
        z * SIDE + wrapped(y - 1),
    )
    for neighbour in around:
        pl.semaphore_signal(barrier, inc=1, device_id=(seq, neighbour), device_id_type=MESH)
    pl.semaphore_wait(barrier, len(around))

    def place(stream):
        kind, half = stream // 2, stream % 2
        step = 1 - 2 * half
        along, across = (z, y) if kind == 0 else (y, z)
        if kind == 0:
            onward, sideways = around[half], around[2 + half]
        else:
            onward, sideways = around[2 + half], around[half]
        return kind, half, step, along, across, onward, sideways

    def own(stream, t, k):
        kind, half, step, along, across, _, _ = place(stream)
        far = wrapped(along - step * (1 + t))
        near = wrapped(across - step * (1 + k))
        zb, yb = (far, near) if kind == 0 else (near, far)
        at = pl.multiple_of((zb * SIDE + yb) * 2 * rows + half * rows, rows)
        return lax.dot_general(
            normed_ref[:, pl.ds(at, rows)],
            grads_ref[:, kind * units : (kind + 1) * units],
            (((0,), (0,)), ((), ())),
            preferred_element_type=jnp.float32,
        )

    def hop(stream, source, t, k):
        onward = place(stream)[5]
        return pltpu.make_async_remote_copy(
            src_ref=source,
            dst_ref=arrived.at[stream, t, k],
            send_sem=put.at[stream, t, k],
            recv_sem=got.at[stream, t, k],
            device_id=(seq, onward),
            device_id_type=MESH,
        )

    def hop2(stream, source, k):
        sideways = place(stream)[6]
        return pltpu.make_async_remote_copy(
            src_ref=source,
            dst_ref=crossed.at[stream, k],
            send_sem=put2.at[stream, k],
            recv_sem=got2.at[stream, k],
            device_id=(seq, sideways),
            device_id_type=MESH,
        )

    def opening(k, carry):
        for stream in range(4):
            first[stream, k] = own(stream, 0, k).astype(jnp.bfloat16)
            hop(stream, first.at[stream, k], 0, k).start()
        return carry

    lax.fori_loop(0, SIDE, opening, 0)

    def middle(index, carry):
        t, k = lax.div(index, SIDE) + 1, lax.rem(index, SIDE)
        for stream in range(4):
            value = own(stream, t, k)
            hop(stream, first.at[stream, k], t - 1, k).wait_recv()
            arrived[stream, t - 1, k] = (
                value + arrived[stream, t - 1, k].astype(jnp.float32)
            ).astype(jnp.bfloat16)
            hop(stream, arrived.at[stream, t - 1, k], t, k).start()
        return carry

    lax.fori_loop(0, 2 * SIDE, middle, 0)

    last = SIDE - 1

    def total(stream, k):
        value = own(stream, last, k)
        hop(stream, first.at[stream, k], last - 1, k).wait_recv()
        return value + arrived[stream, last - 1, k].astype(jnp.float32)

    for stream in range(4):
        second[stream] = total(stream, 0).astype(jnp.bfloat16)
        hop2(stream, second.at[stream], 0).start()

    def crossing(k, carry):
        for stream in range(4):
            value = total(stream, k)
            hop2(stream, second.at[stream], k - 1).wait_recv()
            crossed[stream, k - 1] = (
                value + crossed[stream, k - 1].astype(jnp.float32)
            ).astype(jnp.bfloat16)
            hop2(stream, crossed.at[stream, k - 1], k).start()
        return carry

    lax.fori_loop(1, last, crossing, 0)

    for stream in range(4):
        kind, half = stream // 2, stream % 2
        value = total(stream, last)
        hop2(stream, second.at[stream], last - 1).wait_recv()
        out_ref[kind, half * rows : (half + 1) * rows, :] = value + crossed[
            stream, last - 1
        ].astype(jnp.float32)

    def sent(index, carry):
        t, k = lax.div(index, SIDE), lax.rem(index, SIDE)
        for stream in range(4):
            hop(stream, first.at[stream, k], t, k).wait_send()
        return carry

    lax.fori_loop(0, last * SIDE, sent, 0)
    for stream in range(4):
        for k in range(last):
            hop2(stream, second.at[stream], k).wait_send()


def weight_grads(normed, grads):
    tokens, width = normed.shape
    units = grads.shape[1] // 2
    rows = width // (SIDE * SIDE)
    half = rows // 2
    block = (half, units)
    return pl.pallas_call(
        grad_rings,
        out_shape=jax.ShapeDtypeStruct((2, rows, units), jnp.float32),
        in_specs=[pl.BlockSpec(memory_space=pltpu.VMEM)] * 2,
        out_specs=pl.BlockSpec(memory_space=pltpu.VMEM),
        scratch_shapes=[
            pltpu.VMEM((4, SIDE, *block), jnp.bfloat16),
            pltpu.VMEM((4, SIDE - 1, SIDE, *block), jnp.bfloat16),
            pltpu.VMEM((4, *block), jnp.bfloat16),
            pltpu.VMEM((4, SIDE - 1, *block), jnp.bfloat16),
            pltpu.SemaphoreType.DMA((4, SIDE - 1, SIDE)),
            pltpu.SemaphoreType.DMA((4, SIDE - 1, SIDE)),
            pltpu.SemaphoreType.DMA((4, SIDE - 1)),
            pltpu.SemaphoreType.DMA((4, SIDE - 1)),
        ],
        compiler_params=pltpu.CompilerParams(
            collective_id=0, has_side_effects=True, vmem_limit_bytes=48 * 1024 * 1024
        ),
        cost_estimate=pl.CostEstimate(
            flops=2 * tokens * width * 2 * units,
            bytes_accessed=200_000_000,
            transcendentals=0,
        ),
        name="grad_rings",
    )(normed, grads)


def doc_index(doc_lengths, positions):
    starts = jnp.cumsum(doc_lengths) - doc_lengths
    inside = (starts[None, :] <= positions[:, None]).astype(jnp.int32)
    return jnp.sum(inside, axis=1) - 1


def window_attention(queries, key_rows, values, query_pos, key_pos, query_doc, key_doc):
    row_count = queries.shape[0]
    head_count = queries.shape[1] // HEAD
    query_heads = queries.reshape(row_count, head_count, HEAD)
    key_heads = key_rows.reshape(-1, head_count, HEAD)
    value_heads = values.reshape(-1, head_count, HEAD)
    scores = jnp.einsum(
        "qhd,khd->hqk", query_heads, key_heads, preferred_element_type=jnp.float32
    ) / math.sqrt(HEAD)
    allowed = (key_pos[None, :] <= query_pos[:, None]) & (
        query_pos[:, None] - key_pos[None, :] < WINDOW
    )
    allowed = allowed & (key_pos[None, :] >= 0) & (key_doc[None, :] == query_doc[:, None])
    scores = jnp.where(allowed[None], scores, masked_score)
    row_max = jnp.max(scores, axis=-1, keepdims=True)
    weights = jnp.exp(scores - row_max)
    weights = (weights / jnp.sum(weights, axis=-1, keepdims=True)).astype(jnp.bfloat16)
    mixed = jnp.einsum("hqk,khd->qhd", weights, value_heads, preferred_element_type=jnp.float32)
    return mixed.reshape(row_count, head_count * HEAD)


def pool_patches(states, offsets, count):
    length = states.shape[0]
    slot_count = offsets.shape[0]
    head_count = states.shape[1] // HEAD
    slot_ids = jnp.arange(slot_count, dtype=jnp.int32)
    present = slot_ids < count
    following = jnp.concatenate([offsets[1:], jnp.full((1,), length, jnp.int32)])
    patch_ends = jnp.where(slot_ids == count - 1, length, following)
    byte_ids = jnp.arange(length, dtype=jnp.int32)
    member = (
        present[:, None]
        & (offsets[:, None] <= byte_ids[None, :])
        & (byte_ids[None, :] < patch_ends[:, None])
    )
    patch_sizes = jnp.sum(member.astype(jnp.float32), axis=1, keepdims=True)
    summed = jnp.dot(member.astype(jnp.bfloat16), states, preferred_element_type=jnp.float32)
    pooled = (summed / jnp.maximum(patch_sizes, 1.0)).astype(jnp.bfloat16)
    pooled_heads = pooled.reshape(slot_count, head_count, HEAD)
    state_heads = states.reshape(length, head_count, HEAD)
    scores = jnp.einsum(
        "jhd,bhd->hjb", pooled_heads, state_heads, preferred_element_type=jnp.float32
    ) / math.sqrt(HEAD)
    scores = jnp.where(member[None], scores, masked_score)
    row_max = jnp.max(scores, axis=-1, keepdims=True)
    weights = jnp.exp(scores - row_max)
    weights = (weights / jnp.sum(weights, axis=-1, keepdims=True)).astype(jnp.bfloat16)
    context = jnp.einsum("hjb,bhd->jhd", weights, state_heads, preferred_element_type=jnp.float32)
    context = context.reshape(slot_count, head_count * HEAD)
    return jnp.where(present[:, None], context, 0.0).astype(jnp.bfloat16)


def shards(
    bytes_in,
    doc_lengths,
    patch_offsets,
    patch_counts,
    w_query,
    w_key,
    w_value,
    w_proj,
    norm_gain,
    gate_w,
    up_w,
    d_hidden,
):
    states = bytes_in[0]
    length = states.shape[0]
    hop_count = (WINDOW - 2 + length) // length
    first_pos = lax.axis_index(("seq", "fsdp")) * length
    queries = jnp.dot(states, w_query, preferred_element_type=jnp.float32).astype(jnp.bfloat16)
    key_rows = jnp.dot(states, w_key, preferred_element_type=jnp.float32).astype(jnp.bfloat16)
    values = jnp.dot(states, w_value, preferred_element_type=jnp.float32).astype(jnp.bfloat16)
    key_parts = [key_rows]
    value_parts = [values]
    for distance in range(1, hop_count + 1):
        earlier = shifted(states, ("seq", "fsdp"), distance)
        earlier_keys = jnp.dot(earlier, w_key, preferred_element_type=jnp.float32).astype(
            jnp.bfloat16
        )
        earlier_values = jnp.dot(earlier, w_value, preferred_element_type=jnp.float32).astype(
            jnp.bfloat16
        )
        key_parts.insert(0, earlier_keys)
        value_parts.insert(0, earlier_values)
    key_all = jnp.concatenate(key_parts, axis=0)
    value_all = jnp.concatenate(value_parts, axis=0)
    query_pos = first_pos + jnp.arange(length, dtype=jnp.int32)
    key_pos = first_pos - hop_count * length + jnp.arange((hop_count + 1) * length, dtype=jnp.int32)
    key_doc = doc_index(doc_lengths, key_pos)
    query_doc = key_doc[hop_count * length :]
    mixed = window_attention(queries, key_all, value_all, query_pos, key_pos, query_doc, key_doc)
    hidden_bytes = (states.astype(jnp.float32) + mixed).astype(jnp.bfloat16)
    context = pool_patches(hidden_bytes, patch_offsets[0], patch_counts[0, 0])
    seq_index = lax.axis_index("seq")
    shard_part = gather_directly(context[None], "seq", 0)
    flat_part = shard_part.reshape(-1, shard_part.shape[-1])
    result = jnp.dot(flat_part, w_proj, preferred_element_type=jnp.float32).astype(jnp.bfloat16)
    features = result.reshape(shard_part.shape[0], shard_part.shape[1], -1)
    seq_count, slot_count, model_width = features.shape
    patch_float = features.reshape(seq_count * slot_count, model_width).astype(jnp.float32)
    inverse = lax.rsqrt(jnp.mean(patch_float * patch_float, axis=1, keepdims=True) + epsilon)
    normed = (patch_float * inverse * norm_gain).astype(jnp.bfloat16)
    gate_full, up_full = in_one_piece((gate_w, up_w), "fsdp", 0, 1)
    gate_pre = jnp.dot(normed, gate_full, preferred_element_type=jnp.float32)
    up_pre = jnp.dot(normed, up_full, preferred_element_type=jnp.float32)
    sigmoid_gate = jax.nn.sigmoid(gate_pre)
    hidden = (gate_pre * sigmoid_gate * up_pre).astype(jnp.bfloat16)
    units = gate_w.shape[1]
    cotangent = d_hidden.reshape(seq_count * slot_count, units).astype(jnp.float32)
    gate_grad = (
        cotangent * up_pre * sigmoid_gate * (1.0 + gate_pre * (1.0 - sigmoid_gate))
    ).astype(jnp.bfloat16)
    up_grad = (cotangent * gate_pre * sigmoid_gate).astype(jnp.bfloat16)
    both_grads = jnp.concatenate([gate_grad, up_grad], axis=1)
    input_partial = lax.dot_general(
        gate_grad, gate_full, (((1,), (1,)), ((), ())), preferred_element_type=jnp.float32
    )
    input_partial = input_partial + lax.dot_general(
        up_grad, up_full, (((1,), (1,)), ((), ())), preferred_element_type=jnp.float32
    )
    normed_grad = lax.psum_scatter(
        input_partial.reshape(seq_count, slot_count, model_width).astype(jnp.bfloat16),
        "seq",
        scatter_dimension=0,
        tiled=True,
    )[0].astype(jnp.float32)
    totals = weight_grads(normed, both_grads)
    grad_gate, grad_up = totals[0], totals[1]
    own_float = lax.dynamic_index_in_dim(
        patch_float.reshape(seq_count, slot_count, model_width), seq_index, 0, keepdims=False
    )
    own_inverse = lax.dynamic_index_in_dim(
        inverse.reshape(seq_count, slot_count, 1), seq_index, 0, keepdims=False
    )
    scaled = norm_gain * normed_grad
    patch_grad = own_inverse * scaled - own_float * (
        own_inverse * own_inverse * own_inverse
    ) * jnp.mean(scaled * own_float, axis=1, keepdims=True)
    return (hidden.reshape(seq_count, slot_count, units), grad_gate, grad_up, patch_grad[None])


def solution(mesh):
    return jax.shard_map(
        shards,
        mesh=mesh,
        in_specs=(
            P("seq", "fsdp", None),
            P(),
            P("seq", "fsdp"),
            P("seq", "fsdp"),
            P(),
            P(),
            P(),
            P(),
            P(),
            P("fsdp", "seq"),
            P("fsdp", "seq"),
            P(None, "fsdp", "seq"),
        ),
        out_specs=(
            P(None, "fsdp", "seq"),
            P("fsdp", "seq"),
            P("fsdp", "seq"),
            P("seq", "fsdp", None),
        ),
        check_vma=False,
    )
```

```python
import math

import jax
import jax.numpy as jnp
from jax import lax
from jax.experimental import pallas as pl
from jax.experimental.pallas import tpu as pltpu
from jax.sharding import PartitionSpec as P

HEAD = 128
WINDOW = 512


epsilon = 1e-05
masked_score = -1e30


def from_earlier(shard, by):
    axes = ("seq", "fsdp")
    devices = lax.axis_size(axes)
    pairs = [(i, i + by) for i in range(devices) if i + by < devices]
    if by == 2:
        via = [i - i % SIDE + (i - 1) % SIDE for i in range(devices)]
        shard = lax.ppermute(shard, axes, [(i, via[i]) for i in range(devices)])
        pairs = [(via[i], j) for i, j in pairs if via[i] != j]
    return lax.ppermute(shard, axes, pairs)


def laid_out(pieces, dim):
    lengths = list(pieces.shape[1:])
    lengths[dim] *= pieces.shape[0]
    return jnp.moveaxis(pieces, 0, dim).reshape(lengths)


def copy_for_each(shard, axis):
    copies = jnp.broadcast_to(shard, (lax.axis_size(axis), *shard.shape))
    return lax.all_to_all(copies, axis, split_axis=0, concat_axis=0, tiled=True)


def gather_directly(shard, axis, dim):
    return laid_out(copy_for_each(shard, axis), dim)


MESH = pl.DeviceIdType.MESH
SIDE = 4


def wrapped(value):
    return lax.rem(value + 2 * SIDE, SIDE)


def grad_rings(
    normed_ref,
    grads_ref,
    weights_hbm,
    out_ref,
    inward_ref,
    first,
    arrived,
    second,
    crossed,
    weights,
    parts,
    paired,
    ringed,
    put,
    got,
    put2,
    got2,
    loaded,
    put3,
    got3,
    put4,
    got4,
):
    seq = lax.axis_index("seq")
    spot = lax.axis_index("fsdp")
    x, core = lax.div(seq, 2), lax.rem(seq, 2)
    z, y = lax.div(spot, SIDE), lax.rem(spot, SIDE)
    rows = first.shape[2]
    units = out_ref.shape[2]
    chunks, _, _, slots, wide = parts.shape

    load = pltpu.make_async_copy(weights_hbm, weights, loaded)
    load.start()

    around = (
        (seq, wrapped(z + 1) * SIDE + y),
        (seq, wrapped(z - 1) * SIDE + y),
        (seq, z * SIDE + wrapped(y + 1)),
        (seq, z * SIDE + wrapped(y - 1)),
        (wrapped(x + 1) * 2 + core, spot),
        (wrapped(x - 1) * 2 + core, spot),
        (x * 2 + 1 - core, spot),
    )
    barrier = pltpu.get_barrier_semaphore()
    for neighbour in around:
        pl.semaphore_signal(barrier, inc=1, device_id=neighbour, device_id_type=MESH)
    pl.semaphore_wait(barrier, len(around))

    def place(stream):
        kind, half = stream // 2, stream % 2
        step = 1 - 2 * half
        along, across = (z, y) if kind == 0 else (y, z)
        if kind == 0:
            onward, sideways = around[half], around[2 + half]
        else:
            onward, sideways = around[2 + half], around[half]
        return kind, half, step, along, across, onward, sideways

    def own(stream, t, k):
        kind, half, step, along, across, _, _ = place(stream)
        far = wrapped(along - step * (1 + t))
        near = wrapped(across - step * (1 + k))
        zb, yb = (far, near) if kind == 0 else (near, far)
        at = pl.multiple_of((zb * SIDE + yb) * 2 * rows + half * rows, rows)
        return lax.dot_general(
            normed_ref[:, pl.ds(at, rows)],
            grads_ref[:, kind * units : (kind + 1) * units],
            (((0,), (0,)), ((), ())),
            preferred_element_type=jnp.float32,
        )

    def hop(stream, source, t, k):
        return pltpu.make_async_remote_copy(
            src_ref=source,
            dst_ref=arrived.at[stream, t, k],
            send_sem=put.at[stream, t, k],
            recv_sem=got.at[stream, t, k],
            device_id=place(stream)[5],
            device_id_type=MESH,
        )

    def hop2(stream, source, k):
        return pltpu.make_async_remote_copy(
            src_ref=source,
            dst_ref=crossed.at[stream, k],
            send_sem=put2.at[stream, k],
            recv_sem=got2.at[stream, k],
            device_id=place(stream)[6],
            device_id_type=MESH,
        )

    def across_cores(n):
        return pltpu.make_async_remote_copy(
            src_ref=parts.at[n, 1 - core],
            dst_ref=paired.at[n],
            send_sem=put3.at[n],
            recv_sem=got3.at[n],
            device_id=around[6],
            device_id_type=MESH,
        )

    def x_hop(side, n, source, t):
        return pltpu.make_async_remote_copy(
            src_ref=source,
            dst_ref=ringed.at[t, n],
            send_sem=put4.at[t, n],
            recv_sem=got4.at[t, n],
            device_id=around[4 + side],
            device_id_type=MESH,
        )

    def opening(k, carry):
        for stream in range(4):
            first[stream, k] = own(stream, 0, k).astype(jnp.bfloat16)
            hop(stream, first.at[stream, k], 0, k).start()
        return carry

    lax.fori_loop(0, SIDE, opening, 0)
    load.wait()

    def input_part(n):
        at = pl.multiple_of(n * wide, wide)
        value = lax.dot_general(
            grads_ref[...],
            weights[pl.ds(at, wide), :],
            (((1,), (1,)), ((), ())),
            preferred_element_type=jnp.float32,
        ).astype(jnp.bfloat16)
        for block in range(2 * SIDE):
            parts[n, block % 2, block // 2] = value[block * slots : (block + 1) * slots]
        across_cores(n).start()

    def middle(t, busy):
        def body(k, carry):
            for stream in range(4):
                value = own(stream, t, k)
                hop(stream, first.at[stream, k], t - 1, k).wait_recv()
                arrived[stream, t - 1, k] = (
                    value + arrived[stream, t - 1, k].astype(jnp.float32)
                ).astype(jnp.bfloat16)
                hop(stream, arrived.at[stream, t - 1, k], t, k).start()
            if busy:
                input_part(2 * k)
                input_part(2 * k + 1)
            return carry

        lax.fori_loop(0, SIDE, body, 0)

    def x_phase(t):
        def body(m, carry):
            for side in range(2):
                n = 2 * m + side
                block = wrapped(x - (1 - 2 * side) * (1 + t))
                if t == 0:
                    across_cores(n).wait_recv()
                    paired[n] = (
                        paired[n].astype(jnp.float32) + parts[n, core].astype(jnp.float32)
                    ).astype(jnp.bfloat16)
                    x_hop(side, n, paired.at[n, block], 0).start()
                else:
                    x_hop(side, n, paired.at[n, block], t - 1).wait_recv()
                    value = ringed[t - 1, n].astype(jnp.float32) + paired[n, block].astype(
                        jnp.float32
                    )
                    if t < SIDE - 1:
                        ringed[t - 1, n] = value.astype(jnp.bfloat16)
                        x_hop(side, n, ringed.at[t - 1, n], t).start()
                    else:
                        inward_ref[n] = value
            return carry

        lax.fori_loop(0, chunks // 2, body, 0)

    last = SIDE - 1

    def total(stream, k):
        value = own(stream, last, k)
        hop(stream, first.at[stream, k], last - 1, k).wait_recv()
        return value + arrived[stream, last - 1, k].astype(jnp.float32)

    middle(1, True)
    x_phase(0)
    middle(2, False)
    x_phase(1)

    for stream in range(4):
        second[stream] = total(stream, 0).astype(jnp.bfloat16)
        hop2(stream, second.at[stream], 0).start()
    x_phase(2)

    def crossing(k, carry):
        for stream in range(4):
            value = total(stream, k)
            hop2(stream, second.at[stream], k - 1).wait_recv()
            crossed[stream, k - 1] = (
                value + crossed[stream, k - 1].astype(jnp.float32)
            ).astype(jnp.bfloat16)
            hop2(stream, crossed.at[stream, k - 1], k).start()
        return carry

    lax.fori_loop(1, last, crossing, 0)
    x_phase(3)

    for stream in range(4):
        kind, half = stream // 2, stream % 2
        value = total(stream, last)
        hop2(stream, second.at[stream], last - 1).wait_recv()
        out_ref[kind, half * rows : (half + 1) * rows, :] = value + crossed[
            stream, last - 1
        ].astype(jnp.float32)

    def sent(index, carry):
        t, k = lax.div(index, SIDE), lax.rem(index, SIDE)
        for stream in range(4):
            hop(stream, first.at[stream, k], t, k).wait_send()
        return carry

    lax.fori_loop(0, last * SIDE, sent, 0)
    for stream in range(4):
        for k in range(last):
            hop2(stream, second.at[stream], k).wait_send()

    def x_sent(m, carry):
        for side in range(2):
            n = 2 * m + side
            across_cores(n).wait_send()
            for t in range(last):
                x_hop(side, n, ringed.at[0, n], t).wait_send()
        return carry

    lax.fori_loop(0, chunks // 2, x_sent, 0)


def grad_sums(normed, grads, weights, slots):
    tokens, width = normed.shape
    units = grads.shape[1] // 2
    rows = width // (SIDE * SIDE)
    half = rows // 2
    block = (half, units)
    chunks, wide = 8, width // 8
    whole = pl.BlockSpec(memory_space=pltpu.VMEM)
    return pl.pallas_call(
        grad_rings,
        out_shape=(
            jax.ShapeDtypeStruct((2, rows, units), jnp.float32),
            jax.ShapeDtypeStruct((chunks, slots, wide), jnp.float32),
        ),
        in_specs=[whole, whole, pl.BlockSpec(memory_space=pl.ANY)],
        out_specs=(whole, whole),
        scratch_shapes=[
            pltpu.VMEM((4, SIDE, *block), jnp.bfloat16),
            pltpu.VMEM((4, SIDE - 1, SIDE, *block), jnp.bfloat16),
            pltpu.VMEM((4, *block), jnp.bfloat16),
            pltpu.VMEM((4, SIDE - 1, *block), jnp.bfloat16),
            pltpu.VMEM(weights.shape, jnp.bfloat16),
            pltpu.VMEM((chunks, 2, SIDE, slots, wide), jnp.bfloat16),
            pltpu.VMEM((chunks, SIDE, slots, wide), jnp.bfloat16),
            pltpu.VMEM((SIDE - 1, chunks, slots, wide), jnp.bfloat16),
            pltpu.SemaphoreType.DMA((4, SIDE - 1, SIDE)),
            pltpu.SemaphoreType.DMA((4, SIDE - 1, SIDE)),
            pltpu.SemaphoreType.DMA((4, SIDE - 1)),
            pltpu.SemaphoreType.DMA((4, SIDE - 1)),
            pltpu.SemaphoreType.DMA(()),
            pltpu.SemaphoreType.DMA((chunks,)),
            pltpu.SemaphoreType.DMA((chunks,)),
            pltpu.SemaphoreType.DMA((SIDE - 1, chunks)),
            pltpu.SemaphoreType.DMA((SIDE - 1, chunks)),
        ],
        compiler_params=pltpu.CompilerParams(
            collective_id=0, has_side_effects=True, vmem_limit_bytes=60 * 1024 * 1024
        ),
        cost_estimate=pl.CostEstimate(
            flops=4 * tokens * width * 2 * units,
            bytes_accessed=200_000_000,
            transcendentals=0,
        ),
        name="grad_rings",
    )(normed, grads, weights)


def doc_index(doc_lengths, positions):
    starts = jnp.cumsum(doc_lengths) - doc_lengths
    inside = (starts[None, :] <= positions[:, None]).astype(jnp.int32)
    return jnp.sum(inside, axis=1) - 1


def window_attention(queries, key_rows, values, query_pos, key_pos, query_doc, key_doc):
    row_count = queries.shape[0]
    head_count = queries.shape[1] // HEAD
    query_heads = queries.reshape(row_count, head_count, HEAD)
    key_heads = key_rows.reshape(-1, head_count, HEAD)
    value_heads = values.reshape(-1, head_count, HEAD)
    scores = jnp.einsum(
        "qhd,khd->hqk", query_heads, key_heads, preferred_element_type=jnp.float32
    ) / math.sqrt(HEAD)
    allowed = (key_pos[None, :] <= query_pos[:, None]) & (
        query_pos[:, None] - key_pos[None, :] < WINDOW
    )
    allowed = allowed & (key_pos[None, :] >= 0) & (key_doc[None, :] == query_doc[:, None])
    scores = jnp.where(allowed[None], scores, masked_score)
    row_max = jnp.max(scores, axis=-1, keepdims=True)
    weights = jnp.exp(scores - row_max)
    weights = (weights / jnp.sum(weights, axis=-1, keepdims=True)).astype(jnp.bfloat16)
    mixed = jnp.einsum("hqk,khd->qhd", weights, value_heads, preferred_element_type=jnp.float32)
    return mixed.reshape(row_count, head_count * HEAD)


def pool_patches(states, offsets, count):
    length = states.shape[0]
    slot_count = offsets.shape[0]
    head_count = states.shape[1] // HEAD
    slot_ids = jnp.arange(slot_count, dtype=jnp.int32)
    present = slot_ids < count
    following = jnp.concatenate([offsets[1:], jnp.full((1,), length, jnp.int32)])
    patch_ends = jnp.where(slot_ids == count - 1, length, following)
    byte_ids = jnp.arange(length, dtype=jnp.int32)
    member = (
        present[:, None]
        & (offsets[:, None] <= byte_ids[None, :])
        & (byte_ids[None, :] < patch_ends[:, None])
    )
    patch_sizes = jnp.sum(member.astype(jnp.float32), axis=1, keepdims=True)
    summed = jnp.dot(member.astype(jnp.bfloat16), states, preferred_element_type=jnp.float32)
    pooled = (summed / jnp.maximum(patch_sizes, 1.0)).astype(jnp.bfloat16)
    pooled_heads = pooled.reshape(slot_count, head_count, HEAD)
    state_heads = states.reshape(length, head_count, HEAD)
    scores = jnp.einsum(
        "jhd,bhd->hjb", pooled_heads, state_heads, preferred_element_type=jnp.float32
    ) / math.sqrt(HEAD)
    scores = jnp.where(member[None], scores, masked_score)
    row_max = jnp.max(scores, axis=-1, keepdims=True)
    weights = jnp.exp(scores - row_max)
    weights = (weights / jnp.sum(weights, axis=-1, keepdims=True)).astype(jnp.bfloat16)
    context = jnp.einsum("hjb,bhd->jhd", weights, state_heads, preferred_element_type=jnp.float32)
    context = context.reshape(slot_count, head_count * HEAD)
    return jnp.where(present[:, None], context, 0.0).astype(jnp.bfloat16)


def shards(
    bytes_in,
    doc_lengths,
    patch_offsets,
    patch_counts,
    w_query,
    w_key,
    w_value,
    w_proj,
    norm_gain,
    gate_w,
    up_w,
    d_hidden,
):
    states = bytes_in[0]
    length = states.shape[0]
    hop_count = (WINDOW - 2 + length) // length
    first_pos = lax.axis_index(("seq", "fsdp")) * length
    queries = jnp.dot(states, w_query, preferred_element_type=jnp.float32).astype(jnp.bfloat16)
    key_rows = jnp.dot(states, w_key, preferred_element_type=jnp.float32).astype(jnp.bfloat16)
    values = jnp.dot(states, w_value, preferred_element_type=jnp.float32).astype(jnp.bfloat16)
    key_parts = [key_rows]
    value_parts = [values]
    for distance in range(1, hop_count + 1):
        earlier = from_earlier(states, distance)
        earlier_keys = jnp.dot(earlier, w_key, preferred_element_type=jnp.float32).astype(
            jnp.bfloat16
        )
        earlier_values = jnp.dot(earlier, w_value, preferred_element_type=jnp.float32).astype(
            jnp.bfloat16
        )
        key_parts.insert(0, earlier_keys)
        value_parts.insert(0, earlier_values)
    key_all = jnp.concatenate(key_parts, axis=0)
    value_all = jnp.concatenate(value_parts, axis=0)
    query_pos = first_pos + jnp.arange(length, dtype=jnp.int32)
    key_pos = first_pos - hop_count * length + jnp.arange((hop_count + 1) * length, dtype=jnp.int32)
    key_doc = doc_index(doc_lengths, key_pos)
    query_doc = key_doc[hop_count * length :]
    mixed = window_attention(queries, key_all, value_all, query_pos, key_pos, query_doc, key_doc)
    hidden_bytes = (states.astype(jnp.float32) + mixed).astype(jnp.bfloat16)
    context = pool_patches(hidden_bytes, patch_offsets[0], patch_counts[0, 0])
    seq_index = lax.axis_index("seq")
    shard_part = gather_directly(context[None], "seq", 0)
    flat_part = shard_part.reshape(-1, shard_part.shape[-1])
    result = jnp.dot(flat_part, w_proj, preferred_element_type=jnp.float32).astype(jnp.bfloat16)
    features = result.reshape(shard_part.shape[0], shard_part.shape[1], -1)
    seq_count, slot_count, model_width = features.shape
    patch_float = features.reshape(seq_count * slot_count, model_width).astype(jnp.float32)
    inverse = lax.rsqrt(jnp.mean(patch_float * patch_float, axis=1, keepdims=True) + epsilon)
    normed = (patch_float * inverse * norm_gain).astype(jnp.bfloat16)
    units = gate_w.shape[1]
    weights = lax.all_gather(
        jnp.concatenate((gate_w, up_w), axis=1), "fsdp", axis=0, tiled=True
    )
    gate_pre = jnp.dot(normed, weights[:, :units], preferred_element_type=jnp.float32)
    up_pre = jnp.dot(normed, weights[:, units:], preferred_element_type=jnp.float32)
    sigmoid_gate = jax.nn.sigmoid(gate_pre)
    hidden = (gate_pre * sigmoid_gate * up_pre).astype(jnp.bfloat16)
    cotangent = d_hidden.reshape(seq_count * slot_count, units).astype(jnp.float32)
    gate_grad = (
        cotangent * up_pre * sigmoid_gate * (1.0 + gate_pre * (1.0 - sigmoid_gate))
    ).astype(jnp.bfloat16)
    up_grad = (cotangent * gate_pre * sigmoid_gate).astype(jnp.bfloat16)
    both_grads = jnp.concatenate([gate_grad, up_grad], axis=1)
    totals, inward = grad_sums(normed, both_grads, weights, slot_count)
    grad_gate, grad_up = totals[0], totals[1]
    normed_grad = laid_out(inward, 1)
    own_float = lax.dynamic_index_in_dim(
        patch_float.reshape(seq_count, slot_count, model_width), seq_index, 0, keepdims=False
    )
    own_inverse = lax.dynamic_index_in_dim(
        inverse.reshape(seq_count, slot_count, 1), seq_index, 0, keepdims=False
    )
    scaled = norm_gain * normed_grad
    patch_grad = own_inverse * scaled - own_float * (
        own_inverse * own_inverse * own_inverse
    ) * jnp.mean(scaled * own_float, axis=1, keepdims=True)
    return (hidden.reshape(seq_count, slot_count, units), grad_gate, grad_up, patch_grad[None])


def solution(mesh):
    return jax.shard_map(
        shards,
        mesh=mesh,
        in_specs=(
            P("seq", "fsdp", None),
            P(),
            P("seq", "fsdp"),
            P("seq", "fsdp"),
            P(),
            P(),
            P(),
            P(),
            P(),
            P("fsdp", "seq"),
            P("fsdp", "seq"),
            P(None, "fsdp", "seq"),
        ),
        out_specs=(
            P(None, "fsdp", "seq"),
            P("fsdp", "seq"),
            P("fsdp", "seq"),
            P("seq", "fsdp", None),
        ),
        check_vma=False,
    )
```

```python
import math

import jax
import jax.numpy as jnp
from jax import lax
from jax.experimental import pallas as pl
from jax.experimental.pallas import tpu as pltpu
from jax.sharding import PartitionSpec as P

HEAD = 128
WINDOW = 512


epsilon = 1e-05
masked_score = -1e30


def laid_out(pieces, dim):
    lengths = list(pieces.shape[1:])
    lengths[dim] *= pieces.shape[0]
    return jnp.moveaxis(pieces, 0, dim).reshape(lengths)


MESH = pl.DeviceIdType.MESH
SIDE = 4


def wrapped(value):
    return lax.rem(value + 2 * SIDE, SIDE)


def grad_rings(
    normed_ref,
    grads_ref,
    weights_hbm,
    out_ref,
    inward_ref,
    first,
    arrived,
    second,
    crossed,
    weights,
    parts,
    paired,
    ringed,
    put,
    got,
    put2,
    got2,
    loaded,
    put3,
    got3,
    put4,
    got4,
):
    seq = lax.axis_index("seq")
    spot = lax.axis_index("fsdp")
    x, core = lax.div(seq, 2), lax.rem(seq, 2)
    z, y = lax.div(spot, SIDE), lax.rem(spot, SIDE)
    rows = first.shape[2]
    units = out_ref.shape[2]
    chunks, _, _, slots, wide = parts.shape

    load = pltpu.make_async_copy(weights_hbm, weights, loaded)
    load.start()

    around = (
        (seq, wrapped(z + 1) * SIDE + y),
        (seq, wrapped(z - 1) * SIDE + y),
        (seq, z * SIDE + wrapped(y + 1)),
        (seq, z * SIDE + wrapped(y - 1)),
        (wrapped(x + 1) * 2 + core, spot),
        (wrapped(x - 1) * 2 + core, spot),
        (x * 2 + 1 - core, spot),
    )
    barrier = pltpu.get_barrier_semaphore()
    for neighbour in around:
        pl.semaphore_signal(barrier, inc=1, device_id=neighbour, device_id_type=MESH)
    pl.semaphore_wait(barrier, len(around))

    def place(stream):
        kind, half = stream // 2, stream % 2
        step = 1 - 2 * half
        along, across = (z, y) if kind == 0 else (y, z)
        if kind == 0:
            onward, sideways = around[half], around[2 + half]
        else:
            onward, sideways = around[2 + half], around[half]
        return kind, half, step, along, across, onward, sideways

    def own(stream, t, k):
        kind, half, step, along, across, _, _ = place(stream)
        far = wrapped(along - step * (1 + t))
        near = wrapped(across - step * (1 + k))
        zb, yb = (far, near) if kind == 0 else (near, far)
        at = pl.multiple_of((zb * SIDE + yb) * 2 * rows + half * rows, rows)
        return lax.dot_general(
            normed_ref[:, pl.ds(at, rows)],
            grads_ref[:, kind * units : (kind + 1) * units],
            (((0,), (0,)), ((), ())),
            preferred_element_type=jnp.float32,
        )

    def hop(stream, source, t, k):
        return pltpu.make_async_remote_copy(
            src_ref=source,
            dst_ref=arrived.at[stream, t, k],
            send_sem=put.at[stream, t, k],
            recv_sem=got.at[stream, t, k],
            device_id=place(stream)[5],
            device_id_type=MESH,
        )

    def hop2(stream, source, k):
        return pltpu.make_async_remote_copy(
            src_ref=source,
            dst_ref=crossed.at[stream, k],
            send_sem=put2.at[stream, k],
            recv_sem=got2.at[stream, k],
            device_id=place(stream)[6],
            device_id_type=MESH,
        )

    def across_cores(n):
        return pltpu.make_async_remote_copy(
            src_ref=parts.at[n, 1 - core],
            dst_ref=paired.at[n],
            send_sem=put3.at[n],
            recv_sem=got3.at[n],
            device_id=around[6],
            device_id_type=MESH,
        )

    def x_hop(side, n, source, t):
        return pltpu.make_async_remote_copy(
            src_ref=source,
            dst_ref=ringed.at[t, n],
            send_sem=put4.at[t, n],
            recv_sem=got4.at[t, n],
            device_id=around[4 + side],
            device_id_type=MESH,
        )

    def opening(k, carry):
        for stream in range(4):
            first[stream, k] = own(stream, 0, k).astype(jnp.bfloat16)
            hop(stream, first.at[stream, k], 0, k).start()
        return carry

    lax.fori_loop(0, SIDE, opening, 0)
    load.wait()

    def input_part(n):
        at = pl.multiple_of(n * wide, wide)
        value = lax.dot_general(
            grads_ref[...],
            weights[pl.ds(at, wide), :],
            (((1,), (1,)), ((), ())),
            preferred_element_type=jnp.float32,
        ).astype(jnp.bfloat16)
        for block in range(2 * SIDE):
            parts[n, block % 2, block // 2] = value[block * slots : (block + 1) * slots]
        across_cores(n).start()

    def middle(t, busy):
        def body(k, carry):
            for stream in range(4):
                value = own(stream, t, k)
                hop(stream, first.at[stream, k], t - 1, k).wait_recv()
                arrived[stream, t - 1, k] = (
                    value + arrived[stream, t - 1, k].astype(jnp.float32)
                ).astype(jnp.bfloat16)
                hop(stream, arrived.at[stream, t - 1, k], t, k).start()
            if busy:
                input_part(2 * k)
                input_part(2 * k + 1)
            return carry

        lax.fori_loop(0, SIDE, body, 0)

    def x_phase(t):
        def body(m, carry):
            for side in range(2):
                n = 2 * m + side
                block = wrapped(x - (1 - 2 * side) * (1 + t))
                if t == 0:
                    across_cores(n).wait_recv()
                    paired[n] = (
                        paired[n].astype(jnp.float32) + parts[n, core].astype(jnp.float32)
                    ).astype(jnp.bfloat16)
                    x_hop(side, n, paired.at[n, block], 0).start()
                else:
                    x_hop(side, n, paired.at[n, block], t - 1).wait_recv()
                    value = ringed[t - 1, n].astype(jnp.float32) + paired[n, block].astype(
                        jnp.float32
                    )
                    if t < SIDE - 1:
                        ringed[t - 1, n] = value.astype(jnp.bfloat16)
                        x_hop(side, n, ringed.at[t - 1, n], t).start()
                    else:
                        inward_ref[n] = value
            return carry

        lax.fori_loop(0, chunks // 2, body, 0)

    last = SIDE - 1

    def total(stream, k):
        value = own(stream, last, k)
        hop(stream, first.at[stream, k], last - 1, k).wait_recv()
        return value + arrived[stream, last - 1, k].astype(jnp.float32)

    middle(1, True)
    x_phase(0)
    middle(2, False)
    x_phase(1)

    for stream in range(4):
        second[stream] = total(stream, 0).astype(jnp.bfloat16)
        hop2(stream, second.at[stream], 0).start()
    x_phase(2)

    def crossing(k, carry):
        for stream in range(4):
            value = total(stream, k)
            hop2(stream, second.at[stream], k - 1).wait_recv()
            crossed[stream, k - 1] = (
                value + crossed[stream, k - 1].astype(jnp.float32)
            ).astype(jnp.bfloat16)
            hop2(stream, crossed.at[stream, k - 1], k).start()
        return carry

    lax.fori_loop(1, last, crossing, 0)
    x_phase(3)

    for stream in range(4):
        kind, half = stream // 2, stream % 2
        value = total(stream, last)
        hop2(stream, second.at[stream], last - 1).wait_recv()
        out_ref[kind, half * rows : (half + 1) * rows, :] = value + crossed[
            stream, last - 1
        ].astype(jnp.float32)

    def sent(index, carry):
        t, k = lax.div(index, SIDE), lax.rem(index, SIDE)
        for stream in range(4):
            hop(stream, first.at[stream, k], t, k).wait_send()
        return carry

    lax.fori_loop(0, last * SIDE, sent, 0)
    for stream in range(4):
        for k in range(last):
            hop2(stream, second.at[stream], k).wait_send()

    def x_sent(m, carry):
        for side in range(2):
            n = 2 * m + side
            across_cores(n).wait_send()
            for t in range(last):
                x_hop(side, n, ringed.at[0, n], t).wait_send()
        return carry

    lax.fori_loop(0, chunks // 2, x_sent, 0)


def grad_sums(normed, grads, weights, slots):
    tokens, width = normed.shape
    units = grads.shape[1] // 2
    rows = width // (SIDE * SIDE)
    half = rows // 2
    block = (half, units)
    chunks, wide = 8, width // 8
    whole = pl.BlockSpec(memory_space=pltpu.VMEM)
    return pl.pallas_call(
        grad_rings,
        out_shape=(
            jax.ShapeDtypeStruct((2, rows, units), jnp.float32),
            jax.ShapeDtypeStruct((chunks, slots, wide), jnp.float32),
        ),
        in_specs=[whole, whole, pl.BlockSpec(memory_space=pl.ANY)],
        out_specs=(whole, whole),
        scratch_shapes=[
            pltpu.VMEM((4, SIDE, *block), jnp.bfloat16),
            pltpu.VMEM((4, SIDE - 1, SIDE, *block), jnp.bfloat16),
            pltpu.VMEM((4, *block), jnp.bfloat16),
            pltpu.VMEM((4, SIDE - 1, *block), jnp.bfloat16),
            pltpu.VMEM(weights.shape, jnp.bfloat16),
            pltpu.VMEM((chunks, 2, SIDE, slots, wide), jnp.bfloat16),
            pltpu.VMEM((chunks, SIDE, slots, wide), jnp.bfloat16),
            pltpu.VMEM((SIDE - 1, chunks, slots, wide), jnp.bfloat16),
            pltpu.SemaphoreType.DMA((4, SIDE - 1, SIDE)),
            pltpu.SemaphoreType.DMA((4, SIDE - 1, SIDE)),
            pltpu.SemaphoreType.DMA((4, SIDE - 1)),
            pltpu.SemaphoreType.DMA((4, SIDE - 1)),
            pltpu.SemaphoreType.DMA(()),
            pltpu.SemaphoreType.DMA((chunks,)),
            pltpu.SemaphoreType.DMA((chunks,)),
            pltpu.SemaphoreType.DMA((SIDE - 1, chunks)),
            pltpu.SemaphoreType.DMA((SIDE - 1, chunks)),
        ],
        compiler_params=pltpu.CompilerParams(
            collective_id=0, has_side_effects=True, vmem_limit_bytes=60 * 1024 * 1024
        ),
        cost_estimate=pl.CostEstimate(
            flops=4 * tokens * width * 2 * units,
            bytes_accessed=200_000_000,
            transcendentals=0,
        ),
        name="grad_rings",
    )(normed, grads, weights)


def front(
    states_ref,
    query_doc_ref,
    key_doc_ref,
    spans_ref,
    gain_ref,
    gate_hbm,
    up_hbm,
    query_hbm,
    key_hbm,
    value_hbm,
    proj_hbm,
    weights_ref,
    normed_ref,
    own_features_ref,
    square,
    proj,
    earlier,
    passing,
    queries,
    keys,
    values,
    bias,
    mixed,
    pooled,
    contexts,
    loads,
    put_a,
    got_a,
    put_b,
    got_b,
    put_s,
    got_s,
    put_x,
    got_x,
    put_c,
    got_c,
):
    seq = lax.axis_index("seq")
    spot = lax.axis_index("fsdp")
    x, core = lax.div(seq, 2), lax.rem(seq, 2)
    z, y = lax.div(spot, SIDE), lax.rem(spot, SIDE)
    groups, spots = 2 * SIDE, SIDE * SIDE
    devices = groups * spots
    length, width = states_ref.shape
    slots = spans_ref.shape[0]
    heads = width // HEAD
    units = gate_hbm.shape[1]
    rows = gate_hbm.shape[0]
    half_rows = rows // 2
    model = proj_hbm.shape[1]
    split = 9 * units // 7

    def device_of(position):
        position = lax.rem(position + devices, devices)
        return lax.div(position, spots), lax.rem(position, spots)

    here = seq * spots + spot
    around = (
        (seq, wrapped(z + 1) * SIDE + y),
        (seq, wrapped(z - 1) * SIDE + y),
        (seq, z * SIDE + wrapped(y + 1)),
        (seq, z * SIDE + wrapped(y - 1)),
    )
    next_block = device_of(here + 1)
    relayed_to = device_of(seq * spots + z * SIDE + wrapped(y + 1) + 2)
    origin_seq, origin_spot = device_of(here - 2)
    origin_z, origin_y = lax.div(origin_spot, SIDE), lax.rem(origin_spot, SIDE)
    relayed_from = (origin_seq, origin_z * SIDE + wrapped(origin_y - 1))
    other_core = (x * 2 + 1 - core, spot)
    along_x = tuple((wrapped(x + by) * 2 + core, spot) for by in range(1, SIDE))

    places = [
        (weights_ref.at[pl.ds(pl.multiple_of(spot * rows, rows), rows), 0:units], gate_hbm),
        (weights_ref.at[pl.ds(pl.multiple_of(spot * rows, rows), rows), units:], up_hbm),
        (square.at[0], query_hbm),
        (square.at[1], key_hbm),
        (square.at[2], value_hbm),
        (proj, proj_hbm),
    ]
    load = [
        pltpu.make_async_copy(source, target, loads.at[i])
        for i, (target, source) in enumerate(places)
    ]
    for copy in load:
        copy.start()

    greeted = (
        *around,
        next_block,
        device_of(here - 1),
        relayed_to,
        relayed_from,
        other_core,
        *along_x,
    )
    barrier = pltpu.get_barrier_semaphore()
    for neighbour in greeted:
        pl.semaphore_signal(barrier, inc=1, device_id=neighbour, device_id_type=MESH)
    pl.semaphore_wait(barrier, len(greeted))

    def remote(source, target, sent, arrived, device):
        return pltpu.make_async_remote_copy(
            src_ref=source,
            dst_ref=target,
            send_sem=sent,
            recv_sem=arrived,
            device_id=device,
            device_id_type=MESH,
        )

    recent = earlier.at[length : 2 * length]
    oldest = earlier.at[0:length]
    to_next = remote(states_ref, recent, put_s.at[0], got_s.at[0], next_block)
    to_relay = remote(states_ref, passing, put_s.at[1], got_s.at[1], around[3])
    relay = remote(passing, oldest, put_s.at[2], got_s.at[2], relayed_to)
    to_next.start()
    to_relay.start()
    load[0].wait()
    load[1].wait()

    def piece(stream, t, k):
        kind, half = stream // 2, stream % 2
        step = 1 - 2 * half
        along, across = (z, y) if kind == 0 else (y, z)
        far, near = wrapped(along - step * t), wrapped(across - step * k)
        zb, yb = (far, near) if kind == 0 else (near, far)
        at = pl.multiple_of((zb * SIDE + yb) * rows + half * half_rows, half_rows)
        columns = slice(0, split) if kind == 0 else slice(split, 2 * units)
        return weights_ref.at[pl.ds(at, half_rows), columns]

    def small(stream, k):
        kind, half = stream // 2, stream % 2
        device = around[2 + half] if kind == 0 else around[half]
        region = piece(stream, 0, k)
        return remote(region, region, put_a.at[stream, k], got_a.at[stream, k], device)

    def large(stream, t, k):
        kind, half = stream // 2, stream % 2
        device = around[half] if kind == 0 else around[2 + half]
        region = piece(stream, t, k)
        return remote(
            region, region, put_b.at[stream, t, k], got_b.at[stream, t, k], device
        )

    last = SIDE - 1

    def spread(k):
        for stream in range(4):
            if k > 0:
                small(stream, k - 1).wait_recv()
            if k < last:
                small(stream, k).start()
            large(stream, 0, k).start()

    def pass_on(t, k):
        for stream in range(4):
            large(stream, t - 1, k).wait_recv()
            large(stream, t, k).start()

    spread(0)

    chunk = 2 * HEAD
    scale = 1.0 / math.sqrt(HEAD)

    def dot(a, b):
        return jnp.dot(a, b, preferred_element_type=jnp.float32)

    def dot_t(a, b):
        return lax.dot_general(
            a, b, (((1,), (1,)), ((), ())), preferred_element_type=jnp.float32
        )

    load[2].wait()

    def make_queries(n, carry):
        at = pl.ds(pl.multiple_of(n * chunk, chunk), chunk)
        queries[:, at] = dot(states_ref[...], square[0, :, at]).astype(jnp.bfloat16)
        return carry

    lax.fori_loop(0, width // chunk, make_queries, 0)
    spread(1)
    load[3].wait()
    load[4].wait()

    def keys_and_values(source, row):
        def body(n, carry):
            at = pl.ds(pl.multiple_of(n * chunk, chunk), chunk)
            keys[row : row + length, at] = dot(source[...], square[1, :, at]).astype(
                jnp.bfloat16
            )
            values[row : row + length, at] = dot(source[...], square[2, :, at]).astype(
                jnp.bfloat16
            )
            return carry

        lax.fori_loop(0, width // chunk, body, 0)

    keys_and_values(states_ref, 2 * length)
    pass_on(1, 0)
    to_relay.wait_recv()
    relay.start()
    spread(2)

    span = WINDOW + HEAD
    parts = length // HEAD
    for r in range(parts):
        row = lax.broadcasted_iota(jnp.int32, (HEAD, span), 0)
        column = lax.broadcasted_iota(jnp.int32, (HEAD, span), 1)
        allowed = (column > row) & (column <= row + WINDOW)
        start = 2 * length - WINDOW + r * HEAD
        allowed = allowed & (
            key_doc_ref[:, start : start + span] == query_doc_ref[r * HEAD : (r + 1) * HEAD, :]
        )
        bias[r] = jnp.where(allowed, 0.0, masked_score)

    to_next.wait_recv()
    keys_and_values(recent, length)
    pass_on(1, 1)
    spread(3)
    relay.wait_recv()
    keys_and_values(oldest, 0)
    pass_on(2, 0)
    pass_on(1, 2)

    def attend(h, carry):
        at = pl.ds(pl.multiple_of(h * HEAD, HEAD), HEAD)
        for r in range(parts):
            here_rows = slice(r * HEAD, (r + 1) * HEAD)
            start = 2 * length - WINDOW + r * HEAD
            scores = dot_t(queries[here_rows, at], keys[start : start + span, at])
            scores = scores * scale + bias[r]
            weights = jnp.exp(scores - jnp.max(scores, axis=1, keepdims=True))
            total = jnp.sum(weights, axis=1, keepdims=True)
            summed = dot(weights.astype(jnp.bfloat16), values[start : start + span, at])
            mixed[here_rows, at] = (
                states_ref[here_rows, at].astype(jnp.float32) + summed / total
            ).astype(jnp.bfloat16)
        return carry

    lax.fori_loop(0, heads // 2, attend, 0)
    pass_on(2, 1)
    lax.fori_loop(heads // 2, heads, attend, 0)
    pass_on(1, 3)

    begins, ends = spans_ref[:, 0:1], spans_ref[:, 1:2]
    present = spans_ref[:, 2:3] > 0
    byte = lax.broadcasted_iota(jnp.int32, (slots, length), 1)
    member = (byte >= begins) & (byte < ends)
    ones = jnp.where(member, 1.0, 0.0)
    pool_bias = jnp.where(member, 0.0, masked_score)
    sizes = jnp.maximum(jnp.sum(ones, axis=1, keepdims=True), 1.0)
    pooled[...] = (dot(ones.astype(jnp.bfloat16), mixed[...]) / sizes).astype(jnp.bfloat16)
    mine = pl.ds(pl.multiple_of(seq * slots, slots), slots)

    def pool(h, carry):
        at = pl.ds(pl.multiple_of(h * HEAD, HEAD), HEAD)
        scores = dot_t(pooled[:, at], mixed[:, at]) * scale + pool_bias
        weights = jnp.exp(scores - jnp.max(scores, axis=1, keepdims=True))
        total = jnp.sum(weights, axis=1, keepdims=True)
        summed = dot(weights.astype(jnp.bfloat16), mixed[:, at]) / total
        contexts[mine, at] = jnp.where(present, summed, 0.0).astype(jnp.bfloat16)
        return carry

    lax.fori_loop(0, heads, pool, 0)

    def context_of(group):
        return contexts.at[pl.ds(pl.multiple_of(group * slots, slots), slots)]

    def x_send(by):
        region = context_of(seq)
        return remote(region, region, put_x.at[by - 1], got_x.at[by - 1], along_x[by - 1])

    def core_send(by):
        region = context_of(wrapped(x - by) * 2 + core)
        return remote(region, region, put_c.at[by], got_c.at[by], other_core)

    for by in range(1, SIDE):
        x_send(by).start()
    core_send(0).start()
    pass_on(2, 2)
    for by in (1, 3, 2):
        x_send(by).wait_recv()
        core_send(by).start()
    for by in range(SIDE):
        core_send(by).wait_recv()
    load[5].wait()

    wide = 4 * HEAD

    def project(n, squares):
        at = pl.ds(pl.multiple_of(n * wide, wide), wide)
        features = dot(contexts[...], proj[:, at]).astype(jnp.bfloat16)
        normed_ref[:, at] = features
        full = features.astype(jnp.float32)
        return squares + jnp.sum(full * full, axis=1, keepdims=True)

    squares = jnp.zeros((groups * slots, 1), jnp.float32)
    squares = lax.fori_loop(0, model // wide // 2, project, squares)
    pass_on(2, 3)
    squares = lax.fori_loop(model // wide // 2, model // wide, project, squares)
    inverse = lax.rsqrt(squares / model + epsilon)
    own_features_ref[...] = normed_ref[mine, :]

    def normalize(n, carry):
        at = pl.ds(pl.multiple_of(n * wide, wide), wide)
        normed_ref[:, at] = (
            normed_ref[:, at].astype(jnp.float32) * inverse * gain_ref[:, at]
        ).astype(jnp.bfloat16)
        return carry

    lax.fori_loop(0, model // wide, normalize, 0)

    for stream in range(4):
        for k in range(SIDE):
            large(stream, last - 1, k).wait_recv()
    for copy in (to_next, to_relay, relay):
        copy.wait_send()
    for stream in range(4):
        for k in range(SIDE):
            if k < last:
                small(stream, k).wait_send()
            for t in range(last):
                large(stream, t, k).wait_send()
    for by in range(SIDE):
        if by > 0:
            x_send(by).wait_send()
        core_send(by).wait_send()


def front_part(states, query_doc, key_doc, spans, gain, gate_w, up_w, squares, w_proj):
    length, width = states.shape
    slots = spans.shape[0]
    rows, units = gate_w.shape
    model = w_proj.shape[1]
    tokens = 2 * SIDE * slots
    dma = pltpu.SemaphoreType.DMA
    whole = pl.BlockSpec(memory_space=pltpu.VMEM)
    anywhere = pl.BlockSpec(memory_space=pl.ANY)
    half = jnp.bfloat16
    return pl.pallas_call(
        front,
        out_shape=(
            jax.ShapeDtypeStruct((SIDE * SIDE * rows, 2 * units), half),
            jax.ShapeDtypeStruct((tokens, model), half),
            jax.ShapeDtypeStruct((slots, model), half),
        ),
        in_specs=[whole] * 5 + [anywhere] * 6,
        out_specs=(anywhere, whole, whole),
        scratch_shapes=[
            pltpu.VMEM((3, width, width), half),
            pltpu.VMEM((width, model), half),
            pltpu.VMEM((2 * length, width), half),
            pltpu.VMEM((length, width), half),
            pltpu.VMEM((length, width), half),
            pltpu.VMEM((3 * length, width), half),
            pltpu.VMEM((3 * length, width), half),
            pltpu.VMEM((length // HEAD, HEAD, WINDOW + HEAD), jnp.float32),
            pltpu.VMEM((length, width), half),
            pltpu.VMEM((slots, width), half),
            pltpu.VMEM((tokens, width), half),
            dma((6,)),
            dma((4, SIDE - 1)),
            dma((4, SIDE - 1)),
            dma((4, SIDE - 1, SIDE)),
            dma((4, SIDE - 1, SIDE)),
            dma((3,)),
            dma((3,)),
            dma((SIDE - 1,)),
            dma((SIDE - 1,)),
            dma((SIDE,)),
            dma((SIDE,)),
        ],
        compiler_params=pltpu.CompilerParams(
            collective_id=1, has_side_effects=True, vmem_limit_bytes=56 * 1024 * 1024
        ),
        name="front",
    )(states, query_doc, key_doc, spans, gain, gate_w, up_w, *squares, w_proj)


def doc_index(doc_lengths, positions):
    starts = jnp.cumsum(doc_lengths) - doc_lengths
    inside = (starts[None, :] <= positions[:, None]).astype(jnp.int32)
    return jnp.sum(inside, axis=1) - 1


def slot_spans(offsets, count, length):
    slot_ids = jnp.arange(offsets.shape[0], dtype=jnp.int32)
    following = jnp.concatenate([offsets[1:], jnp.full((1,), length, jnp.int32)])
    ends = jnp.where(slot_ids == count - 1, length, following)
    present = slot_ids < count
    begins, ends = jnp.where(present, offsets, 0), jnp.where(present, ends, 0)
    return jnp.stack([begins, ends, present.astype(jnp.int32)], axis=1)


def shards(
    bytes_in,
    doc_lengths,
    patch_offsets,
    patch_counts,
    w_query,
    w_key,
    w_value,
    w_proj,
    norm_gain,
    gate_w,
    up_w,
    d_hidden,
):
    states = bytes_in[0]
    length = states.shape[0]
    first_pos = lax.axis_index(("seq", "fsdp")) * length
    key_pos = first_pos - 2 * length + jnp.arange(3 * length, dtype=jnp.int32)
    key_doc = doc_index(doc_lengths, key_pos)
    spans = slot_spans(patch_offsets[0], patch_counts[0, 0], length)
    units = gate_w.shape[1]
    weights, normed, own_features = front_part(
        states,
        key_doc[2 * length :, None],
        key_doc[None],
        spans,
        norm_gain[None],
        gate_w,
        up_w,
        (w_query, w_key, w_value),
        w_proj,
    )
    slot_count, model_width = own_features.shape
    seq_count = normed.shape[0] // slot_count
    gate_pre = jnp.dot(normed, weights[:, :units], preferred_element_type=jnp.float32)
    up_pre = jnp.dot(normed, weights[:, units:], preferred_element_type=jnp.float32)
    sigmoid_gate = jax.nn.sigmoid(gate_pre)
    hidden = (gate_pre * sigmoid_gate * up_pre).astype(jnp.bfloat16)
    cotangent = d_hidden.reshape(seq_count * slot_count, units).astype(jnp.float32)
    gate_grad = (
        cotangent * up_pre * sigmoid_gate * (1.0 + gate_pre * (1.0 - sigmoid_gate))
    ).astype(jnp.bfloat16)
    up_grad = (cotangent * gate_pre * sigmoid_gate).astype(jnp.bfloat16)
    both_grads = jnp.concatenate([gate_grad, up_grad], axis=1)
    totals, inward = grad_sums(normed, both_grads, weights, slot_count)
    grad_gate, grad_up = totals[0], totals[1]
    normed_grad = laid_out(inward, 1)
    own_float = own_features.astype(jnp.float32)
    own_inverse = lax.rsqrt(
        jnp.mean(own_float * own_float, axis=1, keepdims=True) + epsilon
    )
    scaled = norm_gain * normed_grad
    patch_grad = own_inverse * scaled - own_float * (
        own_inverse * own_inverse * own_inverse
    ) * jnp.mean(scaled * own_float, axis=1, keepdims=True)
    return (hidden.reshape(seq_count, slot_count, units), grad_gate, grad_up, patch_grad[None])


def solution(mesh):
    return jax.shard_map(
        shards,
        mesh=mesh,
        in_specs=(
            P("seq", "fsdp", None),
            P(),
            P("seq", "fsdp"),
            P("seq", "fsdp"),
            P(),
            P(),
            P(),
            P(),
            P(),
            P("fsdp", "seq"),
            P("fsdp", "seq"),
            P(None, "fsdp", "seq"),
        ),
        out_specs=(
            P(None, "fsdp", "seq"),
            P("fsdp", "seq"),
            P("fsdp", "seq"),
            P("seq", "fsdp", None),
        ),
        check_vma=False,
    )
```

```python
import math

import jax
import jax.numpy as jnp
from jax import lax
from jax.experimental import pallas as pl
from jax.experimental.pallas import tpu as pltpu
from jax.sharding import PartitionSpec as P

HEAD = 128
WINDOW = 512


epsilon = 1e-05
masked_score = -1e30


def laid_out(pieces, dim):
    lengths = list(pieces.shape[1:])
    lengths[dim] *= pieces.shape[0]
    return jnp.moveaxis(pieces, 0, dim).reshape(lengths)


MESH = pl.DeviceIdType.MESH
SIDE = 4


def wrapped(value):
    return lax.rem(value + 2 * SIDE, SIDE)


def grad_rings(
    normed_ref,
    grads_ref,
    weights_hbm,
    out_ref,
    inward_ref,
    first,
    arrived,
    second,
    crossed,
    weights,
    parts,
    paired,
    ringed,
    put,
    got,
    put2,
    got2,
    loaded,
    put3,
    got3,
    put4,
    got4,
):
    seq = lax.axis_index("seq")
    spot = lax.axis_index("fsdp")
    x, core = lax.div(seq, 2), lax.rem(seq, 2)
    z, y = lax.div(spot, SIDE), lax.rem(spot, SIDE)
    rows = first.shape[2]
    units = out_ref.shape[2]
    chunks, _, _, slots, wide = parts.shape

    load = pltpu.make_async_copy(weights_hbm, weights, loaded)
    load.start()

    around = (
        (seq, wrapped(z + 1) * SIDE + y),
        (seq, wrapped(z - 1) * SIDE + y),
        (seq, z * SIDE + wrapped(y + 1)),
        (seq, z * SIDE + wrapped(y - 1)),
        (wrapped(x + 1) * 2 + core, spot),
        (wrapped(x - 1) * 2 + core, spot),
        (x * 2 + 1 - core, spot),
    )
    barrier = pltpu.get_barrier_semaphore()
    for neighbour in around:
        pl.semaphore_signal(barrier, inc=1, device_id=neighbour, device_id_type=MESH)
    pl.semaphore_wait(barrier, len(around))

    def place(stream):
        kind, half = stream // 2, stream % 2
        step = 1 - 2 * half
        along, across = (z, y) if kind == 0 else (y, z)
        if kind == 0:
            onward, sideways = around[half], around[2 + half]
        else:
            onward, sideways = around[2 + half], around[half]
        return kind, half, step, along, across, onward, sideways

    def own(stream, t, k):
        kind, half, step, along, across, _, _ = place(stream)
        far = wrapped(along - step * (1 + t))
        near = wrapped(across - step * (1 + k))
        zb, yb = (far, near) if kind == 0 else (near, far)
        at = pl.multiple_of((zb * SIDE + yb) * 2 * rows + half * rows, rows)
        return lax.dot_general(
            normed_ref[:, pl.ds(at, rows)],
            grads_ref[:, kind * units : (kind + 1) * units],
            (((0,), (0,)), ((), ())),
            preferred_element_type=jnp.float32,
        )

    def hop(stream, source, t, k):
        return pltpu.make_async_remote_copy(
            src_ref=source,
            dst_ref=arrived.at[stream, t, k],
            send_sem=put.at[stream, t, k],
            recv_sem=got.at[stream, t, k],
            device_id=place(stream)[5],
            device_id_type=MESH,
        )

    def hop2(stream, source, k):
        return pltpu.make_async_remote_copy(
            src_ref=source,
            dst_ref=crossed.at[stream, k],
            send_sem=put2.at[stream, k],
            recv_sem=got2.at[stream, k],
            device_id=place(stream)[6],
            device_id_type=MESH,
        )

    def across_cores(n):
        return pltpu.make_async_remote_copy(
            src_ref=parts.at[n, 1 - core],
            dst_ref=paired.at[n],
            send_sem=put3.at[n],
            recv_sem=got3.at[n],
            device_id=around[6],
            device_id_type=MESH,
        )

    def x_hop(side, n, source, t):
        return pltpu.make_async_remote_copy(
            src_ref=source,
            dst_ref=ringed.at[t, n],
            send_sem=put4.at[t, n],
            recv_sem=got4.at[t, n],
            device_id=around[4 + side],
            device_id_type=MESH,
        )

    def opening(k, carry):
        for stream in range(4):
            first[stream, k] = own(stream, 0, k).astype(jnp.bfloat16)
            hop(stream, first.at[stream, k], 0, k).start()
        return carry

    lax.fori_loop(0, SIDE, opening, 0)
    load.wait()

    def input_part(n):
        at = pl.multiple_of(n * wide, wide)
        value = lax.dot_general(
            grads_ref[...],
            weights[pl.ds(at, wide), :],
            (((1,), (1,)), ((), ())),
            preferred_element_type=jnp.float32,
        ).astype(jnp.bfloat16)
        for block in range(2 * SIDE):
            parts[n, block % 2, block // 2] = value[block * slots : (block + 1) * slots]
        across_cores(n).start()

    def middle(t, busy):
        def body(k, carry):
            for stream in range(4):
                value = own(stream, t, k)
                hop(stream, first.at[stream, k], t - 1, k).wait_recv()
                arrived[stream, t - 1, k] = (
                    value + arrived[stream, t - 1, k].astype(jnp.float32)
                ).astype(jnp.bfloat16)
                hop(stream, arrived.at[stream, t - 1, k], t, k).start()
            if busy:
                input_part(2 * k)
                input_part(2 * k + 1)
            return carry

        lax.fori_loop(0, SIDE, body, 0)

    def x_phase(t):
        def body(m, carry):
            for side in range(2):
                n = 2 * m + side
                block = wrapped(x - (1 - 2 * side) * (1 + t))
                if t == 0:
                    across_cores(n).wait_recv()
                    paired[n] = (
                        paired[n].astype(jnp.float32) + parts[n, core].astype(jnp.float32)
                    ).astype(jnp.bfloat16)
                    x_hop(side, n, paired.at[n, block], 0).start()
                else:
                    x_hop(side, n, paired.at[n, block], t - 1).wait_recv()
                    value = ringed[t - 1, n].astype(jnp.float32) + paired[n, block].astype(
                        jnp.float32
                    )
                    if t < SIDE - 1:
                        ringed[t - 1, n] = value.astype(jnp.bfloat16)
                        x_hop(side, n, ringed.at[t - 1, n], t).start()
                    else:
                        inward_ref[n] = value
            return carry

        lax.fori_loop(0, chunks // 2, body, 0)

    last = SIDE - 1

    def total(stream, k):
        value = own(stream, last, k)
        hop(stream, first.at[stream, k], last - 1, k).wait_recv()
        return value + arrived[stream, last - 1, k].astype(jnp.float32)

    middle(1, True)
    x_phase(0)
    middle(2, False)
    x_phase(1)

    for stream in range(4):
        second[stream] = total(stream, 0).astype(jnp.bfloat16)
        hop2(stream, second.at[stream], 0).start()
    x_phase(2)

    def crossing(k, carry):
        for stream in range(4):
            value = total(stream, k)
            hop2(stream, second.at[stream], k - 1).wait_recv()
            crossed[stream, k - 1] = (
                value + crossed[stream, k - 1].astype(jnp.float32)
            ).astype(jnp.bfloat16)
            hop2(stream, crossed.at[stream, k - 1], k).start()
        return carry

    lax.fori_loop(1, last, crossing, 0)
    x_phase(3)

    for stream in range(4):
        kind, half = stream // 2, stream % 2
        value = total(stream, last)
        hop2(stream, second.at[stream], last - 1).wait_recv()
        out_ref[kind, half * rows : (half + 1) * rows, :] = value + crossed[
            stream, last - 1
        ].astype(jnp.float32)

    def sent(index, carry):
        t, k = lax.div(index, SIDE), lax.rem(index, SIDE)
        for stream in range(4):
            hop(stream, first.at[stream, k], t, k).wait_send()
        return carry

    lax.fori_loop(0, last * SIDE, sent, 0)
    for stream in range(4):
        for k in range(last):
            hop2(stream, second.at[stream], k).wait_send()

    def x_sent(m, carry):
        for side in range(2):
            n = 2 * m + side
            across_cores(n).wait_send()
            for t in range(last):
                x_hop(side, n, ringed.at[0, n], t).wait_send()
        return carry

    lax.fori_loop(0, chunks // 2, x_sent, 0)


def grad_sums(normed, grads, weights, slots):
    tokens, width = normed.shape
    units = grads.shape[1] // 2
    rows = width // (SIDE * SIDE)
    half = rows // 2
    block = (half, units)
    chunks, wide = 8, width // 8
    whole = pl.BlockSpec(memory_space=pltpu.VMEM)
    return pl.pallas_call(
        grad_rings,
        out_shape=(
            jax.ShapeDtypeStruct((2, rows, units), jnp.float32),
            jax.ShapeDtypeStruct((chunks, slots, wide), jnp.float32),
        ),
        in_specs=[whole, whole, pl.BlockSpec(memory_space=pl.ANY)],
        out_specs=(whole, whole),
        scratch_shapes=[
            pltpu.VMEM((4, SIDE, *block), jnp.bfloat16),
            pltpu.VMEM((4, SIDE - 1, SIDE, *block), jnp.bfloat16),
            pltpu.VMEM((4, *block), jnp.bfloat16),
            pltpu.VMEM((4, SIDE - 1, *block), jnp.bfloat16),
            pltpu.VMEM(weights.shape, jnp.bfloat16),
            pltpu.VMEM((chunks, 2, SIDE, slots, wide), jnp.bfloat16),
            pltpu.VMEM((chunks, SIDE, slots, wide), jnp.bfloat16),
            pltpu.VMEM((SIDE - 1, chunks, slots, wide), jnp.bfloat16),
            pltpu.SemaphoreType.DMA((4, SIDE - 1, SIDE)),
            pltpu.SemaphoreType.DMA((4, SIDE - 1, SIDE)),
            pltpu.SemaphoreType.DMA((4, SIDE - 1)),
            pltpu.SemaphoreType.DMA((4, SIDE - 1)),
            pltpu.SemaphoreType.DMA(()),
            pltpu.SemaphoreType.DMA((chunks,)),
            pltpu.SemaphoreType.DMA((chunks,)),
            pltpu.SemaphoreType.DMA((SIDE - 1, chunks)),
            pltpu.SemaphoreType.DMA((SIDE - 1, chunks)),
        ],
        compiler_params=pltpu.CompilerParams(
            collective_id=0, has_side_effects=True, vmem_limit_bytes=60 * 1024 * 1024
        ),
        cost_estimate=pl.CostEstimate(
            flops=4 * tokens * width * 2 * units,
            bytes_accessed=200_000_000,
            transcendentals=0,
        ),
        name="grad_rings",
    )(normed, grads, weights)


def front(
    states_ref,
    query_doc_ref,
    key_doc_ref,
    spans_ref,
    gain_ref,
    cotangent_ref,
    gate_hbm,
    up_hbm,
    query_hbm,
    key_hbm,
    value_hbm,
    proj_hbm,
    weights_ref,
    normed_ref,
    own_features_ref,
    hidden_ref,
    grads_ref,
    gates,
    ups,
    maps,
    crossed,
    sums,
    earlier,
    queries,
    keys,
    values,
    bias,
    mixed,
    pooled,
    contexts,
    loads,
    stores,
    put_a,
    got_a,
    put_b,
    got_b,
    put_s,
    got_s,
    put_x,
    got_x,
    put_c,
    got_c,
):
    seq = lax.axis_index("seq")
    spot = lax.axis_index("fsdp")
    x, core = lax.div(seq, 2), lax.rem(seq, 2)
    z, y = lax.div(spot, SIDE), lax.rem(spot, SIDE)
    groups, spots = 2 * SIDE, SIDE * SIDE
    devices = groups * spots
    length, width = states_ref.shape
    slots = spans_ref.shape[0]
    heads = width // HEAD
    units = gate_hbm.shape[1]
    rows = gate_hbm.shape[0]
    model = proj_hbm.shape[1]
    ranges = (slice(0, 3 * HEAD), slice(3 * HEAD, units))

    def device_of(position):
        position = lax.rem(position + devices, devices)
        return lax.div(position, spots), lax.rem(position, spots)

    here = seq * spots + spot
    around = (
        (seq, wrapped(z + 1) * SIDE + y),
        (seq, wrapped(z - 1) * SIDE + y),
        (seq, z * SIDE + wrapped(y + 1)),
        (seq, z * SIDE + wrapped(y - 1)),
    )
    next_block = device_of(here + 1)
    after_next = device_of(here + 2)
    other_core = (x * 2 + 1 - core, spot)
    along_x = tuple((wrapped(x + by) * 2 + core, spot) for by in range(1, SIDE))

    places = [
        (gates.at[z, y], gate_hbm),
        (ups.at[y, z], up_hbm),
        (maps.at[:, 0:width], query_hbm),
        (maps.at[:, width : 2 * width], key_hbm),
        (maps.at[:, 2 * width : 3 * width], value_hbm),
        (maps, proj_hbm),
    ]
    load = [
        pltpu.make_async_copy(source, target, loads.at[i])
        for i, (target, source) in enumerate(places)
    ]
    for copy in load[:5]:
        copy.start()

    greeted = (
        *around,
        next_block,
        device_of(here - 1),
        after_next,
        device_of(here - 2),
        other_core,
        *along_x,
    )
    barrier = pltpu.get_barrier_semaphore()
    for neighbour in greeted:
        pl.semaphore_signal(barrier, inc=1, device_id=neighbour, device_id_type=MESH)
    pl.semaphore_wait(barrier, len(greeted))

    def remote(source, target, sent, arrived, device):
        return pltpu.make_async_remote_copy(
            src_ref=source,
            dst_ref=target,
            send_sem=sent,
            recv_sem=arrived,
            device_id=device,
            device_id_type=MESH,
        )

    recent = earlier.at[length : 2 * length]
    oldest = earlier.at[0:length]
    to_next = remote(states_ref, recent, put_s.at[0], got_s.at[0], next_block)
    to_after = remote(states_ref, oldest, put_s.at[1], got_s.at[1], after_next)
    to_next.start()
    to_after.start()
    load[0].wait()
    load[1].wait()

    def place(stream, t):
        kind, half = stream // 2, stream % 2
        along = z if kind == 0 else y
        return (gates, ups)[kind], wrapped(along - (1 - 2 * half) * t), ranges[half]

    def piece(stream, t, k):
        kind, half = stream // 2, stream % 2
        across = y if kind == 0 else z
        buffer, far, columns = place(stream, t)
        return buffer.at[far, wrapped(across - (1 - 2 * half) * k), :, columns]

    def small(stream, k):
        kind, half = stream // 2, stream % 2
        device = around[2 + half] if kind == 0 else around[half]
        region = piece(stream, 0, k)
        return remote(region, region, put_a.at[stream, k], got_a.at[stream, k], device)

    def large(stream, t, k):
        kind, half = stream // 2, stream % 2
        device = around[half] if kind == 0 else around[2 + half]
        region = piece(stream, t, k)
        return remote(
            region, region, put_b.at[stream, t, k], got_b.at[stream, t, k], device
        )

    def store(stream, t):
        kind, half = stream // 2, stream % 2
        buffer, far, columns = place(stream, t)
        target = slice(kind * units + columns.start, kind * units + columns.stop)
        if kind == 0:
            target = weights_ref.at[far, :, :, target]
        else:
            target = weights_ref.at[:, far, :, target]
        return pltpu.make_async_copy(
            buffer.at[far, :, :, columns], target, stores.at[stream, t]
        )

    last = SIDE - 1

    def spread(k):
        for stream in range(4):
            if k > 0:
                small(stream, k - 1).wait_recv()
            if k < last:
                small(stream, k).start()
            large(stream, 0, k).start()

    def pass_on(t, k):
        for stream in range(4):
            large(stream, t - 1, k).wait_recv()
            large(stream, t, k).start()

    spread(0)

    chunk = 2 * HEAD
    scale = 1.0 / math.sqrt(HEAD)

    def dot(a, b):
        return jnp.dot(a, b, preferred_element_type=jnp.float32)

    def dot_t(a, b):
        return lax.dot_general(
            a, b, (((1,), (1,)), ((), ())), preferred_element_type=jnp.float32
        )

    load[2].wait()

    def make_queries(n, carry):
        at = pl.ds(pl.multiple_of(n * chunk, chunk), chunk)
        queries[:, at] = dot(states_ref[...], maps[:, at]).astype(jnp.bfloat16)
        return carry

    lax.fori_loop(0, width // chunk, make_queries, 0)
    spread(1)
    load[3].wait()
    load[4].wait()

    def keys_and_values(source, row):
        def body(n, carry):
            at = pl.ds(pl.multiple_of(n * chunk, chunk), chunk)
            key_at = pl.ds(pl.multiple_of(width + n * chunk, chunk), chunk)
            value_at = pl.ds(pl.multiple_of(2 * width + n * chunk, chunk), chunk)
            into = slice(row, row + length)
            keys[into, at] = dot(source[...], maps[:, key_at]).astype(jnp.bfloat16)
            values[into, at] = dot(source[...], maps[:, value_at]).astype(jnp.bfloat16)
            return carry

        lax.fori_loop(0, width // chunk, body, 0)

    keys_and_values(states_ref, 2 * length)
    pass_on(1, 0)
    spread(2)

    span = WINDOW + HEAD
    parts = length // HEAD
    for r in range(parts):
        row = lax.broadcasted_iota(jnp.int32, (HEAD, span), 0)
        column = lax.broadcasted_iota(jnp.int32, (HEAD, span), 1)
        allowed = (column > row) & (column <= row + WINDOW)
        start = 2 * length - WINDOW + r * HEAD
        allowed = allowed & (
            key_doc_ref[:, start : start + span] == query_doc_ref[r * HEAD : (r + 1) * HEAD, :]
        )
        bias[r] = jnp.where(allowed, 0.0, masked_score)

    to_next.wait_recv()
    keys_and_values(recent, length)
    pass_on(1, 1)
    spread(3)
    to_after.wait_recv()
    keys_and_values(oldest, 0)
    load[5].start()
    pass_on(2, 0)
    pass_on(1, 2)

    def attend(h, carry):
        at = pl.ds(pl.multiple_of(h * HEAD, HEAD), HEAD)
        for r in range(parts):
            here_rows = slice(r * HEAD, (r + 1) * HEAD)
            start = 2 * length - WINDOW + r * HEAD
            scores = dot_t(queries[here_rows, at], keys[start : start + span, at])
            scores = scores * scale + bias[r]
            weights = jnp.exp(scores - jnp.max(scores, axis=1, keepdims=True))
            total = jnp.sum(weights, axis=1, keepdims=True)
            summed = dot(weights.astype(jnp.bfloat16), values[start : start + span, at])
            mixed[here_rows, at] = (
                states_ref[here_rows, at].astype(jnp.float32) + summed / total
            ).astype(jnp.bfloat16)
        return carry

    lax.fori_loop(0, heads // 2, attend, 0)
    pass_on(2, 1)
    lax.fori_loop(heads // 2, heads, attend, 0)
    pass_on(1, 3)

    begins, ends = spans_ref[:, 0:1], spans_ref[:, 1:2]
    present = spans_ref[:, 2:3] > 0
    byte = lax.broadcasted_iota(jnp.int32, (slots, length), 1)
    member = (byte >= begins) & (byte < ends)
    ones = jnp.where(member, 1.0, 0.0)
    pool_bias = jnp.where(member, 0.0, masked_score)
    sizes = jnp.maximum(jnp.sum(ones, axis=1, keepdims=True), 1.0)
    pooled[...] = (dot(ones.astype(jnp.bfloat16), mixed[...]) / sizes).astype(jnp.bfloat16)
    mine = pl.ds(pl.multiple_of(seq * slots, slots), slots)

    def pool(h, carry):
        at = pl.ds(pl.multiple_of(h * HEAD, HEAD), HEAD)
        scores = dot_t(pooled[:, at], mixed[:, at]) * scale + pool_bias
        weights = jnp.exp(scores - jnp.max(scores, axis=1, keepdims=True))
        total = jnp.sum(weights, axis=1, keepdims=True)
        summed = dot(weights.astype(jnp.bfloat16), mixed[:, at]) / total
        contexts[mine, at] = jnp.where(present, summed, 0.0).astype(jnp.bfloat16)
        return carry

    lax.fori_loop(0, heads, pool, 0)

    def context_of(group):
        return contexts.at[pl.ds(pl.multiple_of(group * slots, slots), slots)]

    def x_send(by):
        region = context_of(seq)
        return remote(region, region, put_x.at[by - 1], got_x.at[by - 1], along_x[by - 1])

    def core_send(by):
        region = context_of(wrapped(x - by) * 2 + core)
        return remote(region, region, put_c.at[by], got_c.at[by], other_core)

    for by in range(1, SIDE):
        x_send(by).start()
    core_send(0).start()
    pass_on(2, 2)
    for by in (1, 3, 2):
        x_send(by).wait_recv()
        core_send(by).start()
    for by in range(SIDE):
        core_send(by).wait_recv()
    load[5].wait()

    wide = 4 * HEAD

    def project(n, squares):
        at = pl.ds(pl.multiple_of(n * wide, wide), wide)
        features = dot(contexts[...], maps[:, at]).astype(jnp.bfloat16)
        normed_ref[:, at] = features
        full = features.astype(jnp.float32)
        return squares + jnp.sum(full * full, axis=1, keepdims=True)

    squares = jnp.zeros((groups * slots, 1), jnp.float32)
    squares = lax.fori_loop(0, model // wide // 2, project, squares)
    pass_on(2, 3)
    squares = lax.fori_loop(model // wide // 2, model // wide, project, squares)
    inverse = lax.rsqrt(squares / model + epsilon)
    own_features_ref[...] = normed_ref[mine, :]

    def normalize(n, carry):
        at = pl.ds(pl.multiple_of(n * rows, rows), rows)
        turned = (n % SIDE) * SIDE + n // SIDE
        value = (normed_ref[:, at].astype(jnp.float32) * inverse * gain_ref[:, at]).astype(
            jnp.bfloat16
        )
        normed_ref[:, at] = value
        crossed[:, pl.ds(pl.multiple_of(turned * rows, rows), rows)] = value
        return carry

    lax.fori_loop(0, model // rows, normalize, 0)
    sums[...] = jnp.zeros_like(sums)

    def accumulate(t, carry):
        @pl.when(t == last)
        def _():
            for stream in range(4):
                for k in range(SIDE):
                    large(stream, last - 1, k).wait_recv()

        for stream in range(4):
            store(stream, t).start()
            buffer, far, columns = place(stream, t)
            kind, count = stream // 2, columns.stop - columns.start
            deep = SIDE * rows
            at = pl.ds(pl.multiple_of(far * deep, deep), deep)
            block = buffer[far, :, :, columns].reshape(deep, count)
            sums[kind, :, columns] += dot((normed_ref, crossed)[kind][:, at], block)
        return carry

    lax.fori_loop(0, SIDE, accumulate, 0)

    def gating(n, carry):
        at = pl.ds(pl.multiple_of(n * slots, slots), slots)
        gate_pre, up_pre = sums[0, at], sums[1, at]
        sigmoid_gate = jax.nn.sigmoid(gate_pre)
        swish = gate_pre * sigmoid_gate
        cotangent = cotangent_ref[at, :].astype(jnp.float32)
        hidden_ref[at, :] = (swish * up_pre).astype(jnp.bfloat16)
        grads_ref[at, 0:units] = (
            cotangent * up_pre * sigmoid_gate * (1.0 + gate_pre * (1.0 - sigmoid_gate))
        ).astype(jnp.bfloat16)
        grads_ref[at, units : 2 * units] = (cotangent * swish).astype(jnp.bfloat16)
        return carry

    lax.fori_loop(0, groups, gating, 0)

    to_next.wait_send()
    to_after.wait_send()
    for stream in range(4):
        for k in range(SIDE):
            if k < last:
                small(stream, k).wait_send()
            for t in range(last):
                large(stream, t, k).wait_send()
            store(stream, k).wait()
    for by in range(SIDE):
        if by > 0:
            x_send(by).wait_send()
        core_send(by).wait_send()


def front_part(
    states, query_doc, key_doc, spans, gain, cotangent, gate_w, up_w, squares, w_proj
):
    length, width = states.shape
    slots = spans.shape[0]
    rows, units = gate_w.shape
    model = w_proj.shape[1]
    tokens = 2 * SIDE * slots
    dma = pltpu.SemaphoreType.DMA
    whole = pl.BlockSpec(memory_space=pltpu.VMEM)
    anywhere = pl.BlockSpec(memory_space=pl.ANY)
    half = jnp.bfloat16
    return pl.pallas_call(
        front,
        out_shape=(
            jax.ShapeDtypeStruct((SIDE, SIDE, rows, 2 * units), half),
            jax.ShapeDtypeStruct((tokens, model), half),
            jax.ShapeDtypeStruct((slots, model), half),
            jax.ShapeDtypeStruct((tokens, units), half),
            jax.ShapeDtypeStruct((tokens, 2 * units), half),
        ),
        in_specs=[whole] * 6 + [anywhere] * 6,
        out_specs=(anywhere, whole, whole, whole, whole),
        scratch_shapes=[
            pltpu.VMEM((SIDE, SIDE, rows, units), half),
            pltpu.VMEM((SIDE, SIDE, rows, units), half),
            pltpu.VMEM((width, model), half),
            pltpu.VMEM((tokens, model), half),
            pltpu.VMEM((2, tokens, units), jnp.float32),
            pltpu.VMEM((2 * length, width), half),
            pltpu.VMEM((length, width), half),
            pltpu.VMEM((3 * length, width), half),
            pltpu.VMEM((3 * length, width), half),
            pltpu.VMEM((length // HEAD, HEAD, WINDOW + HEAD), jnp.float32),
            pltpu.VMEM((length, width), half),
            pltpu.VMEM((slots, width), half),
            pltpu.VMEM((tokens, width), half),
            dma((6,)),
            dma((4, SIDE)),
            dma((4, SIDE - 1)),
            dma((4, SIDE - 1)),
            dma((4, SIDE - 1, SIDE)),
            dma((4, SIDE - 1, SIDE)),
            dma((2,)),
            dma((2,)),
            dma((SIDE - 1,)),
            dma((SIDE - 1,)),
            dma((SIDE,)),
            dma((SIDE,)),
        ],
        compiler_params=pltpu.CompilerParams(
            collective_id=1, has_side_effects=True, vmem_limit_bytes=62 * 1024 * 1024
        ),
        name="front",
    )(states, query_doc, key_doc, spans, gain, cotangent, gate_w, up_w, *squares, w_proj)


def doc_index(doc_lengths, positions):
    starts = jnp.cumsum(doc_lengths) - doc_lengths
    inside = (starts[None, :] <= positions[:, None]).astype(jnp.int32)
    return jnp.sum(inside, axis=1) - 1


def slot_spans(offsets, count, length):
    slot_ids = jnp.arange(offsets.shape[0], dtype=jnp.int32)
    following = jnp.concatenate([offsets[1:], jnp.full((1,), length, jnp.int32)])
    ends = jnp.where(slot_ids == count - 1, length, following)
    present = slot_ids < count
    begins, ends = jnp.where(present, offsets, 0), jnp.where(present, ends, 0)
    return jnp.stack([begins, ends, present.astype(jnp.int32)], axis=1)


def shards(
    bytes_in,
    doc_lengths,
    patch_offsets,
    patch_counts,
    w_query,
    w_key,
    w_value,
    w_proj,
    norm_gain,
    gate_w,
    up_w,
    d_hidden,
):
    states = bytes_in[0]
    length = states.shape[0]
    first_pos = lax.axis_index(("seq", "fsdp")) * length
    key_pos = first_pos - 2 * length + jnp.arange(3 * length, dtype=jnp.int32)
    key_doc = doc_index(doc_lengths, key_pos)
    spans = slot_spans(patch_offsets[0], patch_counts[0, 0], length)
    units = gate_w.shape[1]
    weights, normed, own_features, hidden, both_grads = front_part(
        states,
        key_doc[2 * length :, None],
        key_doc[None],
        spans,
        norm_gain[None],
        d_hidden.reshape(-1, units),
        gate_w,
        up_w,
        (w_query, w_key, w_value),
        w_proj,
    )
    slot_count, model_width = own_features.shape
    seq_count = normed.shape[0] // slot_count
    totals, inward = grad_sums(
        normed, both_grads, weights.reshape(model_width, 2 * units), slot_count
    )
    grad_gate, grad_up = totals[0], totals[1]
    normed_grad = laid_out(inward, 1)
    own_float = own_features.astype(jnp.float32)
    own_inverse = lax.rsqrt(
        jnp.mean(own_float * own_float, axis=1, keepdims=True) + epsilon
    )
    scaled = norm_gain * normed_grad
    patch_grad = own_inverse * scaled - own_float * (
        own_inverse * own_inverse * own_inverse
    ) * jnp.mean(scaled * own_float, axis=1, keepdims=True)
    return (hidden.reshape(seq_count, slot_count, units), grad_gate, grad_up, patch_grad[None])


def solution(mesh):
    return jax.shard_map(
        shards,
        mesh=mesh,
        in_specs=(
            P("seq", "fsdp", None),
            P(),
            P("seq", "fsdp"),
            P("seq", "fsdp"),
            P(),
            P(),
            P(),
            P(),
            P(),
            P("fsdp", "seq"),
            P("fsdp", "seq"),
            P(None, "fsdp", "seq"),
        ),
        out_specs=(
            P(None, "fsdp", "seq"),
            P("fsdp", "seq"),
            P("fsdp", "seq"),
            P("seq", "fsdp", None),
        ),
        check_vma=False,
    )
```

```python
import math

import jax
import jax.numpy as jnp
from jax import lax
from jax.experimental import pallas as pl
from jax.experimental.pallas import tpu as pltpu
from jax.sharding import PartitionSpec as P

HEAD = 128
WINDOW = 512


epsilon = 1e-05
masked_score = -1e30


MESH = pl.DeviceIdType.MESH
SIDE = 4


def wrapped(value):
    return lax.rem(value + 2 * SIDE, SIDE)


def grad_rings(
    normed_ref,
    grads_ref,
    features_ref,
    gain_ref,
    weights_hbm,
    gate_ref,
    up_ref,
    patch_ref,
    inward,
    first,
    arrived,
    second,
    crossed,
    weights,
    parts,
    paired,
    ringed,
    put,
    got,
    put2,
    got2,
    loaded,
    put3,
    got3,
    put4,
    got4,
):
    seq = lax.axis_index("seq")
    spot = lax.axis_index("fsdp")
    x, core = lax.div(seq, 2), lax.rem(seq, 2)
    z, y = lax.div(spot, SIDE), lax.rem(spot, SIDE)
    rows = first.shape[2]
    units = gate_ref.shape[1]
    chunks, _, _, slots, wide = parts.shape

    load = pltpu.make_async_copy(weights_hbm, weights, loaded)
    load.start()

    around = (
        (seq, wrapped(z + 1) * SIDE + y),
        (seq, wrapped(z - 1) * SIDE + y),
        (seq, z * SIDE + wrapped(y + 1)),
        (seq, z * SIDE + wrapped(y - 1)),
        (wrapped(x + 1) * 2 + core, spot),
        (wrapped(x - 1) * 2 + core, spot),
        (x * 2 + 1 - core, spot),
    )
    barrier = pltpu.get_barrier_semaphore()
    for neighbour in around:
        pl.semaphore_signal(barrier, inc=1, device_id=neighbour, device_id_type=MESH)
    pl.semaphore_wait(barrier, len(around))

    def place(stream):
        kind, half = stream // 2, stream % 2
        step = 1 - 2 * half
        along, across = (z, y) if kind == 0 else (y, z)
        if kind == 0:
            onward, sideways = around[half], around[2 + half]
        else:
            onward, sideways = around[2 + half], around[half]
        return kind, half, step, along, across, onward, sideways

    def own(stream, t, k):
        kind, half, step, along, across, _, _ = place(stream)
        far = wrapped(along - step * (1 + t))
        near = wrapped(across - step * (1 + k))
        zb, yb = (far, near) if kind == 0 else (near, far)
        at = pl.multiple_of((zb * SIDE + yb) * 2 * rows + half * rows, rows)
        return lax.dot_general(
            normed_ref[:, pl.ds(at, rows)],
            grads_ref[:, kind * units : (kind + 1) * units],
            (((0,), (0,)), ((), ())),
            preferred_element_type=jnp.float32,
        )

    def hop(stream, source, t, k):
        return pltpu.make_async_remote_copy(
            src_ref=source,
            dst_ref=arrived.at[stream, t, k],
            send_sem=put.at[stream, t, k],
            recv_sem=got.at[stream, t, k],
            device_id=place(stream)[5],
            device_id_type=MESH,
        )

    def hop2(stream, source, k):
        return pltpu.make_async_remote_copy(
            src_ref=source,
            dst_ref=crossed.at[stream, k],
            send_sem=put2.at[stream, k],
            recv_sem=got2.at[stream, k],
            device_id=place(stream)[6],
            device_id_type=MESH,
        )

    def across_cores(n):
        return pltpu.make_async_remote_copy(
            src_ref=parts.at[n, 1 - core],
            dst_ref=paired.at[n],
            send_sem=put3.at[n],
            recv_sem=got3.at[n],
            device_id=around[6],
            device_id_type=MESH,
        )

    def x_hop(side, n, source, t):
        return pltpu.make_async_remote_copy(
            src_ref=source,
            dst_ref=ringed.at[t, n],
            send_sem=put4.at[t, n],
            recv_sem=got4.at[t, n],
            device_id=around[4 + side],
            device_id_type=MESH,
        )

    def opening(k, carry):
        for stream in range(4):
            first[stream, k] = own(stream, 0, k).astype(jnp.bfloat16)
            hop(stream, first.at[stream, k], 0, k).start()
        return carry

    lax.fori_loop(0, SIDE, opening, 0)
    load.wait()

    def input_part(n):
        at = pl.multiple_of(n * wide, wide)
        value = lax.dot_general(
            grads_ref[...],
            weights[pl.ds(at, wide), :],
            (((1,), (1,)), ((), ())),
            preferred_element_type=jnp.float32,
        ).astype(jnp.bfloat16)
        for block in range(2 * SIDE):
            parts[n, block % 2, block // 2] = value[block * slots : (block + 1) * slots]
        across_cores(n).start()

    def middle(t, busy):
        def body(k, carry):
            for stream in range(4):
                value = own(stream, t, k)
                hop(stream, first.at[stream, k], t - 1, k).wait_recv()
                arrived[stream, t - 1, k] = (
                    value + arrived[stream, t - 1, k].astype(jnp.float32)
                ).astype(jnp.bfloat16)
                hop(stream, arrived.at[stream, t - 1, k], t, k).start()
            if busy:
                input_part(2 * k)
                input_part(2 * k + 1)
            return carry

        lax.fori_loop(0, SIDE, body, 0)

    def x_phase(t):
        def body(m, carry):
            for side in range(2):
                n = 2 * m + side
                block = wrapped(x - (1 - 2 * side) * (1 + t))
                if t == 0:
                    across_cores(n).wait_recv()
                    paired[n] = (
                        paired[n].astype(jnp.float32) + parts[n, core].astype(jnp.float32)
                    ).astype(jnp.bfloat16)
                    x_hop(side, n, paired.at[n, block], 0).start()
                else:
                    x_hop(side, n, paired.at[n, block], t - 1).wait_recv()
                    value = ringed[t - 1, n].astype(jnp.float32) + paired[n, block].astype(
                        jnp.float32
                    )
                    if t < SIDE - 1:
                        ringed[t - 1, n] = value.astype(jnp.bfloat16)
                        x_hop(side, n, ringed.at[t - 1, n], t).start()
                    else:
                        inward[n] = value
            return carry

        lax.fori_loop(0, chunks // 2, body, 0)

    last = SIDE - 1

    def total(stream, k):
        value = own(stream, last, k)
        hop(stream, first.at[stream, k], last - 1, k).wait_recv()
        return value + arrived[stream, last - 1, k].astype(jnp.float32)

    middle(1, True)
    x_phase(0)
    middle(2, False)
    x_phase(1)

    for stream in range(4):
        second[stream] = total(stream, 0).astype(jnp.bfloat16)
        hop2(stream, second.at[stream], 0).start()
    x_phase(2)

    def crossing(k, carry):
        for stream in range(4):
            value = total(stream, k)
            hop2(stream, second.at[stream], k - 1).wait_recv()
            crossed[stream, k - 1] = (
                value + crossed[stream, k - 1].astype(jnp.float32)
            ).astype(jnp.bfloat16)
            hop2(stream, crossed.at[stream, k - 1], k).start()
        return carry

    lax.fori_loop(1, last, crossing, 0)
    x_phase(3)

    def columns_of(n):
        at = pl.ds(pl.multiple_of(n * wide, wide), wide)
        return at, features_ref[:, at].astype(jnp.float32), gain_ref[:, at] * inward[n]

    def means(n, carry):
        _, features, scaled = columns_of(n)
        return (
            carry[0] + jnp.sum(features * features, axis=1, keepdims=True),
            carry[1] + jnp.sum(features * scaled, axis=1, keepdims=True),
        )

    nothing = jnp.zeros((slots, 1), jnp.float32)
    squares, products = lax.fori_loop(0, chunks, means, (nothing, nothing))
    inverse = lax.rsqrt(squares / (chunks * wide) + epsilon)
    factor = inverse * inverse * inverse * (products / (chunks * wide))

    def patch_part(n, carry):
        at, features, scaled = columns_of(n)
        patch_ref[:, at] = inverse * scaled - features * factor
        return carry

    lax.fori_loop(0, chunks, patch_part, 0)

    for stream in range(4):
        kind, half = stream // 2, stream % 2
        value = total(stream, last)
        hop2(stream, second.at[stream], last - 1).wait_recv()
        (gate_ref, up_ref)[kind][half * rows : (half + 1) * rows, :] = value + crossed[
            stream, last - 1
        ].astype(jnp.float32)

    def sent(index, carry):
        t, k = lax.div(index, SIDE), lax.rem(index, SIDE)
        for stream in range(4):
            hop(stream, first.at[stream, k], t, k).wait_send()
        return carry

    lax.fori_loop(0, last * SIDE, sent, 0)
    for stream in range(4):
        for k in range(last):
            hop2(stream, second.at[stream], k).wait_send()

    def x_sent(m, carry):
        for side in range(2):
            n = 2 * m + side
            across_cores(n).wait_send()
            for t in range(last):
                x_hop(side, n, ringed.at[0, n], t).wait_send()
        return carry

    lax.fori_loop(0, chunks // 2, x_sent, 0)


def grad_sums(normed, grads, features, gain, weights):
    tokens, width = normed.shape
    slots = features.shape[0]
    units = grads.shape[1] // 2
    rows = width // (SIDE * SIDE)
    half = rows // 2
    block = (half, units)
    chunks, wide = 8, width // 8
    whole = pl.BlockSpec(memory_space=pltpu.VMEM)
    return pl.pallas_call(
        grad_rings,
        out_shape=(
            jax.ShapeDtypeStruct((rows, units), jnp.float32),
            jax.ShapeDtypeStruct((rows, units), jnp.float32),
            jax.ShapeDtypeStruct((slots, width), jnp.float32),
        ),
        in_specs=[whole] * 4 + [pl.BlockSpec(memory_space=pl.ANY)],
        out_specs=(whole, whole, whole),
        scratch_shapes=[
            pltpu.VMEM((chunks, slots, wide), jnp.float32),
            pltpu.VMEM((4, SIDE, *block), jnp.bfloat16),
            pltpu.VMEM((4, SIDE - 1, SIDE, *block), jnp.bfloat16),
            pltpu.VMEM((4, *block), jnp.bfloat16),
            pltpu.VMEM((4, SIDE - 1, *block), jnp.bfloat16),
            pltpu.VMEM(weights.shape, jnp.bfloat16),
            pltpu.VMEM((chunks, 2, SIDE, slots, wide), jnp.bfloat16),
            pltpu.VMEM((chunks, SIDE, slots, wide), jnp.bfloat16),
            pltpu.VMEM((SIDE - 1, chunks, slots, wide), jnp.bfloat16),
            pltpu.SemaphoreType.DMA((4, SIDE - 1, SIDE)),
            pltpu.SemaphoreType.DMA((4, SIDE - 1, SIDE)),
            pltpu.SemaphoreType.DMA((4, SIDE - 1)),
            pltpu.SemaphoreType.DMA((4, SIDE - 1)),
            pltpu.SemaphoreType.DMA(()),
            pltpu.SemaphoreType.DMA((chunks,)),
            pltpu.SemaphoreType.DMA((chunks,)),
            pltpu.SemaphoreType.DMA((SIDE - 1, chunks)),
            pltpu.SemaphoreType.DMA((SIDE - 1, chunks)),
        ],
        compiler_params=pltpu.CompilerParams(
            collective_id=0, has_side_effects=True, vmem_limit_bytes=60 * 1024 * 1024
        ),
        cost_estimate=pl.CostEstimate(
            flops=4 * tokens * width * 2 * units,
            bytes_accessed=200_000_000,
            transcendentals=0,
        ),
        name="grad_rings",
    )(normed, grads, features, gain, weights)


ORDER = (
    "a0 b00",
    "A0 a1 b01",
    "B00 b10",
    "A1 a2 b02",
    "B01 b11",
    "A2 b03",
    "B10 b20",
    "B02 b12",
    "B11 b21",
    "B03 b13",
    "B12 b22",
    "B13 b23"
)


def front(
    states_ref,
    lengths_ref,
    offsets_ref,
    count_ref,
    gain_ref,
    cotangent_ref,
    gate_hbm,
    up_hbm,
    query_hbm,
    key_hbm,
    value_hbm,
    proj_hbm,
    weights_ref,
    normed_hbm,
    own_features_ref,
    hidden_ref,
    grads_ref,
    normed_ref,
    gates,
    ups,
    maps,
    crossed,
    sums,
    earlier,
    queries,
    keys,
    values,
    bias,
    mixed,
    pooled,
    contexts,
    loads,
    stores,
    put_a,
    got_a,
    put_b,
    got_b,
    put_s,
    got_s,
    put_x,
    got_x,
    put_c,
    got_c,
):
    seq = lax.axis_index("seq")
    spot = lax.axis_index("fsdp")
    x, core = lax.div(seq, 2), lax.rem(seq, 2)
    z, y = lax.div(spot, SIDE), lax.rem(spot, SIDE)
    groups, spots = 2 * SIDE, SIDE * SIDE
    devices = groups * spots
    length, width = states_ref.shape
    slots = offsets_ref.shape[1]
    heads = width // HEAD
    units = gate_hbm.shape[1]
    rows = gate_hbm.shape[0]
    model = proj_hbm.shape[1]
    ranges = (slice(0, 3 * HEAD), slice(3 * HEAD, units))

    def device_of(position):
        position = lax.rem(position + devices, devices)
        return lax.div(position, spots), lax.rem(position, spots)

    here = seq * spots + spot
    around = (
        (seq, wrapped(z + 1) * SIDE + y),
        (seq, wrapped(z - 1) * SIDE + y),
        (seq, z * SIDE + wrapped(y + 1)),
        (seq, z * SIDE + wrapped(y - 1)),
    )
    next_block = device_of(here + 1)
    after_next = device_of(here + 2)
    other_core = (x * 2 + 1 - core, spot)
    along_x = tuple((wrapped(x + by) * 2 + core, spot) for by in range(1, SIDE))

    places = [
        (gates.at[z, y], gate_hbm),
        (ups.at[y, z], up_hbm),
        (maps.at[:, 0:width], query_hbm),
        (maps.at[:, width : 2 * width], key_hbm),
        (maps.at[:, 2 * width : 3 * width], value_hbm),
        (maps, proj_hbm),
    ]
    load = [
        pltpu.make_async_copy(source, target, loads.at[i])
        for i, (target, source) in enumerate(places)
    ]
    for copy in load[:2]:
        copy.start()

    greeted = (
        *around,
        next_block,
        device_of(here - 1),
        other_core,
        *along_x,
    )
    barrier = pltpu.get_barrier_semaphore()
    for neighbour in greeted:
        pl.semaphore_signal(barrier, inc=1, device_id=neighbour, device_id_type=MESH)
    pl.semaphore_wait(barrier, len(greeted))

    def remote(source, target, sent, arrived, device):
        return pltpu.make_async_remote_copy(
            src_ref=source,
            dst_ref=target,
            send_sem=sent,
            recv_sem=arrived,
            device_id=device,
            device_id_type=MESH,
        )

    recent = earlier.at[length : 2 * length]
    oldest = earlier.at[0:length]
    to_next = remote(states_ref, recent, put_s.at[0], got_s.at[0], next_block)
    to_after = remote(recent, oldest, put_s.at[1], got_s.at[1], next_block)
    to_next.start()
    load[0].wait()
    load[1].wait()

    def place(stream, t):
        kind, half = stream // 2, stream % 2
        along = z if kind == 0 else y
        return (gates, ups)[kind], wrapped(along - (1 - 2 * half) * t), ranges[half]

    def piece(stream, t, k):
        kind, half = stream // 2, stream % 2
        across = y if kind == 0 else z
        buffer, far, columns = place(stream, t)
        return buffer.at[far, wrapped(across - (1 - 2 * half) * k), :, columns]

    def small(stream, k):
        kind, half = stream // 2, stream % 2
        device = around[2 + half] if kind == 0 else around[half]
        region = piece(stream, 0, k)
        return remote(region, region, put_a.at[stream, k], got_a.at[stream, k], device)

    def large(stream, t, k):
        kind, half = stream // 2, stream % 2
        device = around[half] if kind == 0 else around[2 + half]
        region = piece(stream, t, k)
        return remote(
            region, region, put_b.at[stream, t, k], got_b.at[stream, t, k], device
        )

    def store(stream, t):
        kind, half = stream // 2, stream % 2
        buffer, far, columns = place(stream, t)
        target = slice(kind * units + columns.start, kind * units + columns.stop)
        if kind == 0:
            target = weights_ref.at[far, :, :, target]
        else:
            target = weights_ref.at[:, far, :, target]
        return pltpu.make_async_copy(
            buffer.at[far, :, :, columns], target, stores.at[stream, t]
        )

    last = SIDE - 1

    steps = {
        "a": lambda stream, k: small(stream, k).start(),
        "A": lambda stream, k: small(stream, k).wait_recv(),
        "b": lambda stream, t, k: large(stream, t, k).start(),
        "B": lambda stream, t, k: large(stream, t, k).wait_recv(),
    }

    def tick(number):
        for stream in range(4):
            for step in ORDER[number].split():
                steps[step[0]](stream, *(int(digit) for digit in step[1:]))

    tick(0)
    for copy in load[2:5]:
        copy.start()

    chunk = 2 * HEAD
    scale = 1.0 / math.sqrt(HEAD)

    def dot(a, b):
        return jnp.dot(a, b, preferred_element_type=jnp.float32)

    def dot_t(a, b):
        return lax.dot_general(
            a, b, (((1,), (1,)), ((), ())), preferred_element_type=jnp.float32
        )

    load[2].wait()

    def make_queries(n, carry):
        at = pl.ds(pl.multiple_of(n * chunk, chunk), chunk)
        queries[:, at] = dot(states_ref[...], maps[:, at]).astype(jnp.bfloat16)
        return carry

    lax.fori_loop(0, width // chunk, make_queries, 0)
    tick(1)
    to_next.wait_recv()
    to_after.start()
    tick(2)
    load[3].wait()
    load[4].wait()

    def keys_and_values(source, row):
        def body(n, carry):
            at = pl.ds(pl.multiple_of(n * chunk, chunk), chunk)
            key_at = pl.ds(pl.multiple_of(width + n * chunk, chunk), chunk)
            value_at = pl.ds(pl.multiple_of(2 * width + n * chunk, chunk), chunk)
            into = slice(row, row + length)
            keys[into, at] = dot(source[...], maps[:, key_at]).astype(jnp.bfloat16)
            values[into, at] = dot(source[...], maps[:, value_at]).astype(jnp.bfloat16)
            return carry

        lax.fori_loop(0, width // chunk, body, 0)

    keys_and_values(states_ref, 2 * length)
    tick(3)

    span = WINDOW + HEAD
    parts = length // HEAD

    def iota(shape, dim):
        return lax.broadcasted_iota(jnp.int32, shape, dim)

    def turned(line, by):
        count = line.shape[1]
        picked = iota((count, count), 1) == iota((count, count), 0) + by
        return jnp.sum(jnp.where(picked, line, 0.0), axis=1, keepdims=True)

    docs = lengths_ref.shape[1]
    lengths = lengths_ref[...].astype(jnp.float32)
    earlier_docs = iota((docs, docs), 1) < iota((docs, docs), 0)
    start_column = jnp.sum(jnp.where(earlier_docs, lengths, 0.0), axis=1, keepdims=True)
    same = iota((docs, docs), 1) == iota((docs, docs), 0)
    start_line = jnp.sum(jnp.where(same, start_column, 0.0), axis=0, keepdims=True)
    key_pos = (here - 2) * length + iota((docs, 3 * length), 1)
    query_pos = here * length + iota((length, docs), 0)
    key_doc = jnp.sum(
        jnp.where(start_column <= key_pos.astype(jnp.float32), 1.0, 0.0), axis=0, keepdims=True
    )
    query_doc = jnp.sum(
        jnp.where(start_line <= query_pos.astype(jnp.float32), 1.0, 0.0), axis=1, keepdims=True
    )
    for r in range(parts):
        row = lax.broadcasted_iota(jnp.int32, (HEAD, span), 0)
        column = lax.broadcasted_iota(jnp.int32, (HEAD, span), 1)
        allowed = (column > row) & (column <= row + WINDOW)
        start = 2 * length - WINDOW + r * HEAD
        allowed = allowed & (
            key_doc[:, start : start + span] == query_doc[r * HEAD : (r + 1) * HEAD, :]
        )
        bias[r] = jnp.where(allowed, 0.0, masked_score)

    keys_and_values(recent, length)
    tick(4)
    tick(5)
    to_after.wait_recv()
    keys_and_values(oldest, 0)
    load[5].start()
    tick(6)

    def attend(h, carry):
        at = pl.ds(pl.multiple_of(h * HEAD, HEAD), HEAD)
        for r in range(parts):
            here_rows = slice(r * HEAD, (r + 1) * HEAD)
            start = 2 * length - WINDOW + r * HEAD
            scores = dot_t(queries[here_rows, at], keys[start : start + span, at])
            scores = scores * scale + bias[r]
            weights = jnp.exp(scores - jnp.max(scores, axis=1, keepdims=True))
            total = jnp.sum(weights, axis=1, keepdims=True)
            summed = dot(weights.astype(jnp.bfloat16), values[start : start + span, at])
            mixed[here_rows, at] = (
                states_ref[here_rows, at].astype(jnp.float32) + summed / total
            ).astype(jnp.bfloat16)
        return carry

    lax.fori_loop(0, heads // 2, attend, 0)
    tick(7)
    lax.fori_loop(heads // 2, heads, attend, 0)
    tick(8)
    tick(9)

    offsets = offsets_ref[...].astype(jnp.float32)
    count = count_ref[...].astype(jnp.float32)
    slot = iota((slots, 1), 0).astype(jnp.float32)
    present = slot < count
    begins = turned(offsets, 0)
    ends = jnp.where((slot == count - 1.0) | (slot == slots - 1.0), 1.0 * length, turned(offsets, 1))
    begins, ends = jnp.where(present, begins, 0.0), jnp.where(present, ends, 0.0)
    byte = iota((slots, length), 1).astype(jnp.float32)
    member = (byte >= begins) & (byte < ends)
    ones = jnp.where(member, 1.0, 0.0)
    pool_bias = jnp.where(member, 0.0, masked_score)
    sizes = jnp.maximum(jnp.sum(ones, axis=1, keepdims=True), 1.0)
    pooled[...] = (dot(ones.astype(jnp.bfloat16), mixed[...]) / sizes).astype(jnp.bfloat16)
    mine = pl.ds(pl.multiple_of(seq * slots, slots), slots)

    def pool(h, carry):
        at = pl.ds(pl.multiple_of(h * HEAD, HEAD), HEAD)
        scores = dot_t(pooled[:, at], mixed[:, at]) * scale + pool_bias
        weights = jnp.exp(scores - jnp.max(scores, axis=1, keepdims=True))
        total = jnp.sum(weights, axis=1, keepdims=True)
        summed = dot(weights.astype(jnp.bfloat16), mixed[:, at]) / total
        contexts[mine, at] = jnp.where(present, summed, 0.0).astype(jnp.bfloat16)
        return carry

    lax.fori_loop(0, heads, pool, 0)

    def context_of(group):
        return contexts.at[pl.ds(pl.multiple_of(group * slots, slots), slots)]

    def x_send(by):
        region = context_of(seq)
        return remote(region, region, put_x.at[by - 1], got_x.at[by - 1], along_x[by - 1])

    def core_send(by):
        region = context_of(wrapped(x - by) * 2 + core)
        return remote(region, region, put_c.at[by], got_c.at[by], other_core)

    for by in range(1, SIDE):
        x_send(by).start()
    core_send(0).start()
    tick(10)
    for by in (1, 3, 2):
        x_send(by).wait_recv()
        core_send(by).start()
    for by in range(SIDE):
        core_send(by).wait_recv()
    load[5].wait()

    wide = 4 * HEAD

    def project(n, squares):
        at = pl.ds(pl.multiple_of(n * wide, wide), wide)
        features = dot(contexts[...], maps[:, at]).astype(jnp.bfloat16)
        normed_ref[:, at] = features
        full = features.astype(jnp.float32)
        return squares + jnp.sum(full * full, axis=1, keepdims=True)

    squares = jnp.zeros((groups * slots, 1), jnp.float32)
    squares = lax.fori_loop(0, model // wide // 2, project, squares)
    tick(11)
    squares = lax.fori_loop(model // wide // 2, model // wide, project, squares)
    inverse = lax.rsqrt(squares / model + epsilon)
    own_features_ref[...] = normed_ref[mine, :]

    def normalize(n, carry):
        at = pl.ds(pl.multiple_of(n * rows, rows), rows)
        place_turned = (n % SIDE) * SIDE + n // SIDE
        value = (normed_ref[:, at].astype(jnp.float32) * inverse * gain_ref[:, at]).astype(
            jnp.bfloat16
        )
        normed_ref[:, at] = value
        crossed[:, pl.ds(pl.multiple_of(place_turned * rows, rows), rows)] = value
        return carry

    lax.fori_loop(0, model // rows, normalize, 0)
    keep = pltpu.make_async_copy(normed_ref, normed_hbm, loads.at[6])
    keep.start()
    sums[...] = jnp.zeros_like(sums)

    def accumulate(t, carry):
        @pl.when(t == last)
        def _():
            for stream in range(4):
                for k in range(SIDE):
                    large(stream, last - 1, k).wait_recv()

        for stream in range(4):
            store(stream, t).start()
            buffer, far, columns = place(stream, t)
            kind, count = stream // 2, columns.stop - columns.start
            deep = SIDE * rows
            at = pl.ds(pl.multiple_of(far * deep, deep), deep)
            block = buffer[far, :, :, columns].reshape(deep, count)
            sums[kind, :, columns] += dot((normed_ref, crossed)[kind][:, at], block)
        return carry

    lax.fori_loop(0, SIDE, accumulate, 0)

    def gating(n, carry):
        at = pl.ds(pl.multiple_of(n * slots, slots), slots)
        gate_pre, up_pre = sums[0, at], sums[1, at]
        sigmoid_gate = jax.nn.sigmoid(gate_pre)
        swish = gate_pre * sigmoid_gate
        cotangent = cotangent_ref[at, :].astype(jnp.float32)
        hidden_ref[at, :] = (swish * up_pre).astype(jnp.bfloat16)
        grads_ref[at, 0:units] = (
            cotangent * up_pre * sigmoid_gate * (1.0 + gate_pre * (1.0 - sigmoid_gate))
        ).astype(jnp.bfloat16)
        grads_ref[at, units : 2 * units] = (cotangent * swish).astype(jnp.bfloat16)
        return carry

    lax.fori_loop(0, groups, gating, 0)

    to_next.wait_send()
    to_after.wait_send()
    keep.wait()
    for stream in range(4):
        for k in range(SIDE):
            if k < last:
                small(stream, k).wait_send()
            for t in range(last):
                large(stream, t, k).wait_send()
            store(stream, k).wait()
    for by in range(SIDE):
        if by > 0:
            x_send(by).wait_send()
        core_send(by).wait_send()


def front_part(
    states, lengths, offsets, count, gain, cotangent, gate_w, up_w, squares, w_proj
):
    length, width = states.shape
    slots = offsets.shape[1]
    rows, units = gate_w.shape
    model = w_proj.shape[1]
    tokens = 2 * SIDE * slots
    dma = pltpu.SemaphoreType.DMA
    whole = pl.BlockSpec(memory_space=pltpu.VMEM)
    anywhere = pl.BlockSpec(memory_space=pl.ANY)
    half = jnp.bfloat16
    return pl.pallas_call(
        front,
        out_shape=(
            jax.ShapeDtypeStruct((SIDE, SIDE, rows, 2 * units), half),
            jax.ShapeDtypeStruct((tokens, model), half),
            jax.ShapeDtypeStruct((slots, model), half),
            jax.ShapeDtypeStruct((tokens, units), half),
            jax.ShapeDtypeStruct((tokens, 2 * units), half),
        ),
        in_specs=[whole] * 6 + [anywhere] * 6,
        out_specs=(anywhere, anywhere, whole, whole, whole),
        scratch_shapes=[
            pltpu.VMEM((tokens, model), half),
            pltpu.VMEM((SIDE, SIDE, rows, units), half),
            pltpu.VMEM((SIDE, SIDE, rows, units), half),
            pltpu.VMEM((width, model), half),
            pltpu.VMEM((tokens, model), half),
            pltpu.VMEM((2, tokens, units), jnp.float32),
            pltpu.VMEM((2 * length, width), half),
            pltpu.VMEM((length, width), half),
            pltpu.VMEM((3 * length, width), half),
            pltpu.VMEM((3 * length, width), half),
            pltpu.VMEM((length // HEAD, HEAD, WINDOW + HEAD), jnp.float32),
            pltpu.VMEM((length, width), half),
            pltpu.VMEM((slots, width), half),
            pltpu.VMEM((tokens, width), half),
            dma((7,)),
            dma((4, SIDE)),
            dma((4, SIDE - 1)),
            dma((4, SIDE - 1)),
            dma((4, SIDE - 1, SIDE)),
            dma((4, SIDE - 1, SIDE)),
            dma((2,)),
            dma((2,)),
            dma((SIDE - 1,)),
            dma((SIDE - 1,)),
            dma((SIDE,)),
            dma((SIDE,)),
        ],
        compiler_params=pltpu.CompilerParams(
            collective_id=1, has_side_effects=True, vmem_limit_bytes=62 * 1024 * 1024
        ),
        name="front",
    )(states, lengths, offsets, count, gain, cotangent, gate_w, up_w, *squares, w_proj)


def shards(
    bytes_in,
    doc_lengths,
    patch_offsets,
    patch_counts,
    w_query,
    w_key,
    w_value,
    w_proj,
    norm_gain,
    gate_w,
    up_w,
    d_hidden,
):
    units = gate_w.shape[1]
    weights, normed, own_features, hidden, both_grads = front_part(
        bytes_in[0],
        doc_lengths[None],
        patch_offsets,
        patch_counts,
        norm_gain[None],
        d_hidden.reshape(-1, units),
        gate_w,
        up_w,
        (w_query, w_key, w_value),
        w_proj,
    )
    model_width = normed.shape[1]
    grad_gate, grad_up, patch_grad = grad_sums(
        normed,
        both_grads,
        own_features,
        norm_gain[None],
        weights.reshape(model_width, 2 * units),
    )
    return (hidden.reshape(d_hidden.shape), grad_gate, grad_up, patch_grad[None])


def solution(mesh):
    return jax.shard_map(
        shards,
        mesh=mesh,
        in_specs=(
            P("seq", "fsdp", None),
            P(),
            P("seq", "fsdp"),
            P("seq", "fsdp"),
            P(),
            P(),
            P(),
            P(),
            P(),
            P("fsdp", "seq"),
            P("fsdp", "seq"),
            P(None, "fsdp", "seq"),
        ),
        out_specs=(
            P(None, "fsdp", "seq"),
            P("fsdp", "seq"),
            P("fsdp", "seq"),
            P("seq", "fsdp", None),
        ),
        check_vma=False,
    )
```

```python
import math

import jax
import jax.numpy as jnp
from jax import lax
from jax.experimental import pallas as pl
from jax.experimental.pallas import tpu as pltpu
from jax.sharding import PartitionSpec as P

HEAD = 128
WINDOW = 512


epsilon = 1e-05
masked_score = -1e30


MESH = pl.DeviceIdType.MESH
SIDE = 4


def wrapped(value):
    return lax.rem(value + 2 * SIDE, SIDE)


def grad_rings(
    normed_ref,
    grads_ref,
    features_ref,
    gain_ref,
    gates,
    ups,
    gate_ref,
    up_ref,
    patch_ref,
    inward,
    first,
    arrived,
    second,
    crossed,
    parts,
    paired,
    ringed,
    put,
    got,
    put2,
    got2,
    put3,
    got3,
    put4,
    got4,
    ready,
):
    seq = lax.axis_index("seq")
    spot = lax.axis_index("fsdp")
    x, core = lax.div(seq, 2), lax.rem(seq, 2)
    z, y = lax.div(spot, SIDE), lax.rem(spot, SIDE)
    rows = first.shape[2]
    units = gate_ref.shape[1]
    chunks, _, _, slots, wide = parts.shape

    around = (
        (seq, wrapped(z + 1) * SIDE + y),
        (seq, wrapped(z - 1) * SIDE + y),
        (seq, z * SIDE + wrapped(y + 1)),
        (seq, z * SIDE + wrapped(y - 1)),
        (wrapped(x + 1) * 2 + core, spot),
        (wrapped(x - 1) * 2 + core, spot),
        (x * 2 + 1 - core, spot),
    )
    for neighbour in around:
        pl.semaphore_signal(ready, inc=1, device_id=neighbour, device_id_type=MESH)
    pl.semaphore_wait(ready, len(around))

    def place(stream):
        kind, half = stream // 2, stream % 2
        step = 1 - 2 * half
        along, across = (z, y) if kind == 0 else (y, z)
        if kind == 0:
            onward, sideways = around[half], around[2 + half]
        else:
            onward, sideways = around[2 + half], around[half]
        return kind, half, step, along, across, onward, sideways

    def own(stream, t, k):
        kind, half, step, along, across, _, _ = place(stream)
        far = wrapped(along - step * (1 + t))
        near = wrapped(across - step * (1 + k))
        zb, yb = (far, near) if kind == 0 else (near, far)
        at = pl.multiple_of((zb * SIDE + yb) * 2 * rows + half * rows, rows)
        return lax.dot_general(
            normed_ref[:, pl.ds(at, rows)],
            grads_ref[:, kind * units : (kind + 1) * units],
            (((0,), (0,)), ((), ())),
            preferred_element_type=jnp.float32,
        )

    def hop(stream, source, t, k):
        return pltpu.make_async_remote_copy(
            src_ref=source,
            dst_ref=arrived.at[stream, t, k],
            send_sem=put.at[stream, t, k],
            recv_sem=got.at[stream, t, k],
            device_id=place(stream)[5],
            device_id_type=MESH,
        )

    def hop2(stream, source, k):
        return pltpu.make_async_remote_copy(
            src_ref=source,
            dst_ref=crossed.at[stream, k],
            send_sem=put2.at[stream, k],
            recv_sem=got2.at[stream, k],
            device_id=place(stream)[6],
            device_id_type=MESH,
        )

    def across_cores(n):
        return pltpu.make_async_remote_copy(
            src_ref=parts.at[n, 1 - core],
            dst_ref=paired.at[n],
            send_sem=put3.at[n],
            recv_sem=got3.at[n],
            device_id=around[6],
            device_id_type=MESH,
        )

    def x_hop(side, n, source, t):
        return pltpu.make_async_remote_copy(
            src_ref=source,
            dst_ref=ringed.at[t, n],
            send_sem=put4.at[t, n],
            recv_sem=got4.at[t, n],
            device_id=around[4 + side],
            device_id_type=MESH,
        )

    def opening(k, carry):
        for stream in range(4):
            first[stream, k] = own(stream, 0, k).astype(jnp.bfloat16)
            hop(stream, first.at[stream, k], 0, k).start()
        return carry

    lax.fori_loop(0, SIDE, opening, 0)

    def input_part(n):
        depth = 2 * rows
        for column in range(wide // depth):
            zb, yb = lax.div(n, 2), 2 * lax.rem(n, 2) + column
            value = 0.0
            for kind, block in enumerate((gates[zb, yb], ups[yb, zb])):
                value += lax.dot_general(
                    grads_ref[:, kind * units : (kind + 1) * units],
                    block,
                    (((1,), (1,)), ((), ())),
                    preferred_element_type=jnp.float32,
                )
            value = value.astype(jnp.bfloat16)
            for block in range(2 * SIDE):
                parts[n, block % 2, block // 2, :, column * depth : (column + 1) * depth] = (
                    value[block * slots : (block + 1) * slots]
                )
        across_cores(n).start()

    def middle(t, busy):
        def body(k, carry):
            for stream in range(4):
                value = own(stream, t, k)
                hop(stream, first.at[stream, k], t - 1, k).wait_recv()
                arrived[stream, t - 1, k] = (
                    value + arrived[stream, t - 1, k].astype(jnp.float32)
                ).astype(jnp.bfloat16)
                hop(stream, arrived.at[stream, t - 1, k], t, k).start()
            if busy:
                input_part(2 * k)
                input_part(2 * k + 1)
            return carry

        lax.fori_loop(0, SIDE, body, 0)

    def x_phase(t):
        def body(m, carry):
            for side in range(2):
                n = 2 * m + side
                block = wrapped(x - (1 - 2 * side) * (1 + t))
                if t == 0:
                    across_cores(n).wait_recv()
                    paired[n] = (
                        paired[n].astype(jnp.float32) + parts[n, core].astype(jnp.float32)
                    ).astype(jnp.bfloat16)
                    x_hop(side, n, paired.at[n, block], 0).start()
                else:
                    x_hop(side, n, paired.at[n, block], t - 1).wait_recv()
                    value = ringed[t - 1, n].astype(jnp.float32) + paired[n, block].astype(
                        jnp.float32
                    )
                    if t < SIDE - 1:
                        ringed[t - 1, n] = value.astype(jnp.bfloat16)
                        x_hop(side, n, ringed.at[t - 1, n], t).start()
                    else:
                        inward[n] = value
            return carry

        lax.fori_loop(0, chunks // 2, body, 0)

    last = SIDE - 1

    def total(stream, k):
        value = own(stream, last, k)
        hop(stream, first.at[stream, k], last - 1, k).wait_recv()
        return value + arrived[stream, last - 1, k].astype(jnp.float32)

    middle(1, True)
    x_phase(0)
    middle(2, False)
    x_phase(1)

    for stream in range(4):
        second[stream] = total(stream, 0).astype(jnp.bfloat16)
        hop2(stream, second.at[stream], 0).start()
    x_phase(2)

    def crossing(k, carry):
        for stream in range(4):
            value = total(stream, k)
            hop2(stream, second.at[stream], k - 1).wait_recv()
            crossed[stream, k - 1] = (
                value + crossed[stream, k - 1].astype(jnp.float32)
            ).astype(jnp.bfloat16)
            hop2(stream, crossed.at[stream, k - 1], k).start()
        return carry

    lax.fori_loop(1, last, crossing, 0)
    x_phase(3)

    def columns_of(n):
        at = pl.ds(pl.multiple_of(n * wide, wide), wide)
        return at, features_ref[:, at].astype(jnp.float32), gain_ref[:, at] * inward[n]

    def means(n, carry):
        _, features, scaled = columns_of(n)
        return (
            carry[0] + jnp.sum(features * features, axis=1, keepdims=True),
            carry[1] + jnp.sum(features * scaled, axis=1, keepdims=True),
        )

    nothing = jnp.zeros((slots, 1), jnp.float32)
    squares, products = lax.fori_loop(0, chunks, means, (nothing, nothing))
    inverse = lax.rsqrt(squares / (chunks * wide) + epsilon)
    factor = inverse * inverse * inverse * (products / (chunks * wide))

    def patch_part(n, carry):
        at, features, scaled = columns_of(n)
        patch_ref[:, at] = inverse * scaled - features * factor
        return carry

    lax.fori_loop(0, chunks, patch_part, 0)

    for stream in range(4):
        kind, half = stream // 2, stream % 2
        value = total(stream, last)
        hop2(stream, second.at[stream], last - 1).wait_recv()
        (gate_ref, up_ref)[kind][half * rows : (half + 1) * rows, :] = value + crossed[
            stream, last - 1
        ].astype(jnp.float32)

    def sent(index, carry):
        t, k = lax.div(index, SIDE), lax.rem(index, SIDE)
        for stream in range(4):
            hop(stream, first.at[stream, k], t, k).wait_send()
        return carry

    lax.fori_loop(0, last * SIDE, sent, 0)
    for stream in range(4):
        for k in range(last):
            hop2(stream, second.at[stream], k).wait_send()

    def x_sent(m, carry):
        for side in range(2):
            n = 2 * m + side
            across_cores(n).wait_send()
            for t in range(last):
                x_hop(side, n, ringed.at[0, n], t).wait_send()
        return carry

    lax.fori_loop(0, chunks // 2, x_sent, 0)


ORDER = (
    "a0 b00",
    "A0 a1 b01",
    "B00 b10",
    "A1 a2 b02",
    "B01 b11",
    "A2 b03",
    "B10 b20",
    "B02 b12",
    "B11 b21",
    "B03 b13",
    "B12 b22",
    "B13 b23"
)


def front(
    states_ref,
    lengths_ref,
    offsets_ref,
    count_ref,
    gain_ref,
    cotangent_ref,
    gate_hbm,
    up_hbm,
    query_hbm,
    key_hbm,
    value_hbm,
    proj_hbm,
    own_features_ref,
    hidden_ref,
    grads_ref,
    normed_ref,
    gates,
    ups,
    maps,
    crossed,
    sums,
    earlier,
    queries,
    keys,
    values,
    bias,
    mixed,
    pooled,
    contexts,
    loads,
    put_a,
    got_a,
    put_b,
    got_b,
    put_s,
    got_s,
    put_x,
    got_x,
    put_c,
    got_c,
):
    seq = lax.axis_index("seq")
    spot = lax.axis_index("fsdp")
    x, core = lax.div(seq, 2), lax.rem(seq, 2)
    z, y = lax.div(spot, SIDE), lax.rem(spot, SIDE)
    groups, spots = 2 * SIDE, SIDE * SIDE
    devices = groups * spots
    length, width = states_ref.shape
    slots = offsets_ref.shape[1]
    heads = width // HEAD
    units = gate_hbm.shape[1]
    rows = gate_hbm.shape[0]
    model = proj_hbm.shape[1]
    ranges = (slice(0, 3 * HEAD), slice(3 * HEAD, units))

    def device_of(position):
        position = lax.rem(position + devices, devices)
        return lax.div(position, spots), lax.rem(position, spots)

    here = seq * spots + spot
    around = (
        (seq, wrapped(z + 1) * SIDE + y),
        (seq, wrapped(z - 1) * SIDE + y),
        (seq, z * SIDE + wrapped(y + 1)),
        (seq, z * SIDE + wrapped(y - 1)),
    )
    next_block = device_of(here + 1)
    after_next = device_of(here + 2)
    other_core = (x * 2 + 1 - core, spot)
    along_x = tuple((wrapped(x + by) * 2 + core, spot) for by in range(1, SIDE))

    places = [
        (gates.at[z, y], gate_hbm),
        (ups.at[y, z], up_hbm),
        (maps.at[:, 0:width], query_hbm),
        (maps.at[:, width : 2 * width], key_hbm),
        (maps.at[:, 2 * width : 3 * width], value_hbm),
        (maps, proj_hbm),
    ]
    load = [
        pltpu.make_async_copy(source, target, loads.at[i])
        for i, (target, source) in enumerate(places)
    ]
    for copy in load[:2]:
        copy.start()

    greeted = (
        *around,
        next_block,
        device_of(here - 1),
        other_core,
        *along_x,
    )
    barrier = pltpu.get_barrier_semaphore()
    for neighbour in greeted:
        pl.semaphore_signal(barrier, inc=1, device_id=neighbour, device_id_type=MESH)
    pl.semaphore_wait(barrier, len(greeted))

    def remote(source, target, sent, arrived, device):
        return pltpu.make_async_remote_copy(
            src_ref=source,
            dst_ref=target,
            send_sem=sent,
            recv_sem=arrived,
            device_id=device,
            device_id_type=MESH,
        )

    recent = earlier.at[length : 2 * length]
    oldest = earlier.at[0:length]
    to_next = remote(states_ref, recent, put_s.at[0], got_s.at[0], next_block)
    to_after = remote(recent, oldest, put_s.at[1], got_s.at[1], next_block)
    to_next.start()
    load[0].wait()
    load[1].wait()

    def place(stream, t):
        kind, half = stream // 2, stream % 2
        along = z if kind == 0 else y
        return (gates, ups)[kind], wrapped(along - (1 - 2 * half) * t), ranges[half]

    def piece(stream, t, k):
        kind, half = stream // 2, stream % 2
        across = y if kind == 0 else z
        buffer, far, columns = place(stream, t)
        return buffer.at[far, wrapped(across - (1 - 2 * half) * k), :, columns]

    def small(stream, k):
        kind, half = stream // 2, stream % 2
        device = around[2 + half] if kind == 0 else around[half]
        region = piece(stream, 0, k)
        return remote(region, region, put_a.at[stream, k], got_a.at[stream, k], device)

    def large(stream, t, k):
        kind, half = stream // 2, stream % 2
        device = around[half] if kind == 0 else around[2 + half]
        region = piece(stream, t, k)
        return remote(
            region, region, put_b.at[stream, t, k], got_b.at[stream, t, k], device
        )

    last = SIDE - 1

    steps = {
        "a": lambda stream, k: small(stream, k).start(),
        "A": lambda stream, k: small(stream, k).wait_recv(),
        "b": lambda stream, t, k: large(stream, t, k).start(),
        "B": lambda stream, t, k: large(stream, t, k).wait_recv(),
    }

    def tick(number):
        for stream in range(4):
            for step in ORDER[number].split():
                steps[step[0]](stream, *(int(digit) for digit in step[1:]))

    tick(0)
    for copy in load[2:5]:
        copy.start()

    chunk = 2 * HEAD
    scale = 1.0 / math.sqrt(HEAD)

    def dot(a, b):
        return jnp.dot(a, b, preferred_element_type=jnp.float32)

    def dot_t(a, b):
        return lax.dot_general(
            a, b, (((1,), (1,)), ((), ())), preferred_element_type=jnp.float32
        )

    load[2].wait()

    def make_queries(n, carry):
        at = pl.ds(pl.multiple_of(n * chunk, chunk), chunk)
        queries[:, at] = dot(states_ref[...], maps[:, at]).astype(jnp.bfloat16)
        return carry

    lax.fori_loop(0, width // chunk, make_queries, 0)
    tick(1)
    to_next.wait_recv()
    to_after.start()
    tick(2)
    load[3].wait()
    load[4].wait()

    def keys_and_values(source, row):
        def body(n, carry):
            at = pl.ds(pl.multiple_of(n * chunk, chunk), chunk)
            key_at = pl.ds(pl.multiple_of(width + n * chunk, chunk), chunk)
            value_at = pl.ds(pl.multiple_of(2 * width + n * chunk, chunk), chunk)
            into = slice(row, row + length)
            keys[into, at] = dot(source[...], maps[:, key_at]).astype(jnp.bfloat16)
            values[into, at] = dot(source[...], maps[:, value_at]).astype(jnp.bfloat16)
            return carry

        lax.fori_loop(0, width // chunk, body, 0)

    keys_and_values(states_ref, 2 * length)
    tick(3)

    span = WINDOW + HEAD
    parts = length // HEAD

    def iota(shape, dim):
        return lax.broadcasted_iota(jnp.int32, shape, dim)

    def turned(line, by):
        count = line.shape[1]
        picked = iota((count, count), 1) == iota((count, count), 0) + by
        return jnp.sum(jnp.where(picked, line, 0.0), axis=1, keepdims=True)

    docs = lengths_ref.shape[1]
    lengths = lengths_ref[...].astype(jnp.float32)
    earlier_docs = iota((docs, docs), 1) < iota((docs, docs), 0)
    start_column = jnp.sum(jnp.where(earlier_docs, lengths, 0.0), axis=1, keepdims=True)
    same = iota((docs, docs), 1) == iota((docs, docs), 0)
    start_line = jnp.sum(jnp.where(same, start_column, 0.0), axis=0, keepdims=True)
    key_pos = (here - 2) * length + iota((docs, 3 * length), 1)
    query_pos = here * length + iota((length, docs), 0)
    key_doc = jnp.sum(
        jnp.where(start_column <= key_pos.astype(jnp.float32), 1.0, 0.0), axis=0, keepdims=True
    )
    query_doc = jnp.sum(
        jnp.where(start_line <= query_pos.astype(jnp.float32), 1.0, 0.0), axis=1, keepdims=True
    )
    for r in range(parts):
        row = lax.broadcasted_iota(jnp.int32, (HEAD, span), 0)
        column = lax.broadcasted_iota(jnp.int32, (HEAD, span), 1)
        allowed = (column > row) & (column <= row + WINDOW)
        start = 2 * length - WINDOW + r * HEAD
        allowed = allowed & (
            key_doc[:, start : start + span] == query_doc[r * HEAD : (r + 1) * HEAD, :]
        )
        bias[r] = jnp.where(allowed, 0.0, masked_score)

    keys_and_values(recent, length)
    tick(4)
    tick(5)
    to_after.wait_recv()
    keys_and_values(oldest, 0)
    load[5].start()
    tick(6)

    def attend(h, carry):
        at = pl.ds(pl.multiple_of(h * HEAD, HEAD), HEAD)
        for r in range(parts):
            here_rows = slice(r * HEAD, (r + 1) * HEAD)
            start = 2 * length - WINDOW + r * HEAD
            scores = dot_t(queries[here_rows, at], keys[start : start + span, at])
            scores = scores * scale + bias[r]
            weights = jnp.exp(scores - jnp.max(scores, axis=1, keepdims=True))
            total = jnp.sum(weights, axis=1, keepdims=True)
            summed = dot(weights.astype(jnp.bfloat16), values[start : start + span, at])
            mixed[here_rows, at] = (
                states_ref[here_rows, at].astype(jnp.float32) + summed / total
            ).astype(jnp.bfloat16)
        return carry

    lax.fori_loop(0, heads // 2, attend, 0)
    tick(7)
    lax.fori_loop(heads // 2, heads, attend, 0)
    tick(8)
    tick(9)

    offsets = offsets_ref[...].astype(jnp.float32)
    count = count_ref[...].astype(jnp.float32)
    slot = iota((slots, 1), 0).astype(jnp.float32)
    present = slot < count
    begins = turned(offsets, 0)
    ends = jnp.where((slot == count - 1.0) | (slot == slots - 1.0), 1.0 * length, turned(offsets, 1))
    begins, ends = jnp.where(present, begins, 0.0), jnp.where(present, ends, 0.0)
    byte = iota((slots, length), 1).astype(jnp.float32)
    member = (byte >= begins) & (byte < ends)
    ones = jnp.where(member, 1.0, 0.0)
    pool_bias = jnp.where(member, 0.0, masked_score)
    sizes = jnp.maximum(jnp.sum(ones, axis=1, keepdims=True), 1.0)
    pooled[...] = (dot(ones.astype(jnp.bfloat16), mixed[...]) / sizes).astype(jnp.bfloat16)
    mine = pl.ds(pl.multiple_of(seq * slots, slots), slots)

    def pool(h, carry):
        at = pl.ds(pl.multiple_of(h * HEAD, HEAD), HEAD)
        scores = dot_t(pooled[:, at], mixed[:, at]) * scale + pool_bias
        weights = jnp.exp(scores - jnp.max(scores, axis=1, keepdims=True))
        total = jnp.sum(weights, axis=1, keepdims=True)
        summed = dot(weights.astype(jnp.bfloat16), mixed[:, at]) / total
        contexts[mine, at] = jnp.where(present, summed, 0.0).astype(jnp.bfloat16)
        return carry

    lax.fori_loop(0, heads, pool, 0)

    def context_of(group):
        return contexts.at[pl.ds(pl.multiple_of(group * slots, slots), slots)]

    def x_send(by):
        region = context_of(seq)
        return remote(region, region, put_x.at[by - 1], got_x.at[by - 1], along_x[by - 1])

    def core_send(by):
        region = context_of(wrapped(x - by) * 2 + core)
        return remote(region, region, put_c.at[by], got_c.at[by], other_core)

    for by in range(1, SIDE):
        x_send(by).start()
    core_send(0).start()
    tick(10)
    for by in (1, 3, 2):
        x_send(by).wait_recv()
        core_send(by).start()
    for by in range(SIDE):
        core_send(by).wait_recv()
    load[5].wait()

    wide = 4 * HEAD

    def project(n, squares):
        at = pl.ds(pl.multiple_of(n * wide, wide), wide)
        features = dot(contexts[...], maps[:, at]).astype(jnp.bfloat16)
        normed_ref[:, at] = features
        full = features.astype(jnp.float32)
        return squares + jnp.sum(full * full, axis=1, keepdims=True)

    squares = jnp.zeros((groups * slots, 1), jnp.float32)
    squares = lax.fori_loop(0, model // wide // 2, project, squares)
    tick(11)
    squares = lax.fori_loop(model // wide // 2, model // wide, project, squares)
    inverse = lax.rsqrt(squares / model + epsilon)
    own_features_ref[...] = normed_ref[mine, :]

    def normalize(n, carry):
        at = pl.ds(pl.multiple_of(n * rows, rows), rows)
        place_turned = (n % SIDE) * SIDE + n // SIDE
        value = (normed_ref[:, at].astype(jnp.float32) * inverse * gain_ref[:, at]).astype(
            jnp.bfloat16
        )
        normed_ref[:, at] = value
        crossed[:, pl.ds(pl.multiple_of(place_turned * rows, rows), rows)] = value
        return carry

    lax.fori_loop(0, model // rows, normalize, 0)
    sums[...] = jnp.zeros_like(sums)

    def accumulate(t, carry):
        @pl.when(t == last)
        def _():
            for stream in range(4):
                for k in range(SIDE):
                    large(stream, last - 1, k).wait_recv()

        for stream in range(4):
            buffer, far, columns = place(stream, t)
            kind, count = stream // 2, columns.stop - columns.start
            deep = SIDE * rows
            at = pl.ds(pl.multiple_of(far * deep, deep), deep)
            block = buffer[far, :, :, columns].reshape(deep, count)
            sums[kind, :, columns] += dot((normed_ref, crossed)[kind][:, at], block)
        return carry

    lax.fori_loop(0, SIDE, accumulate, 0)

    def gating(n, carry):
        at = pl.ds(pl.multiple_of(n * slots, slots), slots)
        gate_pre, up_pre = sums[0, at], sums[1, at]
        sigmoid_gate = jax.nn.sigmoid(gate_pre)
        swish = gate_pre * sigmoid_gate
        cotangent = cotangent_ref[at, :].astype(jnp.float32)
        hidden_ref[at, :] = (swish * up_pre).astype(jnp.bfloat16)
        grads_ref[at, 0:units] = (
            cotangent * up_pre * sigmoid_gate * (1.0 + gate_pre * (1.0 - sigmoid_gate))
        ).astype(jnp.bfloat16)
        grads_ref[at, units : 2 * units] = (cotangent * swish).astype(jnp.bfloat16)
        return carry

    lax.fori_loop(0, groups, gating, 0)

    to_next.wait_send()
    to_after.wait_send()
    for stream in range(4):
        for k in range(SIDE):
            if k < last:
                small(stream, k).wait_send()
            for t in range(last):
                large(stream, t, k).wait_send()
    for by in range(SIDE):
        if by > 0:
            x_send(by).wait_send()
        core_send(by).wait_send()


def layer(
    states_ref,
    lengths_ref,
    offsets_ref,
    count_ref,
    gain_ref,
    cotangent_ref,
    gate_hbm,
    up_hbm,
    query_hbm,
    key_hbm,
    value_hbm,
    proj_hbm,
    hidden_ref,
    gate_ref,
    up_ref,
    patch_ref,
    own_features,
    grads,
    normed,
    gates,
    ups,
    earlier,
    contexts,
    *semaphores,
):
    half, full = jnp.bfloat16, jnp.float32
    length, width = states_ref.shape
    rows, units = gate_hbm.shape
    tokens, model = normed.shape
    slots = patch_ref.shape[0]
    chunks, wide = 8, model // 8
    block = (rows // 2, units)

    def first_scope(maps, crossed, sums, queries, keys, values, bias, mixed, pooled):
        front(
            states_ref,
            lengths_ref,
            offsets_ref,
            count_ref,
            gain_ref,
            cotangent_ref,
            gate_hbm,
            up_hbm,
            query_hbm,
            key_hbm,
            value_hbm,
            proj_hbm,
            own_features,
            hidden_ref,
            grads,
            normed,
            gates,
            ups,
            maps,
            crossed,
            sums,
            earlier,
            queries,
            keys,
            values,
            bias,
            mixed,
            pooled,
            contexts,
            *semaphores[:11],
        )

    pl.run_scoped(
        first_scope,
        pltpu.VMEM((width, model), half),
        pltpu.VMEM((tokens, model), half),
        pltpu.VMEM((2, tokens, units), full),
        pltpu.VMEM((length, width), half),
        pltpu.VMEM((3 * length, width), half),
        pltpu.VMEM((3 * length, width), half),
        pltpu.VMEM((length // HEAD, HEAD, WINDOW + HEAD), full),
        pltpu.VMEM((length, width), half),
        pltpu.VMEM((slots, width), half),
    )

    def second_scope(*scratch):
        grad_rings(
            normed,
            grads,
            own_features,
            gain_ref,
            gates,
            ups,
            gate_ref,
            up_ref,
            patch_ref,
            *scratch,
            *semaphores[11:],
        )

    pl.run_scoped(
        second_scope,
        pltpu.VMEM((chunks, slots, wide), full),
        pltpu.VMEM((4, SIDE, *block), half),
        pltpu.VMEM((4, SIDE - 1, SIDE, *block), half),
        pltpu.VMEM((4, *block), half),
        pltpu.VMEM((4, SIDE - 1, *block), half),
        pltpu.VMEM((chunks, 2, SIDE, slots, wide), half),
        pltpu.VMEM((chunks, SIDE, slots, wide), half),
        pltpu.VMEM((SIDE - 1, chunks, slots, wide), half),
    )


def whole_layer(
    states, lengths, offsets, count, gain, cotangent, gate_w, up_w, squares, w_proj
):
    length, width = states.shape
    slots = offsets.shape[1]
    rows, units = gate_w.shape
    model = w_proj.shape[1]
    tokens = 2 * SIDE * slots
    chunks = 8
    dma = pltpu.SemaphoreType.DMA
    whole = pl.BlockSpec(memory_space=pltpu.VMEM)
    anywhere = pl.BlockSpec(memory_space=pl.ANY)
    half, full = jnp.bfloat16, jnp.float32
    return pl.pallas_call(
        layer,
        out_shape=(
            jax.ShapeDtypeStruct((tokens, units), half),
            jax.ShapeDtypeStruct((rows, units), full),
            jax.ShapeDtypeStruct((rows, units), full),
            jax.ShapeDtypeStruct((slots, model), full),
        ),
        in_specs=[whole] * 6 + [anywhere] * 6,
        out_specs=(whole,) * 4,
        scratch_shapes=[
            pltpu.VMEM((slots, model), half),
            pltpu.VMEM((tokens, 2 * units), half),
            pltpu.VMEM((tokens, model), half),
            pltpu.VMEM((SIDE, SIDE, rows, units), half),
            pltpu.VMEM((SIDE, SIDE, rows, units), half),
            pltpu.VMEM((2 * length, width), half),
            pltpu.VMEM((tokens, width), half),
            dma((6,)),
            dma((4, SIDE - 1)),
            dma((4, SIDE - 1)),
            dma((4, SIDE - 1, SIDE)),
            dma((4, SIDE - 1, SIDE)),
            dma((2,)),
            dma((2,)),
            dma((SIDE - 1,)),
            dma((SIDE - 1,)),
            dma((SIDE,)),
            dma((SIDE,)),
            dma((4, SIDE - 1, SIDE)),
            dma((4, SIDE - 1, SIDE)),
            dma((4, SIDE - 1)),
            dma((4, SIDE - 1)),
            dma((chunks,)),
            dma((chunks,)),
            dma((SIDE - 1, chunks)),
            dma((SIDE - 1, chunks)),
            pltpu.SemaphoreType.REGULAR,
        ],
        compiler_params=pltpu.CompilerParams(
            collective_id=0, has_side_effects=True, vmem_limit_bytes=62 * 1024 * 1024
        ),
        name="layer",
    )(states, lengths, offsets, count, gain, cotangent, gate_w, up_w, *squares, w_proj)


def shards(
    bytes_in,
    doc_lengths,
    patch_offsets,
    patch_counts,
    w_query,
    w_key,
    w_value,
    w_proj,
    norm_gain,
    gate_w,
    up_w,
    d_hidden,
):
    units = gate_w.shape[1]
    hidden, grad_gate, grad_up, patch_grad = whole_layer(
        bytes_in[0],
        doc_lengths[None],
        patch_offsets,
        patch_counts,
        norm_gain[None],
        d_hidden.reshape(-1, units),
        gate_w,
        up_w,
        (w_query, w_key, w_value),
        w_proj,
    )
    return (hidden.reshape(d_hidden.shape), grad_gate, grad_up, patch_grad[None])


def solution(mesh):
    return jax.shard_map(
        shards,
        mesh=mesh,
        in_specs=(
            P("seq", "fsdp", None),
            P(),
            P("seq", "fsdp"),
            P("seq", "fsdp"),
            P(),
            P(),
            P(),
            P(),
            P(),
            P("fsdp", "seq"),
            P("fsdp", "seq"),
            P(None, "fsdp", "seq"),
        ),
        out_specs=(
            P(None, "fsdp", "seq"),
            P("fsdp", "seq"),
            P("fsdp", "seq"),
            P("seq", "fsdp", None),
        ),
        check_vma=False,
    )
```

```python
import math

import jax
import jax.numpy as jnp
from jax import lax
from jax.experimental import pallas as pl
from jax.experimental.pallas import tpu as pltpu
from jax.sharding import PartitionSpec as P

HEAD = 128
WINDOW = 512


epsilon = 1e-05
masked_score = -1e30


MESH = pl.DeviceIdType.MESH
SIDE = 4


def wrapped(value):
    return lax.rem(value + 2 * SIDE, SIDE)


def grad_rings(
    normed_ref,
    grads_ref,
    features_ref,
    gain_ref,
    gates,
    ups,
    gate_ref,
    up_ref,
    patch_ref,
    inward,
    first,
    arrived,
    second,
    crossed,
    parts,
    paired,
    ringed,
    put,
    got,
    put2,
    got2,
    put3,
    got3,
    put4,
    got4,
    ready,
):
    seq = lax.axis_index("seq")
    spot = lax.axis_index("fsdp")
    x, core = lax.div(seq, 2), lax.rem(seq, 2)
    z, y = lax.div(spot, SIDE), lax.rem(spot, SIDE)
    rows = first.shape[2]
    units = gate_ref.shape[1]
    chunks, _, _, slots, wide = parts.shape

    around = (
        (seq, wrapped(z + 1) * SIDE + y),
        (seq, wrapped(z - 1) * SIDE + y),
        (seq, z * SIDE + wrapped(y + 1)),
        (seq, z * SIDE + wrapped(y - 1)),
        (wrapped(x + 1) * 2 + core, spot),
        (wrapped(x - 1) * 2 + core, spot),
        (x * 2 + 1 - core, spot),
    )
    for neighbour in around:
        pl.semaphore_signal(ready, inc=1, device_id=neighbour, device_id_type=MESH)
    pl.semaphore_wait(ready, len(around))

    def place(stream):
        kind, half = stream // 2, stream % 2
        step = 1 - 2 * half
        along, across = (z, y) if kind == 0 else (y, z)
        if kind == 0:
            onward, sideways = around[half], around[2 + half]
        else:
            onward, sideways = around[2 + half], around[half]
        return kind, half, step, along, across, onward, sideways

    def own(stream, t, k):
        kind, half, step, along, across, _, _ = place(stream)
        far = wrapped(along - step * (1 + t))
        near = wrapped(across - step * (1 + k))
        zb, yb = (far, near) if kind == 0 else (near, far)
        at = pl.multiple_of((zb * SIDE + yb) * 2 * rows + half * rows, rows)
        return lax.dot_general(
            normed_ref[:, pl.ds(at, rows)],
            grads_ref[:, kind * units : (kind + 1) * units],
            (((0,), (0,)), ((), ())),
            preferred_element_type=jnp.float32,
        )

    def hop(stream, source, t, k):
        return pltpu.make_async_remote_copy(
            src_ref=source,
            dst_ref=arrived.at[stream, t, k],
            send_sem=put.at[stream, t, k],
            recv_sem=got.at[stream, t, k],
            device_id=place(stream)[5],
            device_id_type=MESH,
        )

    def hop2(stream, source, k):
        return pltpu.make_async_remote_copy(
            src_ref=source,
            dst_ref=crossed.at[stream, k],
            send_sem=put2.at[stream, k],
            recv_sem=got2.at[stream, k],
            device_id=place(stream)[6],
            device_id_type=MESH,
        )

    def across_cores(n):
        return pltpu.make_async_remote_copy(
            src_ref=parts.at[n, 1 - core],
            dst_ref=paired.at[n],
            send_sem=put3.at[n],
            recv_sem=got3.at[n],
            device_id=around[6],
            device_id_type=MESH,
        )

    def x_hop(side, n, source, t):
        return pltpu.make_async_remote_copy(
            src_ref=source,
            dst_ref=ringed.at[t, n],
            send_sem=put4.at[t, n],
            recv_sem=got4.at[t, n],
            device_id=around[4 + side],
            device_id_type=MESH,
        )

    def opening(k, carry):
        for stream in range(4):
            first[stream, k] = own(stream, 0, k).astype(jnp.bfloat16)
            hop(stream, first.at[stream, k], 0, k).start()
        return carry

    lax.fori_loop(0, SIDE, opening, 0)

    def input_part(n):
        depth = 2 * rows
        for column in range(wide // depth):
            zb, yb = lax.div(n, 2), 2 * lax.rem(n, 2) + column
            value = 0.0
            for kind, block in enumerate((gates[zb, yb], ups[yb, zb])):
                value += lax.dot_general(
                    grads_ref[:, kind * units : (kind + 1) * units],
                    block,
                    (((1,), (1,)), ((), ())),
                    preferred_element_type=jnp.float32,
                )
            value = value.astype(jnp.bfloat16)
            for block in range(2 * SIDE):
                parts[n, block % 2, block // 2, :, column * depth : (column + 1) * depth] = (
                    value[block * slots : (block + 1) * slots]
                )
        across_cores(n).start()

    def middle(t, busy):
        def body(k, carry):
            for stream in range(4):
                value = own(stream, t, k)
                hop(stream, first.at[stream, k], t - 1, k).wait_recv()
                arrived[stream, t - 1, k] = (
                    value + arrived[stream, t - 1, k].astype(jnp.float32)
                ).astype(jnp.bfloat16)
                hop(stream, arrived.at[stream, t - 1, k], t, k).start()
            if busy:
                input_part(2 * k)
                input_part(2 * k + 1)
            return carry

        lax.fori_loop(0, SIDE, body, 0)

    def x_phase(t):
        def body(m, carry):
            for side in range(2):
                n = 2 * m + side
                block = wrapped(x - (1 - 2 * side) * (1 + t))
                if t == 0:
                    across_cores(n).wait_recv()
                    paired[n] = (
                        paired[n].astype(jnp.float32) + parts[n, core].astype(jnp.float32)
                    ).astype(jnp.bfloat16)
                    x_hop(side, n, paired.at[n, block], 0).start()
                else:
                    x_hop(side, n, paired.at[n, block], t - 1).wait_recv()
                    value = ringed[t - 1, n].astype(jnp.float32) + paired[n, block].astype(
                        jnp.float32
                    )
                    if t < SIDE - 1:
                        ringed[t - 1, n] = value.astype(jnp.bfloat16)
                        x_hop(side, n, ringed.at[t - 1, n], t).start()
                    else:
                        inward[n] = value
            return carry

        lax.fori_loop(0, chunks // 2, body, 0)

    last = SIDE - 1

    def total(stream, k):
        value = own(stream, last, k)
        hop(stream, first.at[stream, k], last - 1, k).wait_recv()
        return value + arrived[stream, last - 1, k].astype(jnp.float32)

    middle(1, True)
    x_phase(0)
    middle(2, False)
    x_phase(1)

    for stream in range(4):
        second[stream] = total(stream, 0).astype(jnp.bfloat16)
        hop2(stream, second.at[stream], 0).start()
    x_phase(2)

    def crossing(k, carry):
        for stream in range(4):
            value = total(stream, k)
            hop2(stream, second.at[stream], k - 1).wait_recv()
            crossed[stream, k - 1] = (
                value + crossed[stream, k - 1].astype(jnp.float32)
            ).astype(jnp.bfloat16)
            hop2(stream, crossed.at[stream, k - 1], k).start()
        return carry

    lax.fori_loop(1, last, crossing, 0)
    x_phase(3)

    def columns_of(n):
        at = pl.ds(pl.multiple_of(n * wide, wide), wide)
        return at, features_ref[:, at].astype(jnp.float32), gain_ref[:, at] * inward[n]

    def means(n, carry):
        _, features, scaled = columns_of(n)
        return (
            carry[0] + jnp.sum(features * features, axis=1, keepdims=True),
            carry[1] + jnp.sum(features * scaled, axis=1, keepdims=True),
        )

    nothing = jnp.zeros((slots, 1), jnp.float32)
    squares, products = lax.fori_loop(0, chunks, means, (nothing, nothing))
    inverse = lax.rsqrt(squares / (chunks * wide) + epsilon)
    factor = inverse * inverse * inverse * (products / (chunks * wide))

    def patch_part(n, carry):
        at, features, scaled = columns_of(n)
        patch_ref[:, at] = inverse * scaled - features * factor
        return carry

    lax.fori_loop(0, chunks, patch_part, 0)

    for stream in range(4):
        kind, half = stream // 2, stream % 2
        value = total(stream, last)
        hop2(stream, second.at[stream], last - 1).wait_recv()
        (gate_ref, up_ref)[kind][half * rows : (half + 1) * rows, :] = value + crossed[
            stream, last - 1
        ].astype(jnp.float32)

    def sent(index, carry):
        t, k = lax.div(index, SIDE), lax.rem(index, SIDE)
        for stream in range(4):
            hop(stream, first.at[stream, k], t, k).wait_send()
        return carry

    lax.fori_loop(0, last * SIDE, sent, 0)
    for stream in range(4):
        for k in range(last):
            hop2(stream, second.at[stream], k).wait_send()

    def x_sent(m, carry):
        for side in range(2):
            n = 2 * m + side
            across_cores(n).wait_send()
            for t in range(last):
                x_hop(side, n, ringed.at[0, n], t).wait_send()
        return carry

    lax.fori_loop(0, chunks // 2, x_sent, 0)


ORDER = (
    "a0 b00",
    "A0 a1 b01",
    "B00 b10",
    "A1 a2 b02",
    "B01 b11",
    "A2 b03",
    "B10 b20",
    "B02 b12",
    "B11 b21",
    "B03 b13",
    "B12 b22",
    "B13 b23"
)


def front(
    states_ref,
    lengths_ref,
    offsets_ref,
    count_ref,
    gain_ref,
    cotangent_ref,
    gate_hbm,
    up_hbm,
    query_hbm,
    key_hbm,
    value_hbm,
    proj_hbm,
    own_features_ref,
    hidden_ref,
    grads_ref,
    normed_ref,
    gates,
    ups,
    maps,
    crossed,
    sums,
    earlier,
    queries,
    keys,
    values,
    bias,
    mixed,
    pooled,
    contexts,
    loads,
    put_a,
    got_a,
    put_b,
    got_b,
    put_s,
    got_s,
    put_x,
    got_x,
    put_c,
    got_c,
):
    seq = lax.axis_index("seq")
    spot = lax.axis_index("fsdp")
    x, core = lax.div(seq, 2), lax.rem(seq, 2)
    z, y = lax.div(spot, SIDE), lax.rem(spot, SIDE)
    groups, spots = 2 * SIDE, SIDE * SIDE
    devices = groups * spots
    length, width = states_ref.shape
    slots = offsets_ref.shape[1]
    heads = width // HEAD
    units = gate_hbm.shape[1]
    rows = gate_hbm.shape[0]
    model = proj_hbm.shape[1]
    ranges = (slice(0, 3 * HEAD), slice(3 * HEAD, units))

    def device_of(position):
        position = lax.rem(position + devices, devices)
        return lax.div(position, spots), lax.rem(position, spots)

    here = seq * spots + spot
    around = (
        (seq, wrapped(z + 1) * SIDE + y),
        (seq, wrapped(z - 1) * SIDE + y),
        (seq, z * SIDE + wrapped(y + 1)),
        (seq, z * SIDE + wrapped(y - 1)),
    )
    next_block = device_of(here + 1)
    after_next = device_of(here + 2)
    other_core = (x * 2 + 1 - core, spot)
    along_x = tuple((wrapped(x + by) * 2 + core, spot) for by in range(1, SIDE))

    places = [
        (gates.at[z, y], gate_hbm),
        (ups.at[y, z], up_hbm),
        (maps.at[:, 0:width], query_hbm),
        (maps.at[:, width : 2 * width], key_hbm),
        (maps.at[:, 2 * width : 3 * width], value_hbm),
        (maps, proj_hbm),
    ]
    load = [
        pltpu.make_async_copy(source, target, loads.at[i])
        for i, (target, source) in enumerate(places)
    ]
    for copy in load[:2]:
        copy.start()

    greeted = (
        *around,
        next_block,
        device_of(here - 1),
        other_core,
        *along_x,
    )
    barrier = pltpu.get_barrier_semaphore()
    for neighbour in greeted:
        pl.semaphore_signal(barrier, inc=1, device_id=neighbour, device_id_type=MESH)
    pl.semaphore_wait(barrier, len(greeted))

    def remote(source, target, sent, arrived, device):
        return pltpu.make_async_remote_copy(
            src_ref=source,
            dst_ref=target,
            send_sem=sent,
            recv_sem=arrived,
            device_id=device,
            device_id_type=MESH,
        )

    recent = earlier.at[length : 2 * length]
    oldest = earlier.at[0:length]
    to_next = remote(states_ref, recent, put_s.at[0], got_s.at[0], next_block)
    to_after = remote(recent, oldest, put_s.at[1], got_s.at[1], next_block)
    to_next.start()
    load[0].wait()
    load[1].wait()

    def place(stream, t):
        kind, half = stream // 2, stream % 2
        along = z if kind == 0 else y
        return (gates, ups)[kind], wrapped(along - (1 - 2 * half) * t), ranges[half]

    def piece(stream, t, k):
        kind, half = stream // 2, stream % 2
        across = y if kind == 0 else z
        buffer, far, columns = place(stream, t)
        return buffer.at[far, wrapped(across - (1 - 2 * half) * k), :, columns]

    def small(stream, k):
        kind, half = stream // 2, stream % 2
        device = around[2 + half] if kind == 0 else around[half]
        region = piece(stream, 0, k)
        return remote(region, region, put_a.at[stream, k], got_a.at[stream, k], device)

    def large(stream, t, k):
        kind, half = stream // 2, stream % 2
        device = around[half] if kind == 0 else around[2 + half]
        region = piece(stream, t, k)
        return remote(
            region, region, put_b.at[stream, t, k], got_b.at[stream, t, k], device
        )

    last = SIDE - 1

    steps = {
        "a": lambda stream, k: small(stream, k).start(),
        "A": lambda stream, k: small(stream, k).wait_recv(),
        "b": lambda stream, t, k: large(stream, t, k).start(),
        "B": lambda stream, t, k: large(stream, t, k).wait_recv(),
    }

    def tick(number):
        for stream in range(4):
            for step in ORDER[number].split():
                steps[step[0]](stream, *(int(digit) for digit in step[1:]))

    tick(0)
    for copy in load[2:5]:
        copy.start()

    chunk = 2 * HEAD
    scale = 1.0 / math.sqrt(HEAD)

    def dot(a, b):
        return jnp.dot(a, b, preferred_element_type=jnp.float32)

    def dot_t(a, b):
        return lax.dot_general(
            a, b, (((1,), (1,)), ((), ())), preferred_element_type=jnp.float32
        )

    load[2].wait()

    def make_queries(n, carry):
        at = pl.ds(pl.multiple_of(n * chunk, chunk), chunk)
        queries[:, at] = dot(states_ref[...], maps[:, at]).astype(jnp.bfloat16)
        return carry

    lax.fori_loop(0, width // chunk, make_queries, 0)
    tick(1)
    to_next.wait_recv()
    to_after.start()
    tick(2)
    load[3].wait()
    load[4].wait()

    def keys_and_values(source, row):
        def body(n, carry):
            at = pl.ds(pl.multiple_of(n * chunk, chunk), chunk)
            key_at = pl.ds(pl.multiple_of(width + n * chunk, chunk), chunk)
            value_at = pl.ds(pl.multiple_of(2 * width + n * chunk, chunk), chunk)
            into = slice(row, row + length)
            keys[into, at] = dot(source[...], maps[:, key_at]).astype(jnp.bfloat16)
            values[into, at] = dot(source[...], maps[:, value_at]).astype(jnp.bfloat16)
            return carry

        lax.fori_loop(0, width // chunk, body, 0)

    keys_and_values(states_ref, 2 * length)
    tick(3)

    span = WINDOW + HEAD
    parts = length // HEAD

    def iota(shape, dim):
        return lax.broadcasted_iota(jnp.int32, shape, dim)

    def turned(line, by):
        count = line.shape[1]
        picked = iota((count, count), 1) == iota((count, count), 0) + by
        return jnp.sum(jnp.where(picked, line, 0.0), axis=1, keepdims=True)

    docs = lengths_ref.shape[1]
    lengths = lengths_ref[...].astype(jnp.float32)
    earlier_docs = iota((docs, docs), 1) < iota((docs, docs), 0)
    start_column = jnp.sum(jnp.where(earlier_docs, lengths, 0.0), axis=1, keepdims=True)
    same = iota((docs, docs), 1) == iota((docs, docs), 0)
    start_line = jnp.sum(jnp.where(same, start_column, 0.0), axis=0, keepdims=True)
    key_pos = (here - 2) * length + iota((docs, 3 * length), 1)
    query_pos = here * length + iota((length, docs), 0)
    key_doc = jnp.sum(
        jnp.where(start_column <= key_pos.astype(jnp.float32), 1.0, 0.0), axis=0, keepdims=True
    )
    query_doc = jnp.sum(
        jnp.where(start_line <= query_pos.astype(jnp.float32), 1.0, 0.0), axis=1, keepdims=True
    )
    for r in range(parts):
        row = lax.broadcasted_iota(jnp.int32, (HEAD, span), 0)
        column = lax.broadcasted_iota(jnp.int32, (HEAD, span), 1)
        allowed = (column > row) & (column <= row + WINDOW)
        start = 2 * length - WINDOW + r * HEAD
        allowed = allowed & (
            key_doc[:, start : start + span] == query_doc[r * HEAD : (r + 1) * HEAD, :]
        )
        bias[r] = jnp.where(allowed, 0.0, masked_score)

    keys_and_values(recent, length)
    tick(4)
    offsets = offsets_ref[...].astype(jnp.float32)
    count = count_ref[...].astype(jnp.float32)
    slot = iota((slots, 1), 0).astype(jnp.float32)
    present = slot < count
    begins = turned(offsets, 0)
    ends = jnp.where((slot == count - 1.0) | (slot == slots - 1.0), 1.0 * length, turned(offsets, 1))
    begins, ends = jnp.where(present, begins, 0.0), jnp.where(present, ends, 0.0)
    byte = iota((slots, length), 1).astype(jnp.float32)
    member = (byte >= begins) & (byte < ends)
    ones = jnp.where(member, 1.0, 0.0)
    pool_bias = jnp.where(member, 0.0, masked_score)
    sizes = jnp.maximum(jnp.sum(ones, axis=1, keepdims=True), 1.0)
    members = ones.astype(jnp.bfloat16)
    tick(5)
    to_after.wait_recv()
    keys_and_values(oldest, 0)
    load[5].start()
    tick(6)

    def attend(h, carry):
        at = pl.ds(pl.multiple_of(h * HEAD, HEAD), HEAD)
        for r in range(parts):
            here_rows = slice(r * HEAD, (r + 1) * HEAD)
            start = 2 * length - WINDOW + r * HEAD
            scores = dot_t(queries[here_rows, at], keys[start : start + span, at])
            scores = scores * scale + bias[r]
            weights = jnp.exp(scores - jnp.max(scores, axis=1, keepdims=True))
            total = jnp.sum(weights, axis=1, keepdims=True)
            summed = dot(weights.astype(jnp.bfloat16), values[start : start + span, at])
            mixed[here_rows, at] = (
                states_ref[here_rows, at].astype(jnp.float32) + summed / total
            ).astype(jnp.bfloat16)
        return carry

    mine = pl.ds(pl.multiple_of(seq * slots, slots), slots)

    def pool(h, carry):
        at = pl.ds(pl.multiple_of(h * HEAD, HEAD), HEAD)
        scores = dot_t(pooled[:, at], mixed[:, at]) * scale + pool_bias
        weights = jnp.exp(scores - jnp.max(scores, axis=1, keepdims=True))
        total = jnp.sum(weights, axis=1, keepdims=True)
        summed = dot(weights.astype(jnp.bfloat16), mixed[:, at]) / total
        contexts[mine, at] = jnp.where(present, summed, 0.0).astype(jnp.bfloat16)
        return carry

    def context_of(group, part):
        at = pl.ds(pl.multiple_of(group * slots, slots), slots)
        return contexts.at[at, part * width // 2 : (part + 1) * width // 2]

    def x_send(by, part):
        region = context_of(seq, part)
        return remote(
            region,
            region,
            put_x.at[part, by - 1],
            got_x.at[part, by - 1],
            along_x[by - 1],
        )

    def core_send(by, part):
        region = context_of(wrapped(x - by) * 2 + core, part)
        return remote(
            region, region, put_c.at[part, by], got_c.at[part, by], other_core
        )

    for part in range(2):
        first_head, stop_head = part * heads // 2, (part + 1) * heads // 2
        some = slice(first_head * HEAD, stop_head * HEAD)
        lax.fori_loop(first_head, stop_head, attend, 0)
        pooled[:, some] = (dot(members, mixed[:, some]) / sizes).astype(jnp.bfloat16)
        lax.fori_loop(first_head, stop_head, pool, 0)
        for by in range(1, SIDE):
            x_send(by, part).start()
        core_send(0, part).start()
        tick(7 + part)
    tick(9)
    for part in range(2):
        for by in (1, 3, 2):
            x_send(by, part).wait_recv()
            core_send(by, part).start()
        if part == 0:
            tick(10)
    for part in range(2):
        for by in range(SIDE):
            core_send(by, part).wait_recv()
    load[5].wait()

    wide = 4 * HEAD

    def project(n, squares):
        at = pl.ds(pl.multiple_of(n * wide, wide), wide)
        features = dot(contexts[...], maps[:, at]).astype(jnp.bfloat16)
        normed_ref[:, at] = features
        full = features.astype(jnp.float32)
        return squares + jnp.sum(full * full, axis=1, keepdims=True)

    squares = jnp.zeros((groups * slots, 1), jnp.float32)
    squares = lax.fori_loop(0, model // wide // 2, project, squares)
    tick(11)
    squares = lax.fori_loop(model // wide // 2, model // wide, project, squares)
    inverse = lax.rsqrt(squares / model + epsilon)
    own_features_ref[...] = normed_ref[mine, :]

    def normalize(n, carry):
        at = pl.ds(pl.multiple_of(n * rows, rows), rows)
        place_turned = (n % SIDE) * SIDE + n // SIDE
        value = (normed_ref[:, at].astype(jnp.float32) * inverse * gain_ref[:, at]).astype(
            jnp.bfloat16
        )
        normed_ref[:, at] = value
        crossed[:, pl.ds(pl.multiple_of(place_turned * rows, rows), rows)] = value
        return carry

    lax.fori_loop(0, model // rows, normalize, 0)
    sums[...] = jnp.zeros_like(sums)

    def accumulate(t, carry):
        @pl.when(t == last)
        def _():
            for stream in range(4):
                for k in range(SIDE):
                    large(stream, last - 1, k).wait_recv()

        for stream in range(4):
            buffer, far, columns = place(stream, t)
            kind, count = stream // 2, columns.stop - columns.start
            deep = SIDE * rows
            at = pl.ds(pl.multiple_of(far * deep, deep), deep)
            block = buffer[far, :, :, columns].reshape(deep, count)
            sums[kind, :, columns] += dot((normed_ref, crossed)[kind][:, at], block)
        return carry

    lax.fori_loop(0, SIDE, accumulate, 0)

    def gating(n, carry):
        at = pl.ds(pl.multiple_of(n * slots, slots), slots)
        gate_pre, up_pre = sums[0, at], sums[1, at]
        sigmoid_gate = jax.nn.sigmoid(gate_pre)
        swish = gate_pre * sigmoid_gate
        cotangent = cotangent_ref[at, :].astype(jnp.float32)
        hidden_ref[at, :] = (swish * up_pre).astype(jnp.bfloat16)
        grads_ref[at, 0:units] = (
            cotangent * up_pre * sigmoid_gate * (1.0 + gate_pre * (1.0 - sigmoid_gate))
        ).astype(jnp.bfloat16)
        grads_ref[at, units : 2 * units] = (cotangent * swish).astype(jnp.bfloat16)
        return carry

    lax.fori_loop(0, groups, gating, 0)

    to_next.wait_send()
    to_after.wait_send()
    for stream in range(4):
        for k in range(SIDE):
            if k < last:
                small(stream, k).wait_send()
            for t in range(last):
                large(stream, t, k).wait_send()
    for part in range(2):
        for by in range(SIDE):
            if by > 0:
                x_send(by, part).wait_send()
            core_send(by, part).wait_send()


def layer(
    states_ref,
    lengths_ref,
    offsets_ref,
    count_ref,
    gain_ref,
    cotangent_ref,
    gate_hbm,
    up_hbm,
    query_hbm,
    key_hbm,
    value_hbm,
    proj_hbm,
    hidden_ref,
    gate_ref,
    up_ref,
    patch_ref,
    own_features,
    grads,
    normed,
    gates,
    ups,
    earlier,
    contexts,
    *semaphores,
):
    half, full = jnp.bfloat16, jnp.float32
    length, width = states_ref.shape
    rows, units = gate_hbm.shape
    tokens, model = normed.shape
    slots = patch_ref.shape[0]
    chunks, wide = 8, model // 8
    block = (rows // 2, units)

    def first_scope(maps, crossed, sums, queries, keys, values, bias, mixed, pooled):
        front(
            states_ref,
            lengths_ref,
            offsets_ref,
            count_ref,
            gain_ref,
            cotangent_ref,
            gate_hbm,
            up_hbm,
            query_hbm,
            key_hbm,
            value_hbm,
            proj_hbm,
            own_features,
            hidden_ref,
            grads,
            normed,
            gates,
            ups,
            maps,
            crossed,
            sums,
            earlier,
            queries,
            keys,
            values,
            bias,
            mixed,
            pooled,
            contexts,
            *semaphores[:11],
        )

    pl.run_scoped(
        first_scope,
        pltpu.VMEM((width, model), half),
        pltpu.VMEM((tokens, model), half),
        pltpu.VMEM((2, tokens, units), full),
        pltpu.VMEM((length, width), half),
        pltpu.VMEM((3 * length, width), half),
        pltpu.VMEM((3 * length, width), half),
        pltpu.VMEM((length // HEAD, HEAD, WINDOW + HEAD), full),
        pltpu.VMEM((length, width), half),
        pltpu.VMEM((slots, width), half),
    )

    def second_scope(*scratch):
        grad_rings(
            normed,
            grads,
            own_features,
            gain_ref,
            gates,
            ups,
            gate_ref,
            up_ref,
            patch_ref,
            *scratch,
            *semaphores[11:],
        )

    pl.run_scoped(
        second_scope,
        pltpu.VMEM((chunks, slots, wide), full),
        pltpu.VMEM((4, SIDE, *block), half),
        pltpu.VMEM((4, SIDE - 1, SIDE, *block), half),
        pltpu.VMEM((4, *block), half),
        pltpu.VMEM((4, SIDE - 1, *block), half),
        pltpu.VMEM((chunks, 2, SIDE, slots, wide), half),
        pltpu.VMEM((chunks, SIDE, slots, wide), half),
        pltpu.VMEM((SIDE - 1, chunks, slots, wide), half),
    )


def whole_layer(
    states, lengths, offsets, count, gain, cotangent, gate_w, up_w, squares, w_proj
):
    length, width = states.shape
    slots = offsets.shape[1]
    rows, units = gate_w.shape
    model = w_proj.shape[1]
    tokens = 2 * SIDE * slots
    chunks = 8
    dma = pltpu.SemaphoreType.DMA
    whole = pl.BlockSpec(memory_space=pltpu.VMEM)
    anywhere = pl.BlockSpec(memory_space=pl.ANY)
    half, full = jnp.bfloat16, jnp.float32
    return pl.pallas_call(
        layer,
        out_shape=(
            jax.ShapeDtypeStruct((tokens, units), half),
            jax.ShapeDtypeStruct((rows, units), full),
            jax.ShapeDtypeStruct((rows, units), full),
            jax.ShapeDtypeStruct((slots, model), full),
        ),
        in_specs=[whole] * 6 + [anywhere] * 6,
        out_specs=(whole,) * 4,
        scratch_shapes=[
            pltpu.VMEM((slots, model), half),
            pltpu.VMEM((tokens, 2 * units), half),
            pltpu.VMEM((tokens, model), half),
            pltpu.VMEM((SIDE, SIDE, rows, units), half),
            pltpu.VMEM((SIDE, SIDE, rows, units), half),
            pltpu.VMEM((2 * length, width), half),
            pltpu.VMEM((tokens, width), half),
            dma((6,)),
            dma((4, SIDE - 1)),
            dma((4, SIDE - 1)),
            dma((4, SIDE - 1, SIDE)),
            dma((4, SIDE - 1, SIDE)),
            dma((2,)),
            dma((2,)),
            dma((2, SIDE - 1)),
            dma((2, SIDE - 1)),
            dma((2, SIDE)),
            dma((2, SIDE)),
            dma((4, SIDE - 1, SIDE)),
            dma((4, SIDE - 1, SIDE)),
            dma((4, SIDE - 1)),
            dma((4, SIDE - 1)),
            dma((chunks,)),
            dma((chunks,)),
            dma((SIDE - 1, chunks)),
            dma((SIDE - 1, chunks)),
            pltpu.SemaphoreType.REGULAR,
        ],
        compiler_params=pltpu.CompilerParams(
            collective_id=0, has_side_effects=True, vmem_limit_bytes=62 * 1024 * 1024
        ),
        name="layer",
    )(states, lengths, offsets, count, gain, cotangent, gate_w, up_w, *squares, w_proj)


def deliver(*refs):
    count = len(refs) // 3
    sources, targets = refs[:count], refs[count : 2 * count]
    buffers, got, put = refs[2 * count : 3 * count], refs[-2], refs[-1]
    inward = [
        pltpu.make_async_copy(sources[i], buffers[i], got.at[i]) for i in range(count)
    ]
    outward = [
        pltpu.make_async_copy(buffers[i], targets[i], put.at[i]) for i in range(count)
    ]
    for copy in inward:
        copy.start()
    for before, after in zip(inward, outward):
        before.wait()
        after.start()
    for copy in outward:
        copy.wait()


def delivered(arrays):
    anywhere = pl.BlockSpec(memory_space=pl.ANY)
    return pl.pallas_call(
        deliver,
        out_shape=tuple(jax.ShapeDtypeStruct(a.shape, a.dtype) for a in arrays),
        in_specs=[anywhere] * len(arrays),
        out_specs=(anywhere,) * len(arrays),
        scratch_shapes=[pltpu.VMEM(a.shape, a.dtype) for a in arrays]
        + [pltpu.SemaphoreType.DMA((len(arrays),))] * 2,
        name="deliver",
    )(*arrays)


def shards(
    bytes_in,
    doc_lengths,
    patch_offsets,
    patch_counts,
    w_query,
    w_key,
    w_value,
    w_proj,
    norm_gain,
    gate_w,
    up_w,
    d_hidden,
):
    units = gate_w.shape[1]
    results = whole_layer(
        bytes_in[0],
        doc_lengths[None],
        patch_offsets,
        patch_counts,
        norm_gain[None],
        d_hidden.reshape(-1, units),
        gate_w,
        up_w,
        (w_query, w_key, w_value),
        w_proj,
    )
    hidden, grad_gate, grad_up, patch_grad = delivered(results)
    return (hidden.reshape(d_hidden.shape), grad_gate, grad_up, patch_grad[None])


def solution(mesh):
    return jax.shard_map(
        shards,
        mesh=mesh,
        in_specs=(
            P("seq", "fsdp", None),
            P(),
            P("seq", "fsdp"),
            P("seq", "fsdp"),
            P(),
            P(),
            P(),
            P(),
            P(),
            P("fsdp", "seq"),
            P("fsdp", "seq"),
            P(None, "fsdp", "seq"),
        ),
        out_specs=(
            P(None, "fsdp", "seq"),
            P("fsdp", "seq"),
            P("fsdp", "seq"),
            P("seq", "fsdp", None),
        ),
        check_vma=False,
    )
```

```python
import math

import jax
import jax.numpy as jnp
from jax import lax
from jax.experimental import pallas as pl
from jax.experimental.pallas import tpu as pltpu
from jax.sharding import PartitionSpec as P

HEAD = 128
WINDOW = 512


epsilon = 1e-05
masked_score = -1e30


MESH = pl.DeviceIdType.MESH
SIDE = 4


def wrapped(value):
    return lax.rem(value + 2 * SIDE, SIDE)


def grad_rings(
    normed_ref,
    grads_ref,
    features_ref,
    gain_ref,
    gates,
    ups,
    gate_ref,
    up_ref,
    patch_ref,
    inward,
    first,
    arrived,
    second,
    crossed,
    parts,
    paired,
    ringed,
    put,
    got,
    put2,
    got2,
    put3,
    got3,
    put4,
    got4,
    ready,
):
    seq = lax.axis_index("seq")
    spot = lax.axis_index("fsdp")
    x, core = lax.div(seq, 2), lax.rem(seq, 2)
    z, y = lax.div(spot, SIDE), lax.rem(spot, SIDE)
    rows = first.shape[2]
    units = gate_ref.shape[1]
    chunks, _, _, slots, wide = parts.shape

    around = (
        (seq, wrapped(z + 1) * SIDE + y),
        (seq, wrapped(z - 1) * SIDE + y),
        (seq, z * SIDE + wrapped(y + 1)),
        (seq, z * SIDE + wrapped(y - 1)),
        (wrapped(x + 1) * 2 + core, spot),
        (wrapped(x - 1) * 2 + core, spot),
        (x * 2 + 1 - core, spot),
    )
    for neighbour in around:
        pl.semaphore_signal(ready, inc=1, device_id=neighbour, device_id_type=MESH)
    pl.semaphore_wait(ready, len(around))

    def place(stream):
        kind, half = stream // 2, stream % 2
        step = 1 - 2 * half
        along, across = (z, y) if kind == 0 else (y, z)
        if kind == 0:
            onward, sideways = around[half], around[2 + half]
        else:
            onward, sideways = around[2 + half], around[half]
        return kind, half, step, along, across, onward, sideways

    def own(stream, t, k):
        kind, half, step, along, across, _, _ = place(stream)
        far = wrapped(along - step * (1 + t))
        near = wrapped(across - step * (1 + k))
        zb, yb = (far, near) if kind == 0 else (near, far)
        at = pl.multiple_of((zb * SIDE + yb) * 2 * rows + half * rows, rows)
        return lax.dot_general(
            normed_ref[:, pl.ds(at, rows)],
            grads_ref[:, kind * units : (kind + 1) * units],
            (((0,), (0,)), ((), ())),
            preferred_element_type=jnp.float32,
        )

    def hop(stream, source, t, k):
        return pltpu.make_async_remote_copy(
            src_ref=source,
            dst_ref=arrived.at[stream, t, k],
            send_sem=put.at[stream, t, k],
            recv_sem=got.at[stream, t, k],
            device_id=place(stream)[5],
            device_id_type=MESH,
        )

    def hop2(stream, source, k):
        return pltpu.make_async_remote_copy(
            src_ref=source,
            dst_ref=crossed.at[stream, k],
            send_sem=put2.at[stream, k],
            recv_sem=got2.at[stream, k],
            device_id=place(stream)[6],
            device_id_type=MESH,
        )

    def across_cores(n):
        return pltpu.make_async_remote_copy(
            src_ref=parts.at[n, 1 - core],
            dst_ref=paired.at[n],
            send_sem=put3.at[n],
            recv_sem=got3.at[n],
            device_id=around[6],
            device_id_type=MESH,
        )

    def x_hop(side, n, source, t):
        return pltpu.make_async_remote_copy(
            src_ref=source,
            dst_ref=ringed.at[t, n],
            send_sem=put4.at[t, n],
            recv_sem=got4.at[t, n],
            device_id=around[4 + side],
            device_id_type=MESH,
        )

    def input_part(n):
        depth = 2 * rows
        for column in range(wide // depth):
            zb, yb = lax.div(n, 2), 2 * lax.rem(n, 2) + column
            value = 0.0
            for kind, block in enumerate((gates[zb, yb], ups[yb, zb])):
                value += lax.dot_general(
                    grads_ref[:, kind * units : (kind + 1) * units],
                    block,
                    (((1,), (1,)), ((), ())),
                    preferred_element_type=jnp.float32,
                )
            value = value.astype(jnp.bfloat16)
            for block in range(2 * SIDE):
                parts[n, block % 2, block // 2, :, column * depth : (column + 1) * depth] = (
                    value[block * slots : (block + 1) * slots]
                )
        across_cores(n).start()

    def x_phase(t):
        def body(m, carry):
            for side in range(2):
                n = 2 * m + side
                block = wrapped(x - (1 - 2 * side) * (1 + t))
                if t == 0:
                    across_cores(n).wait_recv()
                    paired[n] = (
                        paired[n].astype(jnp.float32) + parts[n, core].astype(jnp.float32)
                    ).astype(jnp.bfloat16)
                    x_hop(side, n, paired.at[n, block], 0).start()
                else:
                    x_hop(side, n, paired.at[n, block], t - 1).wait_recv()
                    value = ringed[t - 1, n].astype(jnp.float32) + paired[n, block].astype(
                        jnp.float32
                    )
                    if t < SIDE - 1:
                        ringed[t - 1, n] = value.astype(jnp.bfloat16)
                        x_hop(side, n, ringed.at[t - 1, n], t).start()
                    else:
                        inward[n] = value
            return carry

        lax.fori_loop(0, chunks // 2, body, 0)

    last = SIDE - 1

    def total(stream, k):
        value = own(stream, last, k)
        hop(stream, first.at[stream, k], last - 1, k).wait_recv()
        return value + arrived[stream, last - 1, k].astype(jnp.float32)

    def wave(number, carry):
        @pl.when(number < SIDE)
        def _():
            for stream in range(4):
                first[stream, number] = own(stream, 0, number).astype(jnp.bfloat16)
                hop(stream, first.at[stream, number], 0, number).start()

        for t in (1, 2):

            @pl.when((number >= t) & (number < t + SIDE))
            def _(t=t):
                k = number - t
                for stream in range(4):
                    value = own(stream, t, k)
                    hop(stream, first.at[stream, k], t - 1, k).wait_recv()
                    arrived[stream, t - 1, k] = (
                        value + arrived[stream, t - 1, k].astype(jnp.float32)
                    ).astype(jnp.bfloat16)
                    hop(stream, arrived.at[stream, t - 1, k], t, k).start()

        @pl.when(number == last)
        def _():
            for stream in range(4):
                second[stream] = total(stream, 0).astype(jnp.bfloat16)
                hop2(stream, second.at[stream], 0).start()

        @pl.when(number > last)
        def _():
            k = number - last
            for stream in range(4):
                value = total(stream, k)
                hop2(stream, second.at[stream], k - 1).wait_recv()
                crossed[stream, k - 1] = (
                    value + crossed[stream, k - 1].astype(jnp.float32)
                ).astype(jnp.bfloat16)
                hop2(stream, crossed.at[stream, k - 1], k).start()

        @pl.when((number == 1) | (number == 2))
        def _():
            def part_of(index, inner):
                input_part(index)
                return inner

            lax.fori_loop((number - 1) * SIDE, number * SIDE, part_of, 0)

        for phase in range(last):

            @pl.when(number == last + phase)
            def _(phase=phase):
                x_phase(phase)

        return carry

    lax.fori_loop(0, 2 * last, wave, 0)
    x_phase(last)

    def columns_of(n):
        at = pl.ds(pl.multiple_of(n * wide, wide), wide)
        return at, features_ref[:, at].astype(jnp.float32), gain_ref[:, at] * inward[n]

    def means(n, carry):
        _, features, scaled = columns_of(n)
        return (
            carry[0] + jnp.sum(features * features, axis=1, keepdims=True),
            carry[1] + jnp.sum(features * scaled, axis=1, keepdims=True),
        )

    nothing = jnp.zeros((slots, 1), jnp.float32)
    squares, products = lax.fori_loop(0, chunks, means, (nothing, nothing))
    inverse = lax.rsqrt(squares / (chunks * wide) + epsilon)
    factor = inverse * inverse * inverse * (products / (chunks * wide))

    def patch_part(n, carry):
        at, features, scaled = columns_of(n)
        patch_ref[:, at] = inverse * scaled - features * factor
        return carry

    lax.fori_loop(0, chunks, patch_part, 0)

    for stream in range(4):
        kind, half = stream // 2, stream % 2
        value = total(stream, last)
        hop2(stream, second.at[stream], last - 1).wait_recv()
        (gate_ref, up_ref)[kind][half * rows : (half + 1) * rows, :] = value + crossed[
            stream, last - 1
        ].astype(jnp.float32)

    def sent(index, carry):
        t, k = lax.div(index, SIDE), lax.rem(index, SIDE)
        for stream in range(4):
            hop(stream, first.at[stream, k], t, k).wait_send()
        return carry

    lax.fori_loop(0, last * SIDE, sent, 0)
    for stream in range(4):
        for k in range(last):
            hop2(stream, second.at[stream], k).wait_send()

    def x_sent(m, carry):
        for side in range(2):
            n = 2 * m + side
            across_cores(n).wait_send()
            for t in range(last):
                x_hop(side, n, ringed.at[0, n], t).wait_send()
        return carry

    lax.fori_loop(0, chunks // 2, x_sent, 0)


ORDER = (
    "a0 b00",
    "A0 a1 b01",
    "B00 b10",
    "A1 a2 b02",
    "B01 b11",
    "A2 b03",
    "B10 b20",
    "B02 b12",
    "B11 b21",
    "B03 b13",
    "B12 b22",
    "B13 b23"
)


def front(
    states_ref,
    lengths_ref,
    offsets_ref,
    count_ref,
    gain_ref,
    cotangent_ref,
    gate_hbm,
    up_hbm,
    query_hbm,
    key_hbm,
    value_hbm,
    proj_hbm,
    own_features_ref,
    hidden_ref,
    grads_ref,
    normed_ref,
    gates,
    ups,
    maps,
    crossed,
    sums,
    earlier,
    queries,
    keys,
    values,
    bias,
    mixed,
    pooled,
    contexts,
    loads,
    put_a,
    got_a,
    put_b,
    got_b,
    put_s,
    got_s,
    put_x,
    got_x,
    put_c,
    got_c,
):
    seq = lax.axis_index("seq")
    spot = lax.axis_index("fsdp")
    x, core = lax.div(seq, 2), lax.rem(seq, 2)
    z, y = lax.div(spot, SIDE), lax.rem(spot, SIDE)
    groups, spots = 2 * SIDE, SIDE * SIDE
    devices = groups * spots
    length, width = states_ref.shape
    slots = offsets_ref.shape[1]
    heads = width // HEAD
    units = gate_hbm.shape[1]
    rows = gate_hbm.shape[0]
    model = proj_hbm.shape[1]
    ranges = (slice(0, 3 * HEAD), slice(3 * HEAD, units))

    def device_of(position):
        position = lax.rem(position + devices, devices)
        return lax.div(position, spots), lax.rem(position, spots)

    here = seq * spots + spot
    around = (
        (seq, wrapped(z + 1) * SIDE + y),
        (seq, wrapped(z - 1) * SIDE + y),
        (seq, z * SIDE + wrapped(y + 1)),
        (seq, z * SIDE + wrapped(y - 1)),
    )
    next_block = device_of(here + 1)
    after_next = device_of(here + 2)
    other_core = (x * 2 + 1 - core, spot)
    along_x = tuple((wrapped(x + by) * 2 + core, spot) for by in range(1, SIDE))

    places = [
        (gates.at[z, y], gate_hbm),
        (ups.at[y, z], up_hbm),
        (maps.at[:, 0:width], query_hbm),
        (maps.at[:, width : 2 * width], key_hbm),
        (maps.at[:, 2 * width : 3 * width], value_hbm),
        (maps, proj_hbm),
    ]
    load = [
        pltpu.make_async_copy(source, target, loads.at[i])
        for i, (target, source) in enumerate(places)
    ]
    for copy in load[:2]:
        copy.start()

    greeted = (
        *around,
        next_block,
        device_of(here - 1),
        other_core,
        *along_x,
    )
    barrier = pltpu.get_barrier_semaphore()
    for neighbour in greeted:
        pl.semaphore_signal(barrier, inc=1, device_id=neighbour, device_id_type=MESH)
    pl.semaphore_wait(barrier, len(greeted))

    def remote(source, target, sent, arrived, device):
        return pltpu.make_async_remote_copy(
            src_ref=source,
            dst_ref=target,
            send_sem=sent,
            recv_sem=arrived,
            device_id=device,
            device_id_type=MESH,
        )

    recent = earlier.at[length : 2 * length]
    oldest = earlier.at[0:length]
    to_next = remote(states_ref, recent, put_s.at[0], got_s.at[0], next_block)
    to_after = remote(recent, oldest, put_s.at[1], got_s.at[1], next_block)
    to_next.start()
    load[0].wait()
    load[1].wait()

    def place(stream, t):
        kind, half = stream // 2, stream % 2
        along = z if kind == 0 else y
        return (gates, ups)[kind], wrapped(along - (1 - 2 * half) * t), ranges[half]

    def piece(stream, t, k):
        kind, half = stream // 2, stream % 2
        across = y if kind == 0 else z
        buffer, far, columns = place(stream, t)
        return buffer.at[far, wrapped(across - (1 - 2 * half) * k), :, columns]

    def small(stream, k):
        kind, half = stream // 2, stream % 2
        device = around[2 + half] if kind == 0 else around[half]
        region = piece(stream, 0, k)
        return remote(region, region, put_a.at[stream, k], got_a.at[stream, k], device)

    def large(stream, t, k):
        kind, half = stream // 2, stream % 2
        device = around[half] if kind == 0 else around[2 + half]
        region = piece(stream, t, k)
        return remote(
            region, region, put_b.at[stream, t, k], got_b.at[stream, t, k], device
        )

    last = SIDE - 1

    steps = {
        "a": lambda stream, k: small(stream, k).start(),
        "A": lambda stream, k: small(stream, k).wait_recv(),
        "b": lambda stream, t, k: large(stream, t, k).start(),
        "B": lambda stream, t, k: large(stream, t, k).wait_recv(),
    }

    def tick(number):
        for stream in range(4):
            for step in ORDER[number].split():
                steps[step[0]](stream, *(int(digit) for digit in step[1:]))

    tick(0)
    for copy in load[2:5]:
        copy.start()

    chunk = 2 * HEAD
    scale = 1.0 / math.sqrt(HEAD)

    def dot(a, b):
        return jnp.dot(a, b, preferred_element_type=jnp.float32)

    def dot_t(a, b):
        return lax.dot_general(
            a, b, (((1,), (1,)), ((), ())), preferred_element_type=jnp.float32
        )

    load[2].wait()

    def make_queries(n, carry):
        at = pl.ds(pl.multiple_of(n * chunk, chunk), chunk)
        queries[:, at] = dot(states_ref[...], maps[:, at]).astype(jnp.bfloat16)
        return carry

    lax.fori_loop(0, width // chunk, make_queries, 0)
    tick(1)
    to_next.wait_recv()
    to_after.start()
    tick(2)
    load[3].wait()
    load[4].wait()

    def keys_and_values(source, row):
        def body(n, carry):
            at = pl.ds(pl.multiple_of(n * chunk, chunk), chunk)
            key_at = pl.ds(pl.multiple_of(width + n * chunk, chunk), chunk)
            value_at = pl.ds(pl.multiple_of(2 * width + n * chunk, chunk), chunk)
            into = slice(row, row + length)
            keys[into, at] = dot(source[...], maps[:, key_at]).astype(jnp.bfloat16)
            values[into, at] = dot(source[...], maps[:, value_at]).astype(jnp.bfloat16)
            return carry

        lax.fori_loop(0, width // chunk, body, 0)

    keys_and_values(states_ref, 2 * length)
    tick(3)

    span = WINDOW + HEAD
    parts = length // HEAD

    def iota(shape, dim):
        return lax.broadcasted_iota(jnp.int32, shape, dim)

    def turned(line, by):
        count = line.shape[1]
        picked = iota((count, count), 1) == iota((count, count), 0) + by
        return jnp.sum(jnp.where(picked, line, 0.0), axis=1, keepdims=True)

    docs = lengths_ref.shape[1]
    lengths = lengths_ref[...].astype(jnp.float32)
    earlier_docs = iota((docs, docs), 1) < iota((docs, docs), 0)
    start_column = jnp.sum(jnp.where(earlier_docs, lengths, 0.0), axis=1, keepdims=True)
    same = iota((docs, docs), 1) == iota((docs, docs), 0)
    start_line = jnp.sum(jnp.where(same, start_column, 0.0), axis=0, keepdims=True)
    key_pos = (here - 2) * length + iota((docs, 3 * length), 1)
    query_pos = here * length + iota((length, docs), 0)
    key_doc = jnp.sum(
        jnp.where(start_column <= key_pos.astype(jnp.float32), 1.0, 0.0), axis=0, keepdims=True
    )
    query_doc = jnp.sum(
        jnp.where(start_line <= query_pos.astype(jnp.float32), 1.0, 0.0), axis=1, keepdims=True
    )
    for r in range(parts):
        row = lax.broadcasted_iota(jnp.int32, (HEAD, span), 0)
        column = lax.broadcasted_iota(jnp.int32, (HEAD, span), 1)
        allowed = (column > row) & (column <= row + WINDOW)
        start = 2 * length - WINDOW + r * HEAD
        allowed = allowed & (
            key_doc[:, start : start + span] == query_doc[r * HEAD : (r + 1) * HEAD, :]
        )
        bias[r] = jnp.where(allowed, 0.0, masked_score)

    keys_and_values(recent, length)
    tick(4)
    offsets = offsets_ref[...].astype(jnp.float32)
    count = count_ref[...].astype(jnp.float32)
    slot = iota((slots, 1), 0).astype(jnp.float32)
    present = slot < count
    begins = turned(offsets, 0)
    ends = jnp.where((slot == count - 1.0) | (slot == slots - 1.0), 1.0 * length, turned(offsets, 1))
    begins, ends = jnp.where(present, begins, 0.0), jnp.where(present, ends, 0.0)
    byte = iota((slots, length), 1).astype(jnp.float32)
    member = (byte >= begins) & (byte < ends)
    ones = jnp.where(member, 1.0, 0.0)
    pool_bias = jnp.where(member, 0.0, masked_score)
    sizes = jnp.maximum(jnp.sum(ones, axis=1, keepdims=True), 1.0)
    members = ones.astype(jnp.bfloat16)
    tick(5)
    to_after.wait_recv()
    keys_and_values(oldest, 0)
    load[5].start()
    tick(6)

    def attend(h, carry):
        at = pl.ds(pl.multiple_of(h * HEAD, HEAD), HEAD)
        for r in range(parts):
            here_rows = slice(r * HEAD, (r + 1) * HEAD)
            start = 2 * length - WINDOW + r * HEAD
            scores = dot_t(queries[here_rows, at], keys[start : start + span, at])
            scores = scores * scale + bias[r]
            weights = jnp.exp(scores - jnp.max(scores, axis=1, keepdims=True))
            total = jnp.sum(weights, axis=1, keepdims=True)
            summed = dot(weights.astype(jnp.bfloat16), values[start : start + span, at])
            mixed[here_rows, at] = (
                states_ref[here_rows, at].astype(jnp.float32) + summed / total
            ).astype(jnp.bfloat16)
        return carry

    mine = pl.ds(pl.multiple_of(seq * slots, slots), slots)

    def pool(h, carry):
        at = pl.ds(pl.multiple_of(h * HEAD, HEAD), HEAD)
        scores = dot_t(pooled[:, at], mixed[:, at]) * scale + pool_bias
        weights = jnp.exp(scores - jnp.max(scores, axis=1, keepdims=True))
        total = jnp.sum(weights, axis=1, keepdims=True)
        summed = dot(weights.astype(jnp.bfloat16), mixed[:, at]) / total
        contexts[mine, at] = jnp.where(present, summed, 0.0).astype(jnp.bfloat16)
        return carry

    def context_of(group, part):
        at = pl.ds(pl.multiple_of(group * slots, slots), slots)
        return contexts.at[at, part * width // 2 : (part + 1) * width // 2]

    def x_send(by, part):
        region = context_of(seq, part)
        return remote(
            region,
            region,
            put_x.at[part, by - 1],
            got_x.at[part, by - 1],
            along_x[by - 1],
        )

    def core_send(by, part):
        region = context_of(wrapped(x - by) * 2 + core, part)
        return remote(
            region, region, put_c.at[part, by], got_c.at[part, by], other_core
        )

    for part in range(2):
        first_head, stop_head = part * heads // 2, (part + 1) * heads // 2
        some = slice(first_head * HEAD, stop_head * HEAD)
        lax.fori_loop(first_head, stop_head, attend, 0)
        pooled[:, some] = (dot(members, mixed[:, some]) / sizes).astype(jnp.bfloat16)
        lax.fori_loop(first_head, stop_head, pool, 0)
        for by in range(1, SIDE):
            x_send(by, part).start()
        core_send(0, part).start()
        tick(7 + part)
    tick(9)
    for part in range(2):
        for by in (1, 3, 2):
            x_send(by, part).wait_recv()
            core_send(by, part).start()
        if part == 0:
            tick(10)
    for part in range(2):
        for by in range(SIDE):
            core_send(by, part).wait_recv()
    load[5].wait()

    wide = 4 * HEAD

    def project(n, squares):
        at = pl.ds(pl.multiple_of(n * wide, wide), wide)
        features = dot(contexts[...], maps[:, at]).astype(jnp.bfloat16)
        normed_ref[:, at] = features
        full = features.astype(jnp.float32)
        return squares + jnp.sum(full * full, axis=1, keepdims=True)

    squares = jnp.zeros((groups * slots, 1), jnp.float32)
    squares = lax.fori_loop(0, model // wide // 2, project, squares)
    tick(11)
    squares = lax.fori_loop(model // wide // 2, model // wide, project, squares)
    inverse = lax.rsqrt(squares / model + epsilon)
    own_features_ref[...] = normed_ref[mine, :]

    def normalize(n, carry):
        at = pl.ds(pl.multiple_of(n * rows, rows), rows)
        place_turned = (n % SIDE) * SIDE + n // SIDE
        value = (normed_ref[:, at].astype(jnp.float32) * inverse * gain_ref[:, at]).astype(
            jnp.bfloat16
        )
        normed_ref[:, at] = value
        crossed[:, pl.ds(pl.multiple_of(place_turned * rows, rows), rows)] = value
        return carry

    lax.fori_loop(0, model // rows, normalize, 0)
    sums[...] = jnp.zeros_like(sums)

    def accumulate(t, carry):
        @pl.when(t == last)
        def _():
            for stream in range(4):
                for k in range(SIDE):
                    large(stream, last - 1, k).wait_recv()

        for stream in range(4):
            buffer, far, columns = place(stream, t)
            kind, count = stream // 2, columns.stop - columns.start
            deep = SIDE * rows
            at = pl.ds(pl.multiple_of(far * deep, deep), deep)
            block = buffer[far, :, :, columns].reshape(deep, count)
            sums[kind, :, columns] += dot((normed_ref, crossed)[kind][:, at], block)
        return carry

    lax.fori_loop(0, SIDE, accumulate, 0)

    def gating(n, carry):
        at = pl.ds(pl.multiple_of(n * slots, slots), slots)
        gate_pre, up_pre = sums[0, at], sums[1, at]
        sigmoid_gate = jax.nn.sigmoid(gate_pre)
        swish = gate_pre * sigmoid_gate
        cotangent = cotangent_ref[at, :].astype(jnp.float32)
        hidden_ref[at, :] = (swish * up_pre).astype(jnp.bfloat16)
        grads_ref[at, 0:units] = (
            cotangent * up_pre * sigmoid_gate * (1.0 + gate_pre * (1.0 - sigmoid_gate))
        ).astype(jnp.bfloat16)
        grads_ref[at, units : 2 * units] = (cotangent * swish).astype(jnp.bfloat16)
        return carry

    lax.fori_loop(0, groups, gating, 0)

    to_next.wait_send()
    to_after.wait_send()
    for stream in range(4):
        for k in range(SIDE):
            if k < last:
                small(stream, k).wait_send()
            for t in range(last):
                large(stream, t, k).wait_send()
    for part in range(2):
        for by in range(SIDE):
            if by > 0:
                x_send(by, part).wait_send()
            core_send(by, part).wait_send()


def layer(
    states_ref,
    lengths_ref,
    offsets_ref,
    count_ref,
    gain_ref,
    cotangent_ref,
    gate_hbm,
    up_hbm,
    query_hbm,
    key_hbm,
    value_hbm,
    proj_hbm,
    hidden_ref,
    gate_ref,
    up_ref,
    patch_ref,
    own_features,
    grads,
    normed,
    gates,
    ups,
    earlier,
    contexts,
    *semaphores,
):
    half, full = jnp.bfloat16, jnp.float32
    length, width = states_ref.shape
    rows, units = gate_hbm.shape
    tokens, model = normed.shape
    slots = patch_ref.shape[0]
    chunks, wide = 8, model // 8
    block = (rows // 2, units)

    def first_scope(maps, crossed, sums, queries, keys, values, bias, mixed, pooled):
        front(
            states_ref,
            lengths_ref,
            offsets_ref,
            count_ref,
            gain_ref,
            cotangent_ref,
            gate_hbm,
            up_hbm,
            query_hbm,
            key_hbm,
            value_hbm,
            proj_hbm,
            own_features,
            hidden_ref,
            grads,
            normed,
            gates,
            ups,
            maps,
            crossed,
            sums,
            earlier,
            queries,
            keys,
            values,
            bias,
            mixed,
            pooled,
            contexts,
            *semaphores[:11],
        )

    pl.run_scoped(
        first_scope,
        pltpu.VMEM((width, model), half),
        pltpu.VMEM((tokens, model), half),
        pltpu.VMEM((2, tokens, units), full),
        pltpu.VMEM((length, width), half),
        pltpu.VMEM((3 * length, width), half),
        pltpu.VMEM((3 * length, width), half),
        pltpu.VMEM((length // HEAD, HEAD, WINDOW + HEAD), full),
        pltpu.VMEM((length, width), half),
        pltpu.VMEM((slots, width), half),
    )

    def second_scope(*scratch):
        grad_rings(
            normed,
            grads,
            own_features,
            gain_ref,
            gates,
            ups,
            gate_ref,
            up_ref,
            patch_ref,
            *scratch,
            *semaphores[11:],
        )

    pl.run_scoped(
        second_scope,
        pltpu.VMEM((chunks, slots, wide), full),
        pltpu.VMEM((4, SIDE, *block), half),
        pltpu.VMEM((4, SIDE - 1, SIDE, *block), half),
        pltpu.VMEM((4, *block), half),
        pltpu.VMEM((4, SIDE - 1, *block), half),
        pltpu.VMEM((chunks, 2, SIDE, slots, wide), half),
        pltpu.VMEM((chunks, SIDE, slots, wide), half),
        pltpu.VMEM((SIDE - 1, chunks, slots, wide), half),
    )


def whole_layer(
    states, lengths, offsets, count, gain, cotangent, gate_w, up_w, squares, w_proj
):
    length, width = states.shape
    slots = offsets.shape[1]
    rows, units = gate_w.shape
    model = w_proj.shape[1]
    tokens = 2 * SIDE * slots
    chunks = 8
    dma = pltpu.SemaphoreType.DMA
    whole = pl.BlockSpec(memory_space=pltpu.VMEM)
    anywhere = pl.BlockSpec(memory_space=pl.ANY)
    half, full = jnp.bfloat16, jnp.float32
    return pl.pallas_call(
        layer,
        out_shape=(
            jax.ShapeDtypeStruct((tokens, units), half),
            jax.ShapeDtypeStruct((rows, units), full),
            jax.ShapeDtypeStruct((rows, units), full),
            jax.ShapeDtypeStruct((slots, model), full),
        ),
        in_specs=[whole] * 6 + [anywhere] * 6,
        out_specs=(whole,) * 4,
        scratch_shapes=[
            pltpu.VMEM((slots, model), half),
            pltpu.VMEM((tokens, 2 * units), half),
            pltpu.VMEM((tokens, model), half),
            pltpu.VMEM((SIDE, SIDE, rows, units), half),
            pltpu.VMEM((SIDE, SIDE, rows, units), half),
            pltpu.VMEM((2 * length, width), half),
            pltpu.VMEM((tokens, width), half),
            dma((6,)),
            dma((4, SIDE - 1)),
            dma((4, SIDE - 1)),
            dma((4, SIDE - 1, SIDE)),
            dma((4, SIDE - 1, SIDE)),
            dma((2,)),
            dma((2,)),
            dma((2, SIDE - 1)),
            dma((2, SIDE - 1)),
            dma((2, SIDE)),
            dma((2, SIDE)),
            dma((4, SIDE - 1, SIDE)),
            dma((4, SIDE - 1, SIDE)),
            dma((4, SIDE - 1)),
            dma((4, SIDE - 1)),
            dma((chunks,)),
            dma((chunks,)),
            dma((SIDE - 1, chunks)),
            dma((SIDE - 1, chunks)),
            pltpu.SemaphoreType.REGULAR,
        ],
        compiler_params=pltpu.CompilerParams(
            collective_id=0, has_side_effects=True, vmem_limit_bytes=62 * 1024 * 1024
        ),
        name="layer",
    )(states, lengths, offsets, count, gain, cotangent, gate_w, up_w, *squares, w_proj)


def deliver(*refs):
    count = len(refs) // 3
    sources, targets = refs[:count], refs[count : 2 * count]
    buffers, got, put = refs[2 * count : 3 * count], refs[-2], refs[-1]
    inward = [
        pltpu.make_async_copy(sources[i], buffers[i], got.at[i]) for i in range(count)
    ]
    outward = [
        pltpu.make_async_copy(buffers[i], targets[i], put.at[i]) for i in range(count)
    ]
    for copy in inward:
        copy.start()
    for before, after in zip(inward, outward):
        before.wait()
        after.start()
    for copy in outward:
        copy.wait()


def delivered(arrays):
    anywhere = pl.BlockSpec(memory_space=pl.ANY)
    return pl.pallas_call(
        deliver,
        out_shape=tuple(jax.ShapeDtypeStruct(a.shape, a.dtype) for a in arrays),
        in_specs=[anywhere] * len(arrays),
        out_specs=(anywhere,) * len(arrays),
        scratch_shapes=[pltpu.VMEM(a.shape, a.dtype) for a in arrays]
        + [pltpu.SemaphoreType.DMA((len(arrays),))] * 2,
        name="deliver",
    )(*arrays)


def shards(
    bytes_in,
    doc_lengths,
    patch_offsets,
    patch_counts,
    w_query,
    w_key,
    w_value,
    w_proj,
    norm_gain,
    gate_w,
    up_w,
    d_hidden,
):
    units = gate_w.shape[1]
    results = whole_layer(
        bytes_in[0],
        doc_lengths[None],
        patch_offsets,
        patch_counts,
        norm_gain[None],
        d_hidden.reshape(-1, units),
        gate_w,
        up_w,
        (w_query, w_key, w_value),
        w_proj,
    )
    hidden, grad_gate, grad_up, patch_grad = delivered(results)
    return (hidden.reshape(d_hidden.shape), grad_gate, grad_up, patch_grad[None])


def solution(mesh):
    return jax.shard_map(
        shards,
        mesh=mesh,
        in_specs=(
            P("seq", "fsdp", None),
            P(),
            P("seq", "fsdp"),
            P("seq", "fsdp"),
            P(),
            P(),
            P(),
            P(),
            P(),
            P("fsdp", "seq"),
            P("fsdp", "seq"),
            P(None, "fsdp", "seq"),
        ),
        out_specs=(
            P(None, "fsdp", "seq"),
            P("fsdp", "seq"),
            P("fsdp", "seq"),
            P("seq", "fsdp", None),
        ),
        check_vma=False,
    )
```

```python
import math

import jax
import jax.numpy as jnp
from jax import lax
from jax.experimental import pallas as pl
from jax.experimental.pallas import tpu as pltpu
from jax.sharding import PartitionSpec as P

HEAD = 128
WINDOW = 512


epsilon = 1e-05
masked_score = -1e30


MESH = pl.DeviceIdType.MESH
SIDE = 4


def wrapped(value):
    return lax.rem(value + 2 * SIDE, SIDE)


def grad_rings(
    normed_ref,
    grads_ref,
    features_ref,
    gain_ref,
    gates,
    ups,
    gate_ref,
    up_ref,
    patch_ref,
    inward,
    first,
    arrived,
    second,
    crossed,
    parts,
    paired,
    ringed,
    put,
    got,
    put2,
    got2,
    put3,
    got3,
    put4,
    got4,
    ready,
):
    seq = lax.axis_index("seq")
    spot = lax.axis_index("fsdp")
    x, core = lax.div(seq, 2), lax.rem(seq, 2)
    z, y = lax.div(spot, SIDE), lax.rem(spot, SIDE)
    rows = first.shape[2]
    units = gate_ref.shape[1]
    chunks, _, _, slots, wide = parts.shape

    around = (
        (seq, wrapped(z + 1) * SIDE + y),
        (seq, wrapped(z - 1) * SIDE + y),
        (seq, z * SIDE + wrapped(y + 1)),
        (seq, z * SIDE + wrapped(y - 1)),
        (wrapped(x + 1) * 2 + core, spot),
        (wrapped(x - 1) * 2 + core, spot),
        (x * 2 + 1 - core, spot),
    )
    for neighbour in around:
        pl.semaphore_signal(ready, inc=1, device_id=neighbour, device_id_type=MESH)
    pl.semaphore_wait(ready, len(around))

    def place(stream):
        kind, half = stream // 2, stream % 2
        step = 1 - 2 * half
        along, across = (z, y) if kind == 0 else (y, z)
        if kind == 0:
            onward, sideways = around[half], around[2 + half]
        else:
            onward, sideways = around[2 + half], around[half]
        return kind, half, step, along, across, onward, sideways

    def own(stream, t, k):
        kind, half, step, along, across, _, _ = place(stream)
        far = wrapped(along - step * (1 + t))
        near = wrapped(across - step * (1 + k))
        zb, yb = (far, near) if kind == 0 else (near, far)
        at = pl.multiple_of((zb * SIDE + yb) * 2 * rows + half * rows, rows)
        return lax.dot_general(
            normed_ref[:, pl.ds(at, rows)],
            grads_ref[:, kind * units : (kind + 1) * units],
            (((0,), (0,)), ((), ())),
            preferred_element_type=jnp.float32,
        )

    def hop(stream, source, t, k):
        return pltpu.make_async_remote_copy(
            src_ref=source,
            dst_ref=arrived.at[stream, t, k],
            send_sem=put.at[stream, t, k],
            recv_sem=got.at[stream, t, k],
            device_id=place(stream)[5],
            device_id_type=MESH,
        )

    def hop2(stream, source, k):
        return pltpu.make_async_remote_copy(
            src_ref=source,
            dst_ref=crossed.at[stream, k],
            send_sem=put2.at[stream, k],
            recv_sem=got2.at[stream, k],
            device_id=place(stream)[6],
            device_id_type=MESH,
        )

    def across_cores(n):
        return pltpu.make_async_remote_copy(
            src_ref=parts.at[n, 1 - core],
            dst_ref=paired.at[n],
            send_sem=put3.at[n],
            recv_sem=got3.at[n],
            device_id=around[6],
            device_id_type=MESH,
        )

    def x_hop(side, n, source, t):
        return pltpu.make_async_remote_copy(
            src_ref=source,
            dst_ref=ringed.at[t, n],
            send_sem=put4.at[t, n],
            recv_sem=got4.at[t, n],
            device_id=around[4 + side],
            device_id_type=MESH,
        )

    def input_part(n):
        depth = 2 * rows
        for column in range(wide // depth):
            zb, yb = lax.div(n, 2), 2 * lax.rem(n, 2) + column
            value = 0.0
            for kind, block in enumerate((gates[zb, yb], ups[yb, zb])):
                value += lax.dot_general(
                    grads_ref[:, kind * units : (kind + 1) * units],
                    block,
                    (((1,), (1,)), ((), ())),
                    preferred_element_type=jnp.float32,
                )
            value = value.astype(jnp.bfloat16)
            for block in range(2 * SIDE):
                parts[n, block % 2, block // 2, :, column * depth : (column + 1) * depth] = (
                    value[block * slots : (block + 1) * slots]
                )
        across_cores(n).start()

    def x_phase(t):
        def body(m, carry):
            for side in range(2):
                n = 2 * m + side
                block = wrapped(x - (1 - 2 * side) * (1 + t))
                if t == 0:
                    across_cores(n).wait_recv()
                    paired[n] = (
                        paired[n].astype(jnp.float32) + parts[n, core].astype(jnp.float32)
                    ).astype(jnp.bfloat16)
                    x_hop(side, n, paired.at[n, block], 0).start()
                else:
                    x_hop(side, n, paired.at[n, block], t - 1).wait_recv()
                    value = ringed[t - 1, n].astype(jnp.float32) + paired[n, block].astype(
                        jnp.float32
                    )
                    if t < SIDE - 1:
                        ringed[t - 1, n] = value.astype(jnp.bfloat16)
                        x_hop(side, n, ringed.at[t - 1, n], t).start()
                    else:
                        inward[n] = value
            return carry

        lax.fori_loop(0, chunks // 2, body, 0)

    last = SIDE - 1

    def total(stream, k):
        value = own(stream, last, k)
        hop(stream, first.at[stream, k], last - 1, k).wait_recv()
        return value + arrived[stream, last - 1, k].astype(jnp.float32)

    def wave(number, carry):
        @pl.when(number < SIDE)
        def _():
            for stream in range(4):
                first[stream, number] = own(stream, 0, number).astype(jnp.bfloat16)
                hop(stream, first.at[stream, number], 0, number).start()

        for t in (1, 2):

            @pl.when((number >= t) & (number < t + SIDE))
            def _(t=t):
                k = number - t
                for stream in range(4):
                    value = own(stream, t, k)
                    hop(stream, first.at[stream, k], t - 1, k).wait_recv()
                    arrived[stream, t - 1, k] = (
                        value + arrived[stream, t - 1, k].astype(jnp.float32)
                    ).astype(jnp.bfloat16)
                    hop(stream, arrived.at[stream, t - 1, k], t, k).start()

        @pl.when(number == last)
        def _():
            for stream in range(4):
                second[stream] = total(stream, 0).astype(jnp.bfloat16)
                hop2(stream, second.at[stream], 0).start()

        @pl.when(number > last)
        def _():
            k = number - last
            for stream in range(4):
                value = total(stream, k)
                hop2(stream, second.at[stream], k - 1).wait_recv()
                crossed[stream, k - 1] = (
                    value + crossed[stream, k - 1].astype(jnp.float32)
                ).astype(jnp.bfloat16)
                hop2(stream, crossed.at[stream, k - 1], k).start()

        @pl.when((number == 1) | (number == 2))
        def _():
            def part_of(index, inner):
                input_part(index)
                return inner

            lax.fori_loop((number - 1) * SIDE, number * SIDE, part_of, 0)

        for phase in range(last):

            @pl.when(number == last + phase)
            def _(phase=phase):
                x_phase(phase)

        return carry

    lax.fori_loop(0, 2 * last, wave, 0)
    x_phase(last)

    def columns_of(n):
        at = pl.ds(pl.multiple_of(n * wide, wide), wide)
        return at, features_ref[:, at].astype(jnp.float32), gain_ref[:, at] * inward[n]

    def means(n, carry):
        _, features, scaled = columns_of(n)
        return (
            carry[0] + jnp.sum(features * features, axis=1, keepdims=True),
            carry[1] + jnp.sum(features * scaled, axis=1, keepdims=True),
        )

    nothing = jnp.zeros((slots, 1), jnp.float32)
    squares, products = lax.fori_loop(0, chunks, means, (nothing, nothing))
    inverse = lax.rsqrt(squares / (chunks * wide) + epsilon)
    factor = inverse * inverse * inverse * (products / (chunks * wide))

    def patch_part(n, carry):
        at, features, scaled = columns_of(n)
        patch_ref[:, at] = inverse * scaled - features * factor
        return carry

    lax.fori_loop(0, chunks, patch_part, 0)

    for stream in range(4):
        kind, half = stream // 2, stream % 2
        value = total(stream, last)
        hop2(stream, second.at[stream], last - 1).wait_recv()
        (gate_ref, up_ref)[kind][half * rows : (half + 1) * rows, :] = value + crossed[
            stream, last - 1
        ].astype(jnp.float32)

    def sent(index, carry):
        t, k = lax.div(index, SIDE), lax.rem(index, SIDE)
        for stream in range(4):
            hop(stream, first.at[stream, k], t, k).wait_send()
        return carry

    lax.fori_loop(0, last * SIDE, sent, 0)
    for stream in range(4):
        for k in range(last):
            hop2(stream, second.at[stream], k).wait_send()

    def x_sent(m, carry):
        for side in range(2):
            n = 2 * m + side
            across_cores(n).wait_send()
            for t in range(last):
                x_hop(side, n, ringed.at[0, n], t).wait_send()
        return carry

    lax.fori_loop(0, chunks // 2, x_sent, 0)


ORDER = (
    "a0 b00",
    "A0 a1 b01",
    "B00 b10",
    "A1 a2 b02",
    "B01 b11",
    "A2 b03",
    "B10 b20",
    "B02 b12",
    "B11 b21",
    "B03 b13",
    "B12 b22",
    "B13 b23"
)


def front(
    states_ref,
    lengths_ref,
    offsets_ref,
    count_ref,
    gain_ref,
    cotangent_ref,
    gate_hbm,
    up_hbm,
    query_hbm,
    key_hbm,
    value_hbm,
    proj_hbm,
    own_features_ref,
    hidden_ref,
    grads_ref,
    normed_ref,
    gates,
    ups,
    maps,
    crossed,
    sums,
    earlier,
    queries,
    keys,
    values,
    bias,
    mixed,
    pooled,
    contexts,
    loads,
    put_a,
    got_a,
    put_b,
    got_b,
    put_s,
    got_s,
    put_x,
    got_x,
    put_c,
    got_c,
):
    seq = lax.axis_index("seq")
    spot = lax.axis_index("fsdp")
    x, core = lax.div(seq, 2), lax.rem(seq, 2)
    z, y = lax.div(spot, SIDE), lax.rem(spot, SIDE)
    groups, spots = 2 * SIDE, SIDE * SIDE
    devices = groups * spots
    length, width = states_ref.shape
    slots = offsets_ref.shape[1]
    heads = width // HEAD
    units = gate_hbm.shape[1]
    rows = gate_hbm.shape[0]
    model = proj_hbm.shape[1]
    ranges = (slice(0, 3 * HEAD), slice(3 * HEAD, units))

    def device_of(position):
        position = lax.rem(position + devices, devices)
        return lax.div(position, spots), lax.rem(position, spots)

    here = seq * spots + spot
    around = (
        (seq, wrapped(z + 1) * SIDE + y),
        (seq, wrapped(z - 1) * SIDE + y),
        (seq, z * SIDE + wrapped(y + 1)),
        (seq, z * SIDE + wrapped(y - 1)),
    )
    next_block = device_of(here + 1)
    after_next = device_of(here + 2)
    other_core = (x * 2 + 1 - core, spot)
    along_x = tuple((wrapped(x + by) * 2 + core, spot) for by in range(1, SIDE))

    places = [
        (gates.at[z, y], gate_hbm),
        (ups.at[y, z], up_hbm),
        (maps.at[:, 0:width], query_hbm),
        (maps.at[:, width : 2 * width], key_hbm),
        (maps.at[:, 2 * width : 3 * width], value_hbm),
        (maps, proj_hbm),
    ]
    load = [
        pltpu.make_async_copy(source, target, loads.at[i])
        for i, (target, source) in enumerate(places)
    ]
    for copy in load[:2]:
        copy.start()

    greeted = (
        *around,
        next_block,
        device_of(here - 1),
        other_core,
        *along_x,
    )
    barrier = pltpu.get_barrier_semaphore()
    for neighbour in greeted:
        pl.semaphore_signal(barrier, inc=1, device_id=neighbour, device_id_type=MESH)
    pl.semaphore_wait(barrier, len(greeted))

    def remote(source, target, sent, arrived, device):
        return pltpu.make_async_remote_copy(
            src_ref=source,
            dst_ref=target,
            send_sem=sent,
            recv_sem=arrived,
            device_id=device,
            device_id_type=MESH,
        )

    recent = earlier.at[length : 2 * length]
    oldest = earlier.at[0:length]
    halves = [slice(p * length // 2, (p + 1) * length // 2) for p in range(2)]
    to_next = [
        remote(states_ref.at[at], recent.at[at], put_s.at[p], got_s.at[p], next_block)
        for p, at in enumerate(halves)
    ]
    to_after = [
        remote(recent.at[at], oldest.at[at], put_s.at[2 + p], got_s.at[2 + p], next_block)
        for p, at in enumerate(halves)
    ]
    for copy in to_next:
        copy.start()
    load[0].wait()
    load[1].wait()

    def place(stream, t):
        kind, half = stream // 2, stream % 2
        along = z if kind == 0 else y
        return (gates, ups)[kind], wrapped(along - (1 - 2 * half) * t), ranges[half]

    def piece(stream, t, k):
        kind, half = stream // 2, stream % 2
        across = y if kind == 0 else z
        buffer, far, columns = place(stream, t)
        return buffer.at[far, wrapped(across - (1 - 2 * half) * k), :, columns]

    def small(stream, k):
        kind, half = stream // 2, stream % 2
        device = around[2 + half] if kind == 0 else around[half]
        region = piece(stream, 0, k)
        return remote(region, region, put_a.at[stream, k], got_a.at[stream, k], device)

    def large(stream, t, k):
        kind, half = stream // 2, stream % 2
        device = around[half] if kind == 0 else around[2 + half]
        region = piece(stream, t, k)
        return remote(
            region, region, put_b.at[stream, t, k], got_b.at[stream, t, k], device
        )

    last = SIDE - 1

    steps = {
        "a": lambda stream, k: small(stream, k).start(),
        "A": lambda stream, k: small(stream, k).wait_recv(),
        "b": lambda stream, t, k: large(stream, t, k).start(),
        "B": lambda stream, t, k: large(stream, t, k).wait_recv(),
    }

    def tick(number):
        for stream in range(4):
            for step in ORDER[number].split():
                steps[step[0]](stream, *(int(digit) for digit in step[1:]))

    tick(0)
    for copy in load[2:5]:
        copy.start()

    chunk = 2 * HEAD
    scale = 1.0 / math.sqrt(HEAD)

    def dot(a, b):
        return jnp.dot(a, b, preferred_element_type=jnp.float32)

    def dot_t(a, b):
        return lax.dot_general(
            a, b, (((1,), (1,)), ((), ())), preferred_element_type=jnp.float32
        )

    load[2].wait()

    def make_queries(n, carry):
        at = pl.ds(pl.multiple_of(n * chunk, chunk), chunk)
        queries[:, at] = dot(states_ref[...], maps[:, at]).astype(jnp.bfloat16)
        return carry

    lax.fori_loop(0, width // chunk, make_queries, 0)
    tick(1)
    for before, after in zip(to_next, to_after):
        before.wait_recv()
        after.start()
    tick(2)
    load[3].wait()
    load[4].wait()

    def keys_and_values(source, row):
        def body(n, carry):
            at = pl.ds(pl.multiple_of(n * chunk, chunk), chunk)
            key_at = pl.ds(pl.multiple_of(width + n * chunk, chunk), chunk)
            value_at = pl.ds(pl.multiple_of(2 * width + n * chunk, chunk), chunk)
            into = slice(row, row + length)
            keys[into, at] = dot(source[...], maps[:, key_at]).astype(jnp.bfloat16)
            values[into, at] = dot(source[...], maps[:, value_at]).astype(jnp.bfloat16)
            return carry

        lax.fori_loop(0, width // chunk, body, 0)

    keys_and_values(states_ref, 2 * length)
    tick(3)

    span = WINDOW + HEAD
    parts = length // HEAD

    def iota(shape, dim):
        return lax.broadcasted_iota(jnp.int32, shape, dim)

    def turned(line, by):
        count = line.shape[1]
        picked = iota((count, count), 1) == iota((count, count), 0) + by
        return jnp.sum(jnp.where(picked, line, 0.0), axis=1, keepdims=True)

    docs = lengths_ref.shape[1]
    lengths = lengths_ref[...].astype(jnp.float32)
    earlier_docs = iota((docs, docs), 1) < iota((docs, docs), 0)
    start_column = jnp.sum(jnp.where(earlier_docs, lengths, 0.0), axis=1, keepdims=True)
    same = iota((docs, docs), 1) == iota((docs, docs), 0)
    start_line = jnp.sum(jnp.where(same, start_column, 0.0), axis=0, keepdims=True)
    key_pos = (here - 2) * length + iota((docs, 3 * length), 1)
    query_pos = here * length + iota((length, docs), 0)
    key_doc = jnp.sum(
        jnp.where(start_column <= key_pos.astype(jnp.float32), 1.0, 0.0), axis=0, keepdims=True
    )
    query_doc = jnp.sum(
        jnp.where(start_line <= query_pos.astype(jnp.float32), 1.0, 0.0), axis=1, keepdims=True
    )
    for r in range(parts):
        row = lax.broadcasted_iota(jnp.int32, (HEAD, span), 0)
        column = lax.broadcasted_iota(jnp.int32, (HEAD, span), 1)
        allowed = (column > row) & (column <= row + WINDOW)
        start = 2 * length - WINDOW + r * HEAD
        allowed = allowed & (
            key_doc[:, start : start + span] == query_doc[r * HEAD : (r + 1) * HEAD, :]
        )
        bias[r] = jnp.where(allowed, 0.0, masked_score)

    keys_and_values(recent, length)
    tick(4)
    offsets = offsets_ref[...].astype(jnp.float32)
    count = count_ref[...].astype(jnp.float32)
    slot = iota((slots, 1), 0).astype(jnp.float32)
    present = slot < count
    begins = turned(offsets, 0)
    ends = jnp.where((slot == count - 1.0) | (slot == slots - 1.0), 1.0 * length, turned(offsets, 1))
    begins, ends = jnp.where(present, begins, 0.0), jnp.where(present, ends, 0.0)
    byte = iota((slots, length), 1).astype(jnp.float32)
    member = (byte >= begins) & (byte < ends)
    ones = jnp.where(member, 1.0, 0.0)
    pool_bias = jnp.where(member, 0.0, masked_score)
    sizes = jnp.maximum(jnp.sum(ones, axis=1, keepdims=True), 1.0)
    members = ones.astype(jnp.bfloat16)
    tick(5)
    for copy in to_after:
        copy.wait_recv()
    keys_and_values(oldest, 0)
    load[5].start()
    tick(6)

    def attend(h, carry):
        at = pl.ds(pl.multiple_of(h * HEAD, HEAD), HEAD)
        for r in range(parts):
            here_rows = slice(r * HEAD, (r + 1) * HEAD)
            start = 2 * length - WINDOW + r * HEAD
            scores = dot_t(queries[here_rows, at], keys[start : start + span, at])
            scores = scores * scale + bias[r]
            weights = jnp.exp(scores - jnp.max(scores, axis=1, keepdims=True))
            total = jnp.sum(weights, axis=1, keepdims=True)
            summed = dot(weights.astype(jnp.bfloat16), values[start : start + span, at])
            mixed[here_rows, at] = (
                states_ref[here_rows, at].astype(jnp.float32) + summed / total
            ).astype(jnp.bfloat16)
        return carry

    mine = pl.ds(pl.multiple_of(seq * slots, slots), slots)

    def pool(h, carry):
        at = pl.ds(pl.multiple_of(h * HEAD, HEAD), HEAD)
        scores = dot_t(pooled[:, at], mixed[:, at]) * scale + pool_bias
        weights = jnp.exp(scores - jnp.max(scores, axis=1, keepdims=True))
        total = jnp.sum(weights, axis=1, keepdims=True)
        summed = dot(weights.astype(jnp.bfloat16), mixed[:, at]) / total
        contexts[mine, at] = jnp.where(present, summed, 0.0).astype(jnp.bfloat16)
        return carry

    def context_of(group, part):
        at = pl.ds(pl.multiple_of(group * slots, slots), slots)
        return contexts.at[at, part * width // 2 : (part + 1) * width // 2]

    def x_send(by, part):
        region = context_of(seq, part)
        return remote(
            region,
            region,
            put_x.at[part, by - 1],
            got_x.at[part, by - 1],
            along_x[by - 1],
        )

    def core_send(by, part):
        region = context_of(wrapped(x - by) * 2 + core, part)
        return remote(
            region, region, put_c.at[part, by], got_c.at[part, by], other_core
        )

    for part in range(2):
        first_head, stop_head = part * heads // 2, (part + 1) * heads // 2
        some = slice(first_head * HEAD, stop_head * HEAD)
        lax.fori_loop(first_head, stop_head, attend, 0)
        pooled[:, some] = (dot(members, mixed[:, some]) / sizes).astype(jnp.bfloat16)
        lax.fori_loop(first_head, stop_head, pool, 0)
        for by in range(1, SIDE):
            x_send(by, part).start()
        core_send(0, part).start()
        tick(7 + part)
    tick(9)
    for part in range(2):
        for by in (1, 3, 2):
            x_send(by, part).wait_recv()
            core_send(by, part).start()
        if part == 0:
            tick(10)
    for part in range(2):
        for by in range(SIDE):
            core_send(by, part).wait_recv()
    load[5].wait()

    wide = 4 * HEAD

    def project(n, squares):
        at = pl.ds(pl.multiple_of(n * wide, wide), wide)
        features = dot(contexts[...], maps[:, at]).astype(jnp.bfloat16)
        normed_ref[:, at] = features
        full = features.astype(jnp.float32)
        return squares + jnp.sum(full * full, axis=1, keepdims=True)

    squares = jnp.zeros((groups * slots, 1), jnp.float32)
    squares = lax.fori_loop(0, model // wide // 2, project, squares)
    tick(11)
    squares = lax.fori_loop(model // wide // 2, model // wide, project, squares)
    inverse = lax.rsqrt(squares / model + epsilon)
    own_features_ref[...] = normed_ref[mine, :]

    def normalize(n, carry):
        at = pl.ds(pl.multiple_of(n * rows, rows), rows)
        place_turned = (n % SIDE) * SIDE + n // SIDE
        value = (normed_ref[:, at].astype(jnp.float32) * inverse * gain_ref[:, at]).astype(
            jnp.bfloat16
        )
        normed_ref[:, at] = value
        crossed[:, pl.ds(pl.multiple_of(place_turned * rows, rows), rows)] = value
        return carry

    lax.fori_loop(0, model // rows, normalize, 0)
    sums[...] = jnp.zeros_like(sums)

    def accumulate(t, carry):
        @pl.when(t == last)
        def _():
            for stream in range(4):
                for k in range(SIDE):
                    large(stream, last - 1, k).wait_recv()

        for stream in range(4):
            buffer, far, columns = place(stream, t)
            kind, count = stream // 2, columns.stop - columns.start
            deep = SIDE * rows
            at = pl.ds(pl.multiple_of(far * deep, deep), deep)
            block = buffer[far, :, :, columns].reshape(deep, count)
            sums[kind, :, columns] += dot((normed_ref, crossed)[kind][:, at], block)
        return carry

    lax.fori_loop(0, SIDE, accumulate, 0)

    def gating(n, carry):
        at = pl.ds(pl.multiple_of(n * slots, slots), slots)
        gate_pre, up_pre = sums[0, at], sums[1, at]
        sigmoid_gate = jax.nn.sigmoid(gate_pre)
        swish = gate_pre * sigmoid_gate
        cotangent = cotangent_ref[at, :].astype(jnp.float32)
        hidden_ref[at, :] = (swish * up_pre).astype(jnp.bfloat16)
        grads_ref[at, 0:units] = (
            cotangent * up_pre * sigmoid_gate * (1.0 + gate_pre * (1.0 - sigmoid_gate))
        ).astype(jnp.bfloat16)
        grads_ref[at, units : 2 * units] = (cotangent * swish).astype(jnp.bfloat16)
        return carry

    lax.fori_loop(0, groups, gating, 0)

    for copy in (*to_next, *to_after):
        copy.wait_send()
    for stream in range(4):
        for k in range(SIDE):
            if k < last:
                small(stream, k).wait_send()
            for t in range(last):
                large(stream, t, k).wait_send()
    for part in range(2):
        for by in range(SIDE):
            if by > 0:
                x_send(by, part).wait_send()
            core_send(by, part).wait_send()


def layer(
    states_ref,
    lengths_ref,
    offsets_ref,
    count_ref,
    gain_ref,
    cotangent_ref,
    gate_hbm,
    up_hbm,
    query_hbm,
    key_hbm,
    value_hbm,
    proj_hbm,
    hidden_ref,
    gate_ref,
    up_ref,
    patch_ref,
    own_features,
    grads,
    normed,
    gates,
    ups,
    earlier,
    contexts,
    *semaphores,
):
    half, full = jnp.bfloat16, jnp.float32
    length, width = states_ref.shape
    rows, units = gate_hbm.shape
    tokens, model = normed.shape
    slots = patch_ref.shape[0]
    chunks, wide = 8, model // 8
    block = (rows // 2, units)

    def first_scope(maps, crossed, sums, queries, keys, values, bias, mixed, pooled):
        front(
            states_ref,
            lengths_ref,
            offsets_ref,
            count_ref,
            gain_ref,
            cotangent_ref,
            gate_hbm,
            up_hbm,
            query_hbm,
            key_hbm,
            value_hbm,
            proj_hbm,
            own_features,
            hidden_ref,
            grads,
            normed,
            gates,
            ups,
            maps,
            crossed,
            sums,
            earlier,
            queries,
            keys,
            values,
            bias,
            mixed,
            pooled,
            contexts,
            *semaphores[:11],
        )

    pl.run_scoped(
        first_scope,
        pltpu.VMEM((width, model), half),
        pltpu.VMEM((tokens, model), half),
        pltpu.VMEM((2, tokens, units), full),
        pltpu.VMEM((length, width), half),
        pltpu.VMEM((3 * length, width), half),
        pltpu.VMEM((3 * length, width), half),
        pltpu.VMEM((length // HEAD, HEAD, WINDOW + HEAD), full),
        pltpu.VMEM((length, width), half),
        pltpu.VMEM((slots, width), half),
    )

    def second_scope(*scratch):
        grad_rings(
            normed,
            grads,
            own_features,
            gain_ref,
            gates,
            ups,
            gate_ref,
            up_ref,
            patch_ref,
            *scratch,
            *semaphores[11:],
        )

    pl.run_scoped(
        second_scope,
        pltpu.VMEM((chunks, slots, wide), full),
        pltpu.VMEM((4, SIDE, *block), half),
        pltpu.VMEM((4, SIDE - 1, SIDE, *block), half),
        pltpu.VMEM((4, *block), half),
        pltpu.VMEM((4, SIDE - 1, *block), half),
        pltpu.VMEM((chunks, 2, SIDE, slots, wide), half),
        pltpu.VMEM((chunks, SIDE, slots, wide), half),
        pltpu.VMEM((SIDE - 1, chunks, slots, wide), half),
    )


def whole_layer(
    states, lengths, offsets, count, gain, cotangent, gate_w, up_w, squares, w_proj
):
    length, width = states.shape
    slots = offsets.shape[1]
    rows, units = gate_w.shape
    model = w_proj.shape[1]
    tokens = 2 * SIDE * slots
    chunks = 8
    dma = pltpu.SemaphoreType.DMA
    whole = pl.BlockSpec(memory_space=pltpu.VMEM)
    anywhere = pl.BlockSpec(memory_space=pl.ANY)
    half, full = jnp.bfloat16, jnp.float32
    return pl.pallas_call(
        layer,
        out_shape=(
            jax.ShapeDtypeStruct((tokens, units), half),
            jax.ShapeDtypeStruct((rows, units), full),
            jax.ShapeDtypeStruct((rows, units), full),
            jax.ShapeDtypeStruct((slots, model), full),
        ),
        in_specs=[whole] * 6 + [anywhere] * 6,
        out_specs=(whole,) * 4,
        scratch_shapes=[
            pltpu.VMEM((slots, model), half),
            pltpu.VMEM((tokens, 2 * units), half),
            pltpu.VMEM((tokens, model), half),
            pltpu.VMEM((SIDE, SIDE, rows, units), half),
            pltpu.VMEM((SIDE, SIDE, rows, units), half),
            pltpu.VMEM((2 * length, width), half),
            pltpu.VMEM((tokens, width), half),
            dma((6,)),
            dma((4, SIDE - 1)),
            dma((4, SIDE - 1)),
            dma((4, SIDE - 1, SIDE)),
            dma((4, SIDE - 1, SIDE)),
            dma((4,)),
            dma((4,)),
            dma((2, SIDE - 1)),
            dma((2, SIDE - 1)),
            dma((2, SIDE)),
            dma((2, SIDE)),
            dma((4, SIDE - 1, SIDE)),
            dma((4, SIDE - 1, SIDE)),
            dma((4, SIDE - 1)),
            dma((4, SIDE - 1)),
            dma((chunks,)),
            dma((chunks,)),
            dma((SIDE - 1, chunks)),
            dma((SIDE - 1, chunks)),
            pltpu.SemaphoreType.REGULAR,
        ],
        compiler_params=pltpu.CompilerParams(
            collective_id=0, has_side_effects=True, vmem_limit_bytes=62 * 1024 * 1024
        ),
        name="layer",
    )(states, lengths, offsets, count, gain, cotangent, gate_w, up_w, *squares, w_proj)


def deliver(*refs):
    count = len(refs) // 3
    sources, targets = refs[:count], refs[count : 2 * count]
    buffers, got, put = refs[2 * count : 3 * count], refs[-2], refs[-1]
    inward = [
        pltpu.make_async_copy(sources[i], buffers[i], got.at[i]) for i in range(count)
    ]
    outward = [
        pltpu.make_async_copy(buffers[i], targets[i], put.at[i]) for i in range(count)
    ]
    for copy in inward:
        copy.start()
    for before, after in zip(inward, outward):
        before.wait()
        after.start()
    for copy in outward:
        copy.wait()


def delivered(arrays):
    anywhere = pl.BlockSpec(memory_space=pl.ANY)
    return pl.pallas_call(
        deliver,
        out_shape=tuple(jax.ShapeDtypeStruct(a.shape, a.dtype) for a in arrays),
        in_specs=[anywhere] * len(arrays),
        out_specs=(anywhere,) * len(arrays),
        scratch_shapes=[pltpu.VMEM(a.shape, a.dtype) for a in arrays]
        + [pltpu.SemaphoreType.DMA((len(arrays),))] * 2,
        name="deliver",
    )(*arrays)


def shards(
    bytes_in,
    doc_lengths,
    patch_offsets,
    patch_counts,
    w_query,
    w_key,
    w_value,
    w_proj,
    norm_gain,
    gate_w,
    up_w,
    d_hidden,
):
    units = gate_w.shape[1]
    results = whole_layer(
        bytes_in[0],
        doc_lengths[None],
        patch_offsets,
        patch_counts,
        norm_gain[None],
        d_hidden.reshape(-1, units),
        gate_w,
        up_w,
        (w_query, w_key, w_value),
        w_proj,
    )
    hidden, grad_gate, grad_up, patch_grad = delivered(results)
    return (hidden.reshape(d_hidden.shape), grad_gate, grad_up, patch_grad[None])


def solution(mesh):
    return jax.shard_map(
        shards,
        mesh=mesh,
        in_specs=(
            P("seq", "fsdp", None),
            P(),
            P("seq", "fsdp"),
            P("seq", "fsdp"),
            P(),
            P(),
            P(),
            P(),
            P(),
            P("fsdp", "seq"),
            P("fsdp", "seq"),
            P(None, "fsdp", "seq"),
        ),
        out_specs=(
            P(None, "fsdp", "seq"),
            P("fsdp", "seq"),
            P("fsdp", "seq"),
            P("seq", "fsdp", None),
        ),
        check_vma=False,
    )
```

```python
import math

import jax
import jax.numpy as jnp
from jax import lax
from jax.experimental import pallas as pl
from jax.experimental.pallas import tpu as pltpu
from jax.sharding import PartitionSpec as P

HEAD = 128
WINDOW = 512


epsilon = 1e-05
masked_score = -1e30


MESH = pl.DeviceIdType.MESH
SIDE = 4


def wrapped(value):
    return lax.rem(value + 2 * SIDE, SIDE)


def grad_rings(
    normed_ref,
    grads_ref,
    features_ref,
    gain_ref,
    gates,
    ups,
    gate_ref,
    up_ref,
    patch_ref,
    inward,
    first,
    arrived,
    second,
    crossed,
    parts,
    paired,
    ringed,
    put,
    got,
    put2,
    got2,
    put3,
    got3,
    put4,
    got4,
    ready,
):
    seq = lax.axis_index("seq")
    spot = lax.axis_index("fsdp")
    x, core = lax.div(seq, 2), lax.rem(seq, 2)
    z, y = lax.div(spot, SIDE), lax.rem(spot, SIDE)
    rows = first.shape[2]
    units = gate_ref.shape[1]
    chunks, _, _, slots, wide = parts.shape

    around = (
        (seq, wrapped(z + 1) * SIDE + y),
        (seq, wrapped(z - 1) * SIDE + y),
        (seq, z * SIDE + wrapped(y + 1)),
        (seq, z * SIDE + wrapped(y - 1)),
        (wrapped(x + 1) * 2 + core, spot),
        (wrapped(x - 1) * 2 + core, spot),
        (x * 2 + 1 - core, spot),
    )
    for neighbour in around:
        pl.semaphore_signal(ready, inc=1, device_id=neighbour, device_id_type=MESH)

    def place(stream):
        kind, half = stream // 2, stream % 2
        step = 1 - 2 * half
        along, across = (z, y) if kind == 0 else (y, z)
        if kind == 0:
            onward, sideways = around[half], around[2 + half]
        else:
            onward, sideways = around[2 + half], around[half]
        return kind, half, step, along, across, onward, sideways

    def own(stream, t, k):
        kind, half, step, along, across, _, _ = place(stream)
        far = wrapped(along - step * (1 + t))
        near = wrapped(across - step * (1 + k))
        zb, yb = (far, near) if kind == 0 else (near, far)
        at = pl.multiple_of((zb * SIDE + yb) * 2 * rows + half * rows, rows)
        return lax.dot_general(
            normed_ref[:, pl.ds(at, rows)],
            grads_ref[:, kind * units : (kind + 1) * units],
            (((0,), (0,)), ((), ())),
            preferred_element_type=jnp.float32,
        )

    def hop(stream, source, t, k):
        return pltpu.make_async_remote_copy(
            src_ref=source,
            dst_ref=arrived.at[stream, t, k],
            send_sem=put.at[stream, t, k],
            recv_sem=got.at[stream, t, k],
            device_id=place(stream)[5],
            device_id_type=MESH,
        )

    def hop2(stream, source, k):
        return pltpu.make_async_remote_copy(
            src_ref=source,
            dst_ref=crossed.at[stream, k],
            send_sem=put2.at[stream, k],
            recv_sem=got2.at[stream, k],
            device_id=place(stream)[6],
            device_id_type=MESH,
        )

    def across_cores(n):
        return pltpu.make_async_remote_copy(
            src_ref=parts.at[n, 1 - core],
            dst_ref=paired.at[n],
            send_sem=put3.at[n],
            recv_sem=got3.at[n],
            device_id=around[6],
            device_id_type=MESH,
        )

    def x_hop(side, n, source, t):
        return pltpu.make_async_remote_copy(
            src_ref=source,
            dst_ref=ringed.at[t, n],
            send_sem=put4.at[t, n],
            recv_sem=got4.at[t, n],
            device_id=around[4 + side],
            device_id_type=MESH,
        )

    def input_part(n):
        depth = 2 * rows
        for column in range(wide // depth):
            zb, yb = lax.div(n, 2), 2 * lax.rem(n, 2) + column
            value = 0.0
            for kind, block in enumerate((gates[zb, yb], ups[yb, zb])):
                value += lax.dot_general(
                    grads_ref[:, kind * units : (kind + 1) * units],
                    block,
                    (((1,), (1,)), ((), ())),
                    preferred_element_type=jnp.float32,
                )
            value = value.astype(jnp.bfloat16)
            for block in range(2 * SIDE):
                parts[n, block % 2, block // 2, :, column * depth : (column + 1) * depth] = (
                    value[block * slots : (block + 1) * slots]
                )
        across_cores(n).start()

    def x_phase(t):
        def body(m, carry):
            for side in range(2):
                n = 2 * m + side
                block = wrapped(x - (1 - 2 * side) * (1 + t))
                if t == 0:
                    across_cores(n).wait_recv()
                    paired[n] = (
                        paired[n].astype(jnp.float32) + parts[n, core].astype(jnp.float32)
                    ).astype(jnp.bfloat16)
                    x_hop(side, n, paired.at[n, block], 0).start()
                else:
                    x_hop(side, n, paired.at[n, block], t - 1).wait_recv()
                    value = ringed[t - 1, n].astype(jnp.float32) + paired[n, block].astype(
                        jnp.float32
                    )
                    if t < SIDE - 1:
                        ringed[t - 1, n] = value.astype(jnp.bfloat16)
                        x_hop(side, n, ringed.at[t - 1, n], t).start()
                    else:
                        inward[n] = value
            return carry

        lax.fori_loop(0, chunks // 2, body, 0)

    last = SIDE - 1

    def total(stream, k):
        value = own(stream, last, k)
        hop(stream, first.at[stream, k], last - 1, k).wait_recv()
        return value + arrived[stream, last - 1, k].astype(jnp.float32)

    def wave(number, carry):
        @pl.when((number > 0) & (number < SIDE))
        def _():
            for stream in range(4):
                first[stream, number] = own(stream, 0, number).astype(jnp.bfloat16)
                hop(stream, first.at[stream, number], 0, number).start()

        for t in (1, 2):

            @pl.when((number >= t) & (number < t + SIDE))
            def _(t=t):
                k = number - t
                for stream in range(4):
                    value = own(stream, t, k)
                    hop(stream, first.at[stream, k], t - 1, k).wait_recv()
                    arrived[stream, t - 1, k] = (
                        value + arrived[stream, t - 1, k].astype(jnp.float32)
                    ).astype(jnp.bfloat16)
                    hop(stream, arrived.at[stream, t - 1, k], t, k).start()

        @pl.when(number == last)
        def _():
            for stream in range(4):
                second[stream] = total(stream, 0).astype(jnp.bfloat16)
                hop2(stream, second.at[stream], 0).start()

        @pl.when(number > last)
        def _():
            k = number - last
            for stream in range(4):
                value = total(stream, k)
                hop2(stream, second.at[stream], k - 1).wait_recv()
                crossed[stream, k - 1] = (
                    value + crossed[stream, k - 1].astype(jnp.float32)
                ).astype(jnp.bfloat16)
                hop2(stream, crossed.at[stream, k - 1], k).start()

        @pl.when((number == 1) | (number == 2))
        def _():
            def part_of(index, inner):
                input_part(index)
                return inner

            lax.fori_loop((number - 1) * SIDE, number * SIDE, part_of, 0)

        for phase in range(last):

            @pl.when(number == last + phase)
            def _(phase=phase):
                x_phase(phase)

        return carry

    for stream in range(4):
        first[stream, 0] = own(stream, 0, 0).astype(jnp.bfloat16)
    pl.semaphore_wait(ready, len(around))
    for stream in range(4):
        hop(stream, first.at[stream, 0], 0, 0).start()
    lax.fori_loop(1, 2 * last, wave, 0)
    x_phase(last)

    def columns_of(n):
        at = pl.ds(pl.multiple_of(n * wide, wide), wide)
        return at, features_ref[:, at].astype(jnp.float32), gain_ref[:, at] * inward[n]

    def means(n, carry):
        _, features, scaled = columns_of(n)
        return (
            carry[0] + jnp.sum(features * features, axis=1, keepdims=True),
            carry[1] + jnp.sum(features * scaled, axis=1, keepdims=True),
        )

    nothing = jnp.zeros((slots, 1), jnp.float32)
    squares, products = lax.fori_loop(0, chunks, means, (nothing, nothing))
    inverse = lax.rsqrt(squares / (chunks * wide) + epsilon)
    factor = inverse * inverse * inverse * (products / (chunks * wide))

    def patch_part(n, carry):
        at, features, scaled = columns_of(n)
        patch_ref[:, at] = inverse * scaled - features * factor
        return carry

    lax.fori_loop(0, chunks, patch_part, 0)

    for stream in range(4):
        kind, half = stream // 2, stream % 2
        value = total(stream, last)
        hop2(stream, second.at[stream], last - 1).wait_recv()
        (gate_ref, up_ref)[kind][half * rows : (half + 1) * rows, :] = value + crossed[
            stream, last - 1
        ].astype(jnp.float32)

    def sent(index, carry):
        t, k = lax.div(index, SIDE), lax.rem(index, SIDE)
        for stream in range(4):
            hop(stream, first.at[stream, k], t, k).wait_send()
        return carry

    lax.fori_loop(0, last * SIDE, sent, 0)
    for stream in range(4):
        for k in range(last):
            hop2(stream, second.at[stream], k).wait_send()

    def x_sent(m, carry):
        for side in range(2):
            n = 2 * m + side
            across_cores(n).wait_send()
            for t in range(last):
                x_hop(side, n, ringed.at[0, n], t).wait_send()
        return carry

    lax.fori_loop(0, chunks // 2, x_sent, 0)


ORDER = (
    "a0 b00",
    "A0 a1 b01",
    "B00 b10",
    "A1 a2 b02",
    "B01 b11",
    "A2 b03",
    "B10 b20",
    "B02 b12",
    "B11 b21",
    "B03 b13",
    "B12 b22",
    "B13 b23"
)


def front(
    states_ref,
    lengths_ref,
    offsets_ref,
    count_ref,
    gain_ref,
    cotangent_ref,
    gate_hbm,
    up_hbm,
    query_hbm,
    key_hbm,
    value_hbm,
    proj_hbm,
    own_features_ref,
    hidden_ref,
    grads_ref,
    normed_ref,
    gates,
    ups,
    maps,
    crossed,
    sums,
    earlier,
    queries,
    keys,
    values,
    bias,
    mixed,
    pooled,
    contexts,
    loads,
    put_a,
    got_a,
    put_b,
    got_b,
    put_s,
    got_s,
    put_x,
    got_x,
    put_c,
    got_c,
):
    seq = lax.axis_index("seq")
    spot = lax.axis_index("fsdp")
    x, core = lax.div(seq, 2), lax.rem(seq, 2)
    z, y = lax.div(spot, SIDE), lax.rem(spot, SIDE)
    groups, spots = 2 * SIDE, SIDE * SIDE
    devices = groups * spots
    length, width = states_ref.shape
    slots = offsets_ref.shape[1]
    heads = width // HEAD
    units = gate_hbm.shape[1]
    rows = gate_hbm.shape[0]
    model = proj_hbm.shape[1]
    ranges = (slice(0, 3 * HEAD), slice(3 * HEAD, units))

    def device_of(position):
        position = lax.rem(position + devices, devices)
        return lax.div(position, spots), lax.rem(position, spots)

    here = seq * spots + spot
    around = (
        (seq, wrapped(z + 1) * SIDE + y),
        (seq, wrapped(z - 1) * SIDE + y),
        (seq, z * SIDE + wrapped(y + 1)),
        (seq, z * SIDE + wrapped(y - 1)),
    )
    next_block = device_of(here + 1)
    after_next = device_of(here + 2)
    other_core = (x * 2 + 1 - core, spot)
    along_x = tuple((wrapped(x + by) * 2 + core, spot) for by in range(1, SIDE))

    places = [
        (gates.at[z, y], gate_hbm),
        (ups.at[y, z], up_hbm),
        (maps.at[:, 0:width], query_hbm),
        (maps.at[:, width : 2 * width], key_hbm),
        (maps.at[:, 2 * width : 3 * width], value_hbm),
        (maps, proj_hbm),
    ]
    load = [
        pltpu.make_async_copy(source, target, loads.at[i])
        for i, (target, source) in enumerate(places)
    ]
    for copy in load[:2]:
        copy.start()

    greeted = (
        *around,
        next_block,
        device_of(here - 1),
        other_core,
        *along_x,
    )
    barrier = pltpu.get_barrier_semaphore()
    for neighbour in greeted:
        pl.semaphore_signal(barrier, inc=1, device_id=neighbour, device_id_type=MESH)
    pl.semaphore_wait(barrier, len(greeted))

    def remote(source, target, sent, arrived, device):
        return pltpu.make_async_remote_copy(
            src_ref=source,
            dst_ref=target,
            send_sem=sent,
            recv_sem=arrived,
            device_id=device,
            device_id_type=MESH,
        )

    recent = earlier.at[length : 2 * length]
    oldest = earlier.at[0:length]
    halves = [slice(p * length // 2, (p + 1) * length // 2) for p in range(2)]
    to_next = [
        remote(states_ref.at[at], recent.at[at], put_s.at[p], got_s.at[p], next_block)
        for p, at in enumerate(halves)
    ]
    to_after = [
        remote(recent.at[at], oldest.at[at], put_s.at[2 + p], got_s.at[2 + p], next_block)
        for p, at in enumerate(halves)
    ]
    for copy in to_next:
        copy.start()
    load[0].wait()
    load[1].wait()

    def place(stream, t):
        kind, half = stream // 2, stream % 2
        along = z if kind == 0 else y
        return (gates, ups)[kind], wrapped(along - (1 - 2 * half) * t), ranges[half]

    def piece(stream, t, k):
        kind, half = stream // 2, stream % 2
        across = y if kind == 0 else z
        buffer, far, columns = place(stream, t)
        return buffer.at[far, wrapped(across - (1 - 2 * half) * k), :, columns]

    def small(stream, k):
        kind, half = stream // 2, stream % 2
        device = around[2 + half] if kind == 0 else around[half]
        region = piece(stream, 0, k)
        return remote(region, region, put_a.at[stream, k], got_a.at[stream, k], device)

    def large(stream, t, k):
        kind, half = stream // 2, stream % 2
        device = around[half] if kind == 0 else around[2 + half]
        region = piece(stream, t, k)
        return remote(
            region, region, put_b.at[stream, t, k], got_b.at[stream, t, k], device
        )

    last = SIDE - 1

    steps = {
        "a": lambda stream, k: small(stream, k).start(),
        "A": lambda stream, k: small(stream, k).wait_recv(),
        "b": lambda stream, t, k: large(stream, t, k).start(),
        "B": lambda stream, t, k: large(stream, t, k).wait_recv(),
    }

    def tick(number):
        for stream in range(4):
            for step in ORDER[number].split():
                steps[step[0]](stream, *(int(digit) for digit in step[1:]))

    tick(0)
    for copy in load[2:5]:
        copy.start()

    chunk = 2 * HEAD
    scale = 1.0 / math.sqrt(HEAD)

    def dot(a, b):
        return jnp.dot(a, b, preferred_element_type=jnp.float32)

    def dot_t(a, b):
        return lax.dot_general(
            a, b, (((1,), (1,)), ((), ())), preferred_element_type=jnp.float32
        )

    load[2].wait()

    def make_queries(n, carry):
        at = pl.ds(pl.multiple_of(n * chunk, chunk), chunk)
        queries[:, at] = dot(states_ref[...], maps[:, at]).astype(jnp.bfloat16)
        return carry

    lax.fori_loop(0, width // chunk, make_queries, 0)
    tick(1)
    for before, after in zip(to_next, to_after):
        before.wait_recv()
        after.start()
    tick(2)
    load[3].wait()
    load[4].wait()

    def keys_and_values(source, row):
        def body(n, carry):
            at = pl.ds(pl.multiple_of(n * chunk, chunk), chunk)
            key_at = pl.ds(pl.multiple_of(width + n * chunk, chunk), chunk)
            value_at = pl.ds(pl.multiple_of(2 * width + n * chunk, chunk), chunk)
            into = slice(row, row + length)
            keys[into, at] = dot(source[...], maps[:, key_at]).astype(jnp.bfloat16)
            values[into, at] = dot(source[...], maps[:, value_at]).astype(jnp.bfloat16)
            return carry

        lax.fori_loop(0, width // chunk, body, 0)

    keys_and_values(states_ref, 2 * length)
    tick(3)

    span = WINDOW + HEAD
    parts = length // HEAD

    def iota(shape, dim):
        return lax.broadcasted_iota(jnp.int32, shape, dim)

    def turned(line, by):
        count = line.shape[1]
        picked = iota((count, count), 1) == iota((count, count), 0) + by
        return jnp.sum(jnp.where(picked, line, 0.0), axis=1, keepdims=True)

    docs = lengths_ref.shape[1]
    lengths = lengths_ref[...].astype(jnp.float32)
    earlier_docs = iota((docs, docs), 1) < iota((docs, docs), 0)
    start_column = jnp.sum(jnp.where(earlier_docs, lengths, 0.0), axis=1, keepdims=True)
    same = iota((docs, docs), 1) == iota((docs, docs), 0)
    start_line = jnp.sum(jnp.where(same, start_column, 0.0), axis=0, keepdims=True)
    key_pos = (here - 2) * length + iota((docs, 3 * length), 1)
    query_pos = here * length + iota((length, docs), 0)
    key_doc = jnp.sum(
        jnp.where(start_column <= key_pos.astype(jnp.float32), 1.0, 0.0), axis=0, keepdims=True
    )
    query_doc = jnp.sum(
        jnp.where(start_line <= query_pos.astype(jnp.float32), 1.0, 0.0), axis=1, keepdims=True
    )
    for r in range(parts):
        row = lax.broadcasted_iota(jnp.int32, (HEAD, span), 0)
        column = lax.broadcasted_iota(jnp.int32, (HEAD, span), 1)
        allowed = (column > row) & (column <= row + WINDOW)
        start = 2 * length - WINDOW + r * HEAD
        allowed = allowed & (
            key_doc[:, start : start + span] == query_doc[r * HEAD : (r + 1) * HEAD, :]
        )
        bias[r] = jnp.where(allowed, 0.0, masked_score)

    keys_and_values(recent, length)
    tick(4)
    offsets = offsets_ref[...].astype(jnp.float32)
    count = count_ref[...].astype(jnp.float32)
    slot = iota((slots, 1), 0).astype(jnp.float32)
    present = slot < count
    begins = turned(offsets, 0)
    ends = jnp.where((slot == count - 1.0) | (slot == slots - 1.0), 1.0 * length, turned(offsets, 1))
    begins, ends = jnp.where(present, begins, 0.0), jnp.where(present, ends, 0.0)
    byte = iota((slots, length), 1).astype(jnp.float32)
    member = (byte >= begins) & (byte < ends)
    ones = jnp.where(member, 1.0, 0.0)
    pool_bias = jnp.where(member, 0.0, masked_score)
    sizes = jnp.maximum(jnp.sum(ones, axis=1, keepdims=True), 1.0)
    members = ones.astype(jnp.bfloat16)
    tick(5)
    for copy in to_after:
        copy.wait_recv()
    keys_and_values(oldest, 0)
    load[5].start()
    tick(6)

    def attend(h, carry):
        at = pl.ds(pl.multiple_of(h * HEAD, HEAD), HEAD)
        for r in range(parts):
            here_rows = slice(r * HEAD, (r + 1) * HEAD)
            start = 2 * length - WINDOW + r * HEAD
            scores = dot_t(queries[here_rows, at], keys[start : start + span, at])
            scores = scores * scale + bias[r]
            weights = jnp.exp(scores - jnp.max(scores, axis=1, keepdims=True))
            total = jnp.sum(weights, axis=1, keepdims=True)
            summed = dot(weights.astype(jnp.bfloat16), values[start : start + span, at])
            mixed[here_rows, at] = (
                states_ref[here_rows, at].astype(jnp.float32) + summed / total
            ).astype(jnp.bfloat16)
        return carry

    mine = pl.ds(pl.multiple_of(seq * slots, slots), slots)

    def pool(h, carry):
        at = pl.ds(pl.multiple_of(h * HEAD, HEAD), HEAD)
        scores = dot_t(pooled[:, at], mixed[:, at]) * scale + pool_bias
        weights = jnp.exp(scores - jnp.max(scores, axis=1, keepdims=True))
        total = jnp.sum(weights, axis=1, keepdims=True)
        summed = dot(weights.astype(jnp.bfloat16), mixed[:, at]) / total
        contexts[mine, at] = jnp.where(present, summed, 0.0).astype(jnp.bfloat16)
        return carry

    def context_of(group, part):
        at = pl.ds(pl.multiple_of(group * slots, slots), slots)
        return contexts.at[at, part * width // 2 : (part + 1) * width // 2]

    def x_send(by, part):
        region = context_of(seq, part)
        return remote(
            region,
            region,
            put_x.at[part, by - 1],
            got_x.at[part, by - 1],
            along_x[by - 1],
        )

    def core_send(by, part):
        region = context_of(wrapped(x - by) * 2 + core, part)
        return remote(
            region, region, put_c.at[part, by], got_c.at[part, by], other_core
        )

    for part in range(2):
        first_head, stop_head = part * heads // 2, (part + 1) * heads // 2
        some = slice(first_head * HEAD, stop_head * HEAD)
        lax.fori_loop(first_head, stop_head, attend, 0)
        pooled[:, some] = (dot(members, mixed[:, some]) / sizes).astype(jnp.bfloat16)
        lax.fori_loop(first_head, stop_head, pool, 0)
        for by in range(1, SIDE):
            x_send(by, part).start()
        core_send(0, part).start()
        tick(7 + part)
    tick(9)
    for part in range(2):
        for by in (1, 3, 2):
            x_send(by, part).wait_recv()
            core_send(by, part).start()
        if part == 0:
            tick(10)
    for part in range(2):
        for by in range(SIDE):
            core_send(by, part).wait_recv()
    load[5].wait()

    wide = 4 * HEAD

    def project(n, squares):
        at = pl.ds(pl.multiple_of(n * wide, wide), wide)
        features = dot(contexts[...], maps[:, at]).astype(jnp.bfloat16)
        normed_ref[:, at] = features
        full = features.astype(jnp.float32)
        return squares + jnp.sum(full * full, axis=1, keepdims=True)

    squares = jnp.zeros((groups * slots, 1), jnp.float32)
    squares = lax.fori_loop(0, model // wide // 2, project, squares)
    tick(11)
    squares = lax.fori_loop(model // wide // 2, model // wide, project, squares)
    inverse = lax.rsqrt(squares / model + epsilon)
    own_features_ref[...] = normed_ref[mine, :]

    def normalize(n, carry):
        at = pl.ds(pl.multiple_of(n * rows, rows), rows)
        place_turned = (n % SIDE) * SIDE + n // SIDE
        value = (normed_ref[:, at].astype(jnp.float32) * inverse * gain_ref[:, at]).astype(
            jnp.bfloat16
        )
        normed_ref[:, at] = value
        crossed[:, pl.ds(pl.multiple_of(place_turned * rows, rows), rows)] = value
        return carry

    lax.fori_loop(0, model // rows, normalize, 0)
    sums[...] = jnp.zeros_like(sums)

    def accumulate(t, carry):
        @pl.when(t == last)
        def _():
            for stream in range(4):
                for k in range(SIDE):
                    large(stream, last - 1, k).wait_recv()

        for stream in range(4):
            buffer, far, columns = place(stream, t)
            kind, count = stream // 2, columns.stop - columns.start
            deep = SIDE * rows
            at = pl.ds(pl.multiple_of(far * deep, deep), deep)
            block = buffer[far, :, :, columns].reshape(deep, count)
            sums[kind, :, columns] += dot((normed_ref, crossed)[kind][:, at], block)
        return carry

    lax.fori_loop(0, SIDE, accumulate, 0)

    def gating(n, carry):
        at = pl.ds(pl.multiple_of(n * slots, slots), slots)
        gate_pre, up_pre = sums[0, at], sums[1, at]
        sigmoid_gate = jax.nn.sigmoid(gate_pre)
        swish = gate_pre * sigmoid_gate
        cotangent = cotangent_ref[at, :].astype(jnp.float32)
        hidden_ref[at, :] = (swish * up_pre).astype(jnp.bfloat16)
        grads_ref[at, 0:units] = (
            cotangent * up_pre * sigmoid_gate * (1.0 + gate_pre * (1.0 - sigmoid_gate))
        ).astype(jnp.bfloat16)
        grads_ref[at, units : 2 * units] = (cotangent * swish).astype(jnp.bfloat16)
        return carry

    lax.fori_loop(0, groups, gating, 0)

    for copy in (*to_next, *to_after):
        copy.wait_send()
    for stream in range(4):
        for k in range(SIDE):
            if k < last:
                small(stream, k).wait_send()
            for t in range(last):
                large(stream, t, k).wait_send()
    for part in range(2):
        for by in range(SIDE):
            if by > 0:
                x_send(by, part).wait_send()
            core_send(by, part).wait_send()


def layer(
    states_ref,
    lengths_ref,
    offsets_ref,
    count_ref,
    gain_ref,
    cotangent_ref,
    gate_hbm,
    up_hbm,
    query_hbm,
    key_hbm,
    value_hbm,
    proj_hbm,
    hidden_ref,
    gate_ref,
    up_ref,
    patch_ref,
    own_features,
    grads,
    normed,
    gates,
    ups,
    earlier,
    contexts,
    *semaphores,
):
    half, full = jnp.bfloat16, jnp.float32
    length, width = states_ref.shape
    rows, units = gate_hbm.shape
    tokens, model = normed.shape
    slots = patch_ref.shape[0]
    chunks, wide = 8, model // 8
    block = (rows // 2, units)

    def first_scope(maps, crossed, sums, queries, keys, values, bias, mixed, pooled):
        front(
            states_ref,
            lengths_ref,
            offsets_ref,
            count_ref,
            gain_ref,
            cotangent_ref,
            gate_hbm,
            up_hbm,
            query_hbm,
            key_hbm,
            value_hbm,
            proj_hbm,
            own_features,
            hidden_ref,
            grads,
            normed,
            gates,
            ups,
            maps,
            crossed,
            sums,
            earlier,
            queries,
            keys,
            values,
            bias,
            mixed,
            pooled,
            contexts,
            *semaphores[:11],
        )

    pl.run_scoped(
        first_scope,
        pltpu.VMEM((width, model), half),
        pltpu.VMEM((tokens, model), half),
        pltpu.VMEM((2, tokens, units), full),
        pltpu.VMEM((length, width), half),
        pltpu.VMEM((3 * length, width), half),
        pltpu.VMEM((3 * length, width), half),
        pltpu.VMEM((length // HEAD, HEAD, WINDOW + HEAD), full),
        pltpu.VMEM((length, width), half),
        pltpu.VMEM((slots, width), half),
    )

    def second_scope(*scratch):
        grad_rings(
            normed,
            grads,
            own_features,
            gain_ref,
            gates,
            ups,
            gate_ref,
            up_ref,
            patch_ref,
            *scratch,
            *semaphores[11:],
        )

    pl.run_scoped(
        second_scope,
        pltpu.VMEM((chunks, slots, wide), full),
        pltpu.VMEM((4, SIDE, *block), half),
        pltpu.VMEM((4, SIDE - 1, SIDE, *block), half),
        pltpu.VMEM((4, *block), half),
        pltpu.VMEM((4, SIDE - 1, *block), half),
        pltpu.VMEM((chunks, 2, SIDE, slots, wide), half),
        pltpu.VMEM((chunks, SIDE, slots, wide), half),
        pltpu.VMEM((SIDE - 1, chunks, slots, wide), half),
    )


def whole_layer(
    states, lengths, offsets, count, gain, cotangent, gate_w, up_w, squares, w_proj
):
    length, width = states.shape
    slots = offsets.shape[1]
    rows, units = gate_w.shape
    model = w_proj.shape[1]
    tokens = 2 * SIDE * slots
    chunks = 8
    dma = pltpu.SemaphoreType.DMA
    whole = pl.BlockSpec(memory_space=pltpu.VMEM)
    anywhere = pl.BlockSpec(memory_space=pl.ANY)
    half, full = jnp.bfloat16, jnp.float32
    return pl.pallas_call(
        layer,
        out_shape=(
            jax.ShapeDtypeStruct((tokens, units), half),
            jax.ShapeDtypeStruct((rows, units), full),
            jax.ShapeDtypeStruct((rows, units), full),
            jax.ShapeDtypeStruct((slots, model), full),
        ),
        in_specs=[whole] * 6 + [anywhere] * 6,
        out_specs=(whole,) * 4,
        scratch_shapes=[
            pltpu.VMEM((slots, model), half),
            pltpu.VMEM((tokens, 2 * units), half),
            pltpu.VMEM((tokens, model), half),
            pltpu.VMEM((SIDE, SIDE, rows, units), half),
            pltpu.VMEM((SIDE, SIDE, rows, units), half),
            pltpu.VMEM((2 * length, width), half),
            pltpu.VMEM((tokens, width), half),
            dma((6,)),
            dma((4, SIDE - 1)),
            dma((4, SIDE - 1)),
            dma((4, SIDE - 1, SIDE)),
            dma((4, SIDE - 1, SIDE)),
            dma((4,)),
            dma((4,)),
            dma((2, SIDE - 1)),
            dma((2, SIDE - 1)),
            dma((2, SIDE)),
            dma((2, SIDE)),
            dma((4, SIDE - 1, SIDE)),
            dma((4, SIDE - 1, SIDE)),
            dma((4, SIDE - 1)),
            dma((4, SIDE - 1)),
            dma((chunks,)),
            dma((chunks,)),
            dma((SIDE - 1, chunks)),
            dma((SIDE - 1, chunks)),
            pltpu.SemaphoreType.REGULAR,
        ],
        compiler_params=pltpu.CompilerParams(
            collective_id=0, has_side_effects=True, vmem_limit_bytes=62 * 1024 * 1024
        ),
        name="layer",
    )(states, lengths, offsets, count, gain, cotangent, gate_w, up_w, *squares, w_proj)


def deliver(*refs):
    count = len(refs) // 3
    sources, targets = refs[:count], refs[count : 2 * count]
    buffers, got, put = refs[2 * count : 3 * count], refs[-2], refs[-1]
    inward = [
        pltpu.make_async_copy(sources[i], buffers[i], got.at[i]) for i in range(count)
    ]
    outward = [
        pltpu.make_async_copy(buffers[i], targets[i], put.at[i]) for i in range(count)
    ]
    for copy in inward:
        copy.start()
    for before, after in zip(inward, outward):
        before.wait()
        after.start()
    for copy in outward:
        copy.wait()


def delivered(arrays):
    anywhere = pl.BlockSpec(memory_space=pl.ANY)
    return pl.pallas_call(
        deliver,
        out_shape=tuple(jax.ShapeDtypeStruct(a.shape, a.dtype) for a in arrays),
        in_specs=[anywhere] * len(arrays),
        out_specs=(anywhere,) * len(arrays),
        scratch_shapes=[pltpu.VMEM(a.shape, a.dtype) for a in arrays]
        + [pltpu.SemaphoreType.DMA((len(arrays),))] * 2,
        name="deliver",
    )(*arrays)


def shards(
    bytes_in,
    doc_lengths,
    patch_offsets,
    patch_counts,
    w_query,
    w_key,
    w_value,
    w_proj,
    norm_gain,
    gate_w,
    up_w,
    d_hidden,
):
    units = gate_w.shape[1]
    results = whole_layer(
        bytes_in[0],
        doc_lengths[None],
        patch_offsets,
        patch_counts,
        norm_gain[None],
        d_hidden.reshape(-1, units),
        gate_w,
        up_w,
        (w_query, w_key, w_value),
        w_proj,
    )
    hidden, grad_gate, grad_up, patch_grad = delivered(results)
    return (hidden.reshape(d_hidden.shape), grad_gate, grad_up, patch_grad[None])


def solution(mesh):
    return jax.shard_map(
        shards,
        mesh=mesh,
        in_specs=(
            P("seq", "fsdp", None),
            P(),
            P("seq", "fsdp"),
            P("seq", "fsdp"),
            P(),
            P(),
            P(),
            P(),
            P(),
            P("fsdp", "seq"),
            P("fsdp", "seq"),
            P(None, "fsdp", "seq"),
        ),
        out_specs=(
            P(None, "fsdp", "seq"),
            P("fsdp", "seq"),
            P("fsdp", "seq"),
            P("seq", "fsdp", None),
        ),
        check_vma=False,
    )
```
